32 devices in a mesh: rows: 8 (over z, y), blk: 4 (over x, core).
Axes of the slice: x: 2, y: 2, z: 4, core: 2. Of those that a mesh axis runs over, the one named last changes fastest.
Arguments:
- block_input: bfloat16 [16, 256, 1536], P('rows', 'blk'), may hold values from -6 to 6
- cotangent: bfloat16 [16, 256, 1536], P('rows', 'blk'), may hold values from -6 to 6
- query_w: float32 [1536, 768], P(('rows', 'blk')), may hold values from -0.0390625 to 0.0390625
- key_w: float32 [1536, 768], P(('rows', 'blk')), may hold values from -0.15625 to 0.15625
- value_w: float32 [1536, 768], P(('rows', 'blk')), may hold values from -0.15625 to 0.15625
- output_w: float32 [768, 1536], P(None, ('rows', 'blk')), may hold values from -1.25 to 1.25
- gate_w: float32 [1536, 3968], P(('rows', 'blk')), may hold values from -0.15625 to 0.15625
- up_w: float32 [1536, 3968], P(('rows', 'blk')), may hold values from -0.15625 to 0.15625
- down_w: float32 [3968, 1536], P(None, ('rows', 'blk')), may hold values from -0.09375 to 0.09375
- first_gain: float32 [1536], P(('rows', 'blk')), may hold values from 0.5 to 1.5
- second_gain: float32 [1536], P(('rows', 'blk')), may hold values from 0.5 to 1.5
- bias_table: float32 [32, 12], replicated, may hold values from -4 to 4
- rel_bucket: int32 [512], replicated, may hold values from 0 to 31
- doc_ids: int32 [16, 256], P('rows'), may hold values from 0 to 1, as said below
Outputs:
- block_output: bfloat16 [16, 256, 1536], P('rows', 'blk')
- input_grad: float32 [16, 256, 1536], P('rows', 'blk')
- query_grad: float32 [1536, 768], P(('rows', 'blk'))
- key_grad: float32 [1536, 768], P(('rows', 'blk'))
- value_grad: float32 [1536, 768], P(('rows', 'blk'))
- output_grad: float32 [768, 1536], P(None, ('rows', 'blk'))
- gate_grad: float32 [1536, 3968], P(('rows', 'blk'))
- up_grad: float32 [1536, 3968], P(('rows', 'blk'))
- down_grad: float32 [3968, 1536], P(None, ('rows', 'blk'))
- first_grad: float32 [1536], P(('rows', 'blk'))
- second_grad: float32 [1536], P(('rows', 'blk'))
- table_grad: float32 [32, 12], replicated
The draws below stay inside these ranges and needn't reach their ends.
Inputs may be any that keep to these rules, and one draw needn't show every extreme that they name: `doc_ids`: each row is either one document of 256 positions (all ids 0) or 2 documents of 128 positions with ids rising from 0; the first row is of the second kind and the second row of the first.
All inputs are finite; a program needn't handle non-finite values.
Results may differ from the reference program's by a relative error of at most 0.024.
Values may be sent and summed in bfloat16 or wider, within the bound.
No kernel may reach another device: no remote copies, remote signals or barrier semaphores. Data moves between devices by JAX's collectives and lax.ppermute only.
A program may use at most 256 MiB of HBM per device.

```python
import jax
import jax.numpy as jnp
from jax import lax

D = 1536
HEADS = 12
FF = 3968
BUCKETS = 32
SEQ = 256
ROWS = 16
SHORT_ROW = 128
INNER = 768


def draw_doc_ids(key, part):
    flags = jax.random.randint(jax.random.fold_in(key, 7), (ROWS, 1), 0, 8)
    row_index = jnp.arange(ROWS, dtype=jnp.int32)[:, None]
    single = jnp.where(row_index == 0, False, jnp.where(row_index == 1, True, flags < 3))
    positions = jnp.arange(SEQ, dtype=jnp.int32)[None, :]
    return jnp.where(single, 0, positions // SHORT_ROW).astype(jnp.int32)


def set_ends(values, own_key, least, top_value):
    place = [jax.random.randint(jax.random.fold_in(own_key, axis), (), 0, length) for axis, length in enumerate(values.shape)]
    longest = values.shape.index(max(values.shape))
    beside = place[:longest] + [(place[longest] + 1) % values.shape[longest]] + place[longest + 1:]
    return values.at[tuple(place)].set(least).at[tuple(beside)].set(top_value)


def shard_levels(key, extent, shards, smallest, largest):
    def one(dim, parts):
        draws = jax.random.uniform(jax.random.fold_in(jax.random.fold_in(key, 6), dim), (parts,), jnp.float32, smallest / len(shards), largest / len(shards))
        return jnp.repeat(jnp.exp(draws), extent[dim] // parts).reshape((-1,) + (1,) * (len(extent) - dim - 1))

    level = one(*shards[0])
    for cut in shards[1:]:
        level = level * one(*cut)
    return level


def normal_values(key, extent, deviation, limit, pieces=(), held_as=jnp.bfloat16):
    entries = deviation * jax.random.normal(key, extent, jnp.float32)
    if pieces:
        entries = entries * shard_levels(key, extent, pieces, -0.22, 0.18)
    return jnp.clip(entries, -limit, limit).astype(held_as)


def setup_inputs(seed: int = 0) -> dict:
    arg_keys = jax.random.split(jax.random.key(seed), 15)
    return {
        "block_input": normal_values(arg_keys[0], (ROWS, SEQ, D), 1.0, 6.0, ((0, 8), (1, 4))),
        "cotangent": normal_values(arg_keys[1], (ROWS, SEQ, D), 1.0, 6.0, ((0, 8), (1, 4))),
        "query_w": normal_values(arg_keys[2], (D, INNER), (16 * D) ** -0.5, 0.0390625, ((0, 32),), jnp.float32),
        "key_w": normal_values(arg_keys[3], (D, INNER), D ** -0.5, 0.15625, ((0, 32),), jnp.float32),
        "value_w": normal_values(arg_keys[4], (D, INNER), D ** -0.5, 0.15625, ((0, 32),), jnp.float32),
        "output_w": normal_values(arg_keys[5], (INNER, D), (INNER // 32) ** -0.5, 1.25, ((1, 32),), jnp.float32),
        "gate_w": normal_values(arg_keys[6], (D, FF), D ** -0.5, 0.15625, ((0, 32),), jnp.float32),
        "up_w": normal_values(arg_keys[7], (D, FF), D ** -0.5, 0.15625, ((0, 32),), jnp.float32),
        "down_w": normal_values(arg_keys[8], (FF, D), FF ** -0.5, 0.09375, ((1, 32),), jnp.float32),
        "first_gain": jnp.clip(1.0 + 0.1 * jax.random.normal(arg_keys[9], (D,), jnp.float32), 0.5, 1.5),
        "second_gain": jnp.clip(1.0 + 0.1 * jax.random.normal(arg_keys[10], (D,), jnp.float32), 0.5, 1.5),
        "bias_table": normal_values(arg_keys[11], (BUCKETS, HEADS), 1.0, 4.0, (), jnp.float32),
        "rel_bucket": set_ends(jax.random.randint(arg_keys[12], (2 * SEQ,), 0, BUCKETS), jax.random.fold_in(arg_keys[12], 1), 0, BUCKETS - 1).astype(jnp.int32),
        "doc_ids": draw_doc_ids(jax.random.fold_in(arg_keys[14], 71), 0),
    }


@jax.custom_vjp
def low(v):
    return lax.optimization_barrier(v.astype(jnp.bfloat16)).astype(jnp.float32)

@jax.custom_vjp
def low_back(v):
    return v

def low_keep(v):
    return (low(v), None)

def low_pass(kept, grad):
    return (grad,)

def back_keep(v):
    return (v, None)

def back_low(kept, grad):
    return (low(grad),)
low.defvjp(low_keep, low_pass)
low_back.defvjp(back_keep, back_low)
EPSILON = 1e-06
HIGHEST = lax.Precision.HIGHEST

def matmul(left, right):
    return jnp.dot(left, right, precision=HIGHEST)

def norm_scale(values, gain):
    return values * lax.rsqrt(lax.optimization_barrier(jnp.mean(values * values, axis=-1, keepdims=True)) + EPSILON) * gain

def attention(queries, key_rows, value_rows, bias_table, rel_bucket, doc_row):
    seq_len = key_rows.shape[0]
    head_count = bias_table.shape[1]
    head_dim = queries.shape[1] // head_count
    block_len = min(512, seq_len)
    block_count = seq_len // block_len
    key_heads = key_rows.reshape(seq_len, head_count, head_dim)
    value_heads = value_rows.reshape(seq_len, head_count, head_dim)
    query_blocks = queries.reshape(block_count, block_len, head_count, head_dim)
    offsets = jnp.arange(block_count, dtype=jnp.int32) * block_len

    def one_block(block_args):
        query_blk, offset = block_args
        query_pos = offset + jnp.arange(block_len, dtype=jnp.int32)
        key_pos = jnp.arange(seq_len, dtype=jnp.int32)
        bucket_ids = rel_bucket[key_pos[None, :] - query_pos[:, None] + seq_len]
        rel_bias = jnp.transpose(bias_table[bucket_ids], (0, 2, 1))
        scores = low_back(jnp.einsum('qhd,khd->qhk', query_blk, key_heads, precision=HIGHEST) + rel_bias)
        query_doc = lax.dynamic_slice_in_dim(doc_row, offset, block_len)
        same_doc = (query_doc[:, None] == doc_row[None, :])[:, None, :]
        expo_low = low(jnp.where(same_doc, jnp.exp(scores), 0.0))
        totals = lax.optimization_barrier(jnp.sum(expo_low, axis=2))
        weighted = low_back(jnp.einsum('qhk,khd->qhd', expo_low, value_heads, precision=HIGHEST))
        return low(weighted / totals[:, :, None])
    attended = lax.map(jax.checkpoint(one_block), (query_blocks, offsets))
    return attended.reshape(seq_len, head_count * head_dim)

def row_forward(params, row_input, doc_row, rel_bucket):
    query_w, key_w, value_w, output_w, gate_w, up_w, down_w, first_gain, second_gain, bias_table = params
    normed = low(norm_scale(row_input, low(first_gain)))
    queries = low(low_back(matmul(normed, low(query_w))))
    key_rows = low(low_back(matmul(normed, low(key_w))))
    value_rows = low(low_back(matmul(normed, low(value_w))))
    attended = attention(queries, key_rows, value_rows, bias_table, rel_bucket, doc_row)
    middle = row_input + low_back(matmul(attended, low(output_w)))
    normed_mlp = low(norm_scale(middle, low(second_gain)))
    gate_pre = low_back(matmul(normed_mlp, low(gate_w)))
    up_pre = low_back(matmul(normed_mlp, low(up_w)))
    hidden = low(jax.nn.gelu(gate_pre, approximate=True) * up_pre)
    return middle + matmul(hidden, low(down_w))

def reference(block_input, cotangent, query_w, key_w, value_w, output_w, gate_w, up_w, down_w, first_gain, second_gain, bias_table, rel_bucket, doc_ids):
    params = (query_w, key_w, value_w, output_w, gate_w, up_w, down_w, first_gain, second_gain, bias_table)

    def one_row(grad_sums, row_args):
        row_input, row_cot, doc_row = row_args

        def forward(weights, inputs):
            return row_forward(weights, inputs, doc_row, rel_bucket)
        result, pullback = jax.vjp(forward, params, row_input.astype(jnp.float32))
        weight_grads, input_grad = pullback(row_cot.astype(jnp.float32))
        grad_sums = jax.tree.map(jnp.add, grad_sums, weight_grads)
        return (grad_sums, (result.astype(jnp.bfloat16), input_grad))
    zeros = jax.tree.map(jnp.zeros_like, params)
    grad_sums, (outputs, input_grads) = lax.scan(one_row, zeros, (block_input, cotangent, doc_ids))
    return (outputs, input_grads, grad_sums[0], grad_sums[1], grad_sums[2], grad_sums[3], grad_sums[4], grad_sums[5], grad_sums[6], grad_sums[7], grad_sums[8], grad_sums[9])
```

```python
import math

import jax
import jax.numpy as jnp
from jax import lax
from jax.experimental import pallas as pl
from jax.experimental.pallas import tpu as pltpu
from jax.sharding import Mesh, PartitionSpec as P

EPSILON = 1e-06
BF = jnp.bfloat16
F32 = jnp.float32
HIGHEST = lax.Precision.HIGHEST
RING = ("rows", "seq")
MAX_RING = 8
EXTRA = 16


def dot(left, right, dims, out=F32):
    return lax.dot_general(left, right, (dims, ((), ())), preferred_element_type=out)


NN = ((1,), (0,))
NT = ((1,), (1,))
TN = ((0,), (0,))


def ring_order(count):
    return list(range(0, count, 2)) + list(range(count - 1, 0, -2))


def ring_places(count):
    order = ring_order(count)
    table = [[order[(order.index(r) - k) % count] for k in range(count)] for r in range(count)]
    return jnp.asarray(table, jnp.int32)[lax.axis_index(RING)]


def ring_shift(value, count, step):
    order = ring_order(count)
    pairs = [(order[i], order[(i + step) % count]) for i in range(count)]
    return lax.ppermute(value, RING, pairs)


def ring_ok(count):
    return count <= MAX_RING and count % 2 == 0


def gather_ring(chunk, count):
    if count == 1:
        return chunk[None]
    if not ring_ok(count):
        return lax.all_gather(chunk, RING, axis=0)
    places = ring_places(count)
    half = chunk.shape[0] // 2
    got = [(0, 0, chunk)]
    ahead = behind = chunk
    for k in range(1, count // 2):
        ahead = ring_shift(ahead, count, 1)
        behind = ring_shift(behind, count, -1)
        got += [(k, 0, ahead), (count - k, 0, behind)]
    got += [
        (count // 2, 0, ring_shift(ahead[:half], count, 1)),
        (count // 2, half, ring_shift(behind[half:], count, -1)),
    ]
    whole = jnp.zeros((count, *chunk.shape), chunk.dtype)
    for k, first, piece in got:
        whole = lax.dynamic_update_slice(whole, piece[None], (places[k], jnp.int32(first), jnp.int32(0)))
    return whole


def scatter_ring(blocks, count):
    if count == 1:
        return blocks[0].astype(F32)
    if not ring_ok(count):
        return lax.psum_scatter(blocks, RING, scatter_dimension=0, tiled=True)[0].astype(F32)
    places = ring_places(count)
    half = blocks.shape[1] // 2

    def own(k):
        return lax.dynamic_index_in_dim(blocks, places[k % count], 0, keepdims=False)

    far = own(count // 2)
    ahead = ring_shift(far[:half], count, 1).astype(F32)
    behind = ring_shift(far[half:], count, -1).astype(F32)
    for j in range(count // 2 - 1, 0, -1):
        up, down = own(-j).astype(F32), own(j).astype(F32)
        if ahead.shape[0] == half:
            up = jnp.concatenate([up[:half] + ahead, up[half:]], axis=0)
            down = jnp.concatenate([down[:half], down[half:] + behind], axis=0)
        else:
            up, down = up + ahead, down + behind
        ahead = ring_shift(up.astype(BF), count, 1).astype(F32)
        behind = ring_shift(down.astype(BF), count, -1).astype(F32)
    mine = own(0).astype(F32)
    if ahead.shape[0] == half:
        return mine + jnp.concatenate([ahead, behind], axis=0)
    return mine + ahead + behind


def partner(value, ways, bit):
    return lax.ppermute(value, "tp", [(i, i ^ bit) for i in range(ways)])


def block_of(index, ways):
    place = index * 0
    bit = 1
    while bit < ways:
        place = place * 2 + ((index // bit) % 2)
        bit *= 2
    return place


def gather_tokens(value, ways):
    bit = ways // 2
    while bit:
        value = jnp.concatenate([value, partner(value, ways, bit)], axis=0)
        bit //= 2
    return value


def sum_tokens(value, ways):
    if ways == 1:
        return value
    half = value.shape[0] // 2
    near = value[:half] + partner(value[half:].astype(BF), ways, 1).astype(F32)
    if ways == 4:
        low = near.astype(BF)
        far = partner(low, ways, 2)
        quarter = half // 2
        far = jnp.concatenate([far[quarter:], far[:quarter]], axis=0)
        near = low.astype(F32) + far.astype(F32)
    elif ways > 2:
        raise NotImplementedError
    low = near.astype(BF)
    return jnp.concatenate([low, partner(low, ways, 1)], axis=0).astype(F32)


def scatter_tokens(value, ways):
    bit = 1
    while bit < ways:
        half = value.shape[0] // 2
        value = value[:half] + partner(value[half:].astype(BF), ways, bit).astype(F32)
        bit *= 2
    return value


def exchange(blocks, ways):
    if ways == 1:
        return blocks
    own = lax.axis_index("tp")
    whole = jnp.zeros(blocks.shape, blocks.dtype)
    for k in range(ways):
        piece = lax.dynamic_slice_in_dim(blocks, own ^ k, 1, 0)
        if k:
            piece = partner(piece, ways, k)
        whole = lax.dynamic_update_slice_in_dim(whole, piece, own ^ k, 0)
    return whole


def head_scores(own, row, head, dim, ways, rows, length, q_ref, k_ref, w_ref, qd_ref, kd_ref):
    lanes = slice(head * dim, (head + 1) * dim)
    starts = [pl.multiple_of((block_of(own ^ a, ways) * rows + row) * length, length) for a in range(ways)]
    queries = jnp.concatenate([q_ref[pl.ds(s, length), lanes] for s in starts], axis=0)
    keys = take_keys(k_ref, starts, length, lanes)
    q_len, k_len = queries.shape[0], keys.shape[0]
    scores = dot(queries, keys, NT)
    bias = jnp.broadcast_to(w_ref[pl.ds(head, 1), :], (q_len, q_len + k_len))
    bias = pltpu.roll(bias, k_len, 1, stride=1, stride_axis=0)[:, :k_len]
    same = qd_ref[0] == kd_ref[0]
    expo = jnp.where(same, jnp.exp(scores + bias), 0.0)
    return queries, keys, expo, starts, lanes


def take_keys(ref, starts, length, lanes):
    return jnp.concatenate(
        [ref[g, pl.ds(s, length), lanes] for g in range(ref.shape[0]) for s in starts], axis=0
    )


def attn_forward(heads, dim, ways, rows, length, own_ref, q_ref, k_ref, v_ref, w_ref, qd_ref, kd_ref, attn_ref):
    row, own = pl.program_id(0), own_ref[0]
    out = []
    for head in range(heads):
        _, _, expo, starts, lanes = head_scores(
            own, row, head, dim, ways, rows, length, q_ref, k_ref, w_ref, qd_ref, kd_ref
        )
        values = take_keys(v_ref, starts, length, lanes)
        low = expo.astype(BF)
        totals = jnp.sum(low.astype(F32), axis=1, keepdims=True)
        out.append(dot(low, values, NN) / totals)
    out = jnp.concatenate(out, axis=1)
    for a, s in enumerate(starts):
        attn_ref[pl.ds(s, length), :] = out[a * length : (a + 1) * length]


def attn_backward(
    heads, dim, ways, rows, length, own_ref, q_ref, k_ref, v_ref, w_ref, qd_ref, kd_ref, attn_ref, grad_ref,
    gq_ref, gk_ref, gv_ref, diag_ref,
):
    row, own = pl.program_id(0), own_ref[0]
    grads_q, grads_k, grads_v, diags = [], [], [], []
    for head in range(heads):
        queries, keys, expo, starts, lanes = head_scores(
            own, row, head, dim, ways, rows, length, q_ref, k_ref, w_ref, qd_ref, kd_ref
        )
        values = take_keys(v_ref, starts, length, lanes)
        grad = jnp.concatenate([grad_ref[pl.ds(s, length), lanes] for s in starts], axis=0)
        attn = jnp.concatenate([attn_ref[pl.ds(s, length), lanes] for s in starts], axis=0)
        low = expo.astype(BF)
        totals = jnp.sum(low.astype(F32), axis=1, keepdims=True)
        grad_low = (grad / totals).astype(BF)
        grad_total = -jnp.sum(grad * attn, axis=1, keepdims=True) / totals
        grad_score = (expo * (dot(grad_low, values, NT) + grad_total)).astype(BF)
        grads_q.append(dot(grad_score, keys, NN))
        grads_k.append(dot(grad_score, queries, TN))
        grads_v.append(dot(low, grad_low, TN))
        q_len, k_len = grad_score.shape
        row_at = lax.broadcasted_iota(jnp.int32, (q_len, q_len), 0)
        column_at = lax.broadcasted_iota(jnp.int32, (q_len, q_len), 1)
        flip = jnp.where(row_at + column_at == q_len - 1, 1.0, 0.0).astype(BF)
        turned = dot(flip, grad_score, NN)
        turned = jnp.concatenate([turned, jnp.zeros((q_len, q_len), F32)], axis=1)
        turned = pltpu.roll(turned, 1, 1, stride=1, stride_axis=0)
        diags.append(jnp.sum(turned, axis=0, keepdims=True))
    for parts, ref in ((grads_q, gq_ref),):
        whole = jnp.concatenate(parts, axis=1).astype(BF)
        for a, s in enumerate(starts):
            ref[pl.ds(s, length), :] = whole[a * length : (a + 1) * length]
    for parts, ref in ((grads_k, gk_ref), (grads_v, gv_ref)):
        whole = jnp.concatenate(parts, axis=1).astype(BF)
        for g in range(ref.shape[0]):
            for a, s in enumerate(starts):
                at = (g * ways + a) * length
                ref[g, pl.ds(s, length), :] = whole[at : at + length]
    diag = jnp.concatenate(diags, axis=0)

    @pl.when(row == 0)
    def _():
        diag_ref[...] = diag

    @pl.when(row != 0)
    def _():
        diag_ref[...] += diag


def attn_call(body, own, operands, docs, outs, rows):
    whole = [pl.BlockSpec(a.shape, lambda r, *_, n=a.ndim: (0,) * n) for a in operands]
    by_row = [pl.BlockSpec((1, *a.shape[1:]), lambda r, *_: (r, 0, 0)) for a in docs]
    return pl.pallas_call(
        body,
        grid_spec=pltpu.PrefetchScalarGridSpec(
            num_scalar_prefetch=1,
            grid=(rows,),
            in_specs=whole[:4] + by_row + whole[4:],
            out_specs=[pl.BlockSpec(o.shape, lambda r, *_, n=len(o.shape): (0,) * n) for o in outs],
        ),
        out_shape=outs,
        compiler_params=pltpu.CompilerParams(
            dimension_semantics=("arbitrary",), vmem_limit_bytes=48 << 20
        ),
    )(own, *operands[:4], *docs, *operands[4:])


def split_columns(value, ways, width):
    value = jnp.pad(value, ((0, 0), (0, ways * width - value.shape[1])))
    return value.reshape(value.shape[0], ways, width).transpose(1, 0, 2)


def join_columns(blocks, width):
    ways, count, _ = blocks.shape
    return blocks.transpose(1, 0, 2).reshape(count, -1)[:, :width].astype(F32)


def shards(
    ways, block_input, cotangent, query_w, key_w, value_w, output_w, gate_w, up_w, down_w,
    first_gain, second_gain, bias_table, rel_bucket, doc_ids,
):
    rows, length, model = block_input.shape
    tokens = rows * length
    own = lax.axis_index("tp")
    parts = lax.axis_size("seq")
    count = lax.axis_size("rows") * parts
    bucket_count, head_count = bias_table.shape
    inner = query_w.shape[1]
    heads = head_count // ways
    dim = inner // head_count
    width = heads * dim
    depth = query_w.shape[0]
    chunk = ways * depth
    hidden_count = gate_w.shape[1]
    ff = -(-hidden_count // (ways * 128)) * 128
    seq_len = doc_ids.shape[1]
    q_len = ways * length

    four = jnp.stack([query_w, key_w, value_w, output_w.T]).astype(BF)
    four = four.reshape(4, depth, ways, width).transpose(2, 1, 0, 3).reshape(ways, depth, 4 * width)
    gains = jnp.pad(jnp.stack([first_gain, second_gain]).astype(BF), ((0, EXTRA - 2), (0, 4 * width - depth)))
    four = jnp.concatenate([four, jnp.broadcast_to(gains[None], (ways, *gains.shape))], axis=1)
    four = exchange(four, ways)
    gains = four[:, depth : depth + 2, :depth].transpose(1, 0, 2).reshape(2, chunk)
    gains = jnp.pad(gains, ((0, EXTRA - 2), (0, 4 * width - chunk)))
    four = gather_ring(jnp.concatenate([four[:, :depth].reshape(chunk, 4 * width), gains], axis=0), count)
    gain_one = four[:, chunk, :chunk].reshape(1, model).astype(F32)
    gain_two = four[:, chunk + 1, :chunk].reshape(1, model).astype(F32)
    attn_w = four[:, :chunk].reshape(model, 4 * width)
    pair = jnp.concatenate(
        [split_columns(gate_w.astype(BF), ways, ff), split_columns(up_w.astype(BF), ways, ff)], axis=2
    )
    pair_w = gather_ring(exchange(pair, ways).reshape(chunk, 2 * ff), count).reshape(model, 2 * ff)
    down = split_columns(down_w.T.astype(BF), ways, ff)
    down_b = gather_ring(exchange(down, ways).reshape(chunk, ff), count).reshape(model, ff)

    inputs = gather_tokens(block_input.reshape(tokens, model), ways)
    cot = gather_tokens(cotangent.reshape(tokens, model), ways)

    one_hot = (rel_bucket[:, None] == jnp.arange(bucket_count, dtype=jnp.int32)).astype(F32)
    first = lax.axis_index("seq") * q_len
    one_hot = lax.dynamic_slice_in_dim(one_hot, seq_len - first - q_len, seq_len + q_len, 0)
    own_table = lax.dynamic_slice_in_dim(bias_table, own * heads, heads, 1)
    by_distance = lax.dot_general(own_table, one_hot, (((0,), (1,)), ((), ())), precision=HIGHEST)
    query_doc = lax.dynamic_slice_in_dim(doc_ids, first, q_len, 1)[:, :, None]
    key_doc = doc_ids[:, None, :]

    inputs = inputs.astype(F32)
    rsq_one = lax.rsqrt(jnp.mean(inputs * inputs, axis=1, keepdims=True) + EPSILON)
    normed = (inputs * rsq_one * gain_one).astype(BF)
    three = dot(normed, attn_w[:, : 3 * width], NN, BF)
    queries, keys, values = three[:, :width], three[:, width : 2 * width], three[:, 2 * width :]
    if parts > 1:
        keys = lax.all_gather(keys, "seq", axis=0)
        values = lax.all_gather(values, "seq", axis=0)
    else:
        keys, values = keys[None], values[None]
    shape = (heads, dim, ways, rows, length)
    own_at = own.reshape(1).astype(jnp.int32)
    (attn,) = attn_call(
        lambda *refs: attn_forward(*shape, *refs), own_at, (queries, keys, values, by_distance),
        (query_doc, key_doc), [jax.ShapeDtypeStruct(queries.shape, F32)], rows,
    )
    attended = attn.astype(BF)
    output_b = attn_w[:, 3 * width :]
    middle = inputs + sum_tokens(dot(attended, output_b, NT), ways)
    rsq_two = lax.rsqrt(jnp.mean(middle * middle, axis=1, keepdims=True) + EPSILON)
    normed_mlp = (middle * rsq_two * gain_two).astype(BF)

    both = dot(normed_mlp, pair_w, NN)
    gate_pre, up_pre = both[:, :ff], both[:, ff:]
    scale = math.sqrt(2.0 / math.pi)
    tanh = jnp.tanh(scale * (gate_pre + 0.044715 * gate_pre * gate_pre * gate_pre))
    activated = 0.5 * gate_pre * (1.0 + tanh)
    slope = 0.5 * (1.0 + tanh) + 0.5 * gate_pre * (1.0 - tanh * tanh) * scale * (
        1.0 + 3 * 0.044715 * gate_pre * gate_pre
    )
    hidden = (activated * up_pre).astype(BF)
    down_grad = dot(cot, hidden, TN, BF).reshape(count, chunk, ff)
    down_sum = scatter_ring(down_grad, count)
    grad_hidden = dot(cot, down_b, NN)
    grad_both = jnp.concatenate(
        [(grad_hidden * up_pre * slope).astype(BF), (grad_hidden * activated).astype(BF)], axis=1
    )
    grad_normed_mlp = sum_tokens(dot(grad_both, pair_w, NT), ways)
    pair_grad = dot(normed_mlp, grad_both, TN, BF).reshape(count, chunk, 2 * ff)
    pair_sum = scatter_ring(pair_grad, count)
    result = middle[:tokens] + scatter_tokens(dot(hidden, down_b, NT), ways)
    block_output = result.astype(BF).reshape(rows, length, model)

    second_part = jnp.sum(grad_normed_mlp * middle * rsq_two, axis=0)
    scaled = grad_normed_mlp * gain_two
    grad_middle = (
        cot.astype(F32) + rsq_two * scaled
        - middle * (rsq_two * rsq_two * rsq_two * jnp.mean(scaled * middle, axis=1, keepdims=True))
    )
    grad_branch = grad_middle.astype(BF)
    grad_attn = dot(grad_branch, output_b, NN)
    wide = jax.ShapeDtypeStruct(keys.shape, BF)
    grad_q, grad_k, grad_v, diag = attn_call(
        lambda *refs: attn_backward(*shape, *refs), own_at,
        (queries, keys, values, by_distance, attn, grad_attn), (query_doc, key_doc),
        [jax.ShapeDtypeStruct(queries.shape, BF), wide, wide, jax.ShapeDtypeStruct(by_distance.shape, F32)], rows,
    )
    if parts > 1:
        grad_k = lax.psum_scatter(grad_k, "seq", scatter_dimension=0, tiled=True)
        grad_v = lax.psum_scatter(grad_v, "seq", scatter_dimension=0, tiled=True)
    grad_three = jnp.concatenate([grad_q, grad_k[0], grad_v[0]], axis=1)
    grad_normed = dot(grad_three, attn_w[:, : 3 * width], NT)
    table_part = lax.dot_general(diag, one_hot, (((1,), (0,)), ((), ())), precision=HIGHEST)
    first_part = jnp.sum(grad_normed * inputs * rsq_one, axis=0)

    small = jnp.stack([first_part, second_part]).reshape(2, count, chunk).transpose(1, 0, 2)
    small = jnp.pad(small, ((0, 0), (0, EXTRA - 2), (0, 4 * width - chunk)))
    tables = jnp.pad(table_part.reshape(1, -1), ((2, EXTRA - 3), (0, 4 * width - heads * bucket_count)))
    small = (small + tables[None]).astype(BF)
    four_grad = jnp.concatenate([dot(normed, grad_three, TN, BF), dot(grad_branch, attended, TN, BF)], axis=1)
    four_grad = jnp.concatenate([four_grad.reshape(count, chunk, 4 * width), small], axis=1)
    four_sum = scatter_ring(four_grad, count).astype(BF)

    grad_own = scatter_tokens(grad_normed, ways)
    inputs, rsq_one = inputs[:tokens], rsq_one[:tokens]
    scaled = grad_own * gain_one
    input_grad = grad_middle[:tokens] + rsq_one * scaled - inputs * (
        rsq_one * rsq_one * rsq_one * jnp.mean(scaled * inputs, axis=1, keepdims=True)
    )

    pair_own = exchange(pair_sum.astype(BF).reshape(ways, depth, 2 * ff), ways)
    down_own = exchange(down_sum.astype(BF).reshape(ways, depth, ff), ways)
    gate_grad = join_columns(pair_own[:, :, :ff], hidden_count)
    up_grad = join_columns(pair_own[:, :, ff:], hidden_count)
    down_grad = join_columns(down_own, hidden_count).T
    small = four_sum[chunk : chunk + 2, :chunk].reshape(2, ways, depth).transpose(1, 0, 2)
    small = jnp.pad(small, ((0, 0), (0, EXTRA - 2), (0, 4 * width - depth)))
    tables = jnp.pad(four_sum[chunk + 2 : chunk + 3], ((2, EXTRA - 3), (0, 0)))
    small = small + tables[None]
    four_own = jnp.concatenate([four_sum[:chunk].reshape(ways, depth, 4 * width), small], axis=1)
    four_own = exchange(four_own, ways)
    grads = [join_columns(four_own[:, :depth, i * width : (i + 1) * width], inner) for i in range(4)]
    first_grad = jnp.sum(four_own[:, depth, :depth].astype(F32), axis=0)
    second_grad = four_own[0, depth + 1, :depth].astype(F32)
    table_grad = four_own[:, depth + 2, : heads * bucket_count].astype(F32)
    table_grad = table_grad.reshape(head_count, bucket_count).T
    return (
        block_output, input_grad.reshape(rows, length, model), grads[0], grads[1], grads[2], grads[3].T,
        gate_grad, up_grad, down_grad, first_grad, second_grad, table_grad,
    )


def solution(mesh):
    def program(*arrays):
        row_count, blk_count = mesh.shape["rows"], mesh.shape["blk"]
        ways = math.gcd(math.gcd(blk_count, arrays[11].shape[1]), 4)
        fine = Mesh(mesh.devices.reshape(row_count, blk_count // ways, ways), ("rows", "seq", "tp"))
        every = ("rows", "seq", "tp")
        tokens = P("rows", ("seq", "tp"), None)
        deep, wide, flat = P(every, None), P(None, every), P(every)
        return jax.shard_map(
            lambda *blocks: shards(ways, *blocks),
            mesh=fine,
            in_specs=(
                tokens, tokens, deep, deep, deep, wide, deep, deep, wide, flat, flat, P(), P(), P("rows", None),
            ),
            out_specs=(tokens, tokens, deep, deep, deep, wide, deep, deep, wide, flat, flat, P()),
            check_vma=False,
        )(*arrays)

    return program
```

```python
import math

import jax
import jax.numpy as jnp
from jax import lax
from jax.experimental import pallas as pl
from jax.experimental.pallas import tpu as pltpu
from jax.sharding import Mesh, PartitionSpec as P

EPSILON = 1e-06
BF = jnp.bfloat16
F32 = jnp.float32
HIGHEST = lax.Precision.HIGHEST
RING = ("rows", "seq")
MAX_RING = 8
EXTRA = 16
FREE = pl.CostEstimate(flops=0, transcendentals=0, bytes_accessed=0)


def dot(left, right, dims, out=F32):
    return lax.dot_general(left, right, (dims, ((), ())), preferred_element_type=out)


NN = ((1,), (0,))
NT = ((1,), (1,))
TN = ((0,), (0,))


def ring_order(count):
    return list(range(0, count, 2)) + list(range(count - 1, 0, -2))


def ring_places(count):
    half = count // 2
    group = lax.axis_index(RING)
    place = jnp.where(group % 2 == 0, group // 2, count - 1 - group // 2)
    places = []
    for k in range(count):
        at = place - k
        at = jnp.where(at < 0, at + count, at)
        places.append(jnp.where(at < half, 2 * at, 2 * (count - 1 - at) + 1))
    return places


def split_at(size):
    half = size // 2
    return half // 16 * 16 if half > 16 else half


def ring_ok(count):
    return count <= MAX_RING and count % 2 == 0


class Lanes:
    def __init__(self, count, ways):
        order = ring_order(count)
        self.pairs = {
            step: [(order[i], order[(i + step) % count]) for i in range(count)] for step in (1, -1)
        }
        self.count, self.ways, self.last = count, ways, None

    def pin(self, *values):
        if self.last is not None:
            values = lax.optimization_barrier((*values, self.last))[:-1]
        self.last = values[0]
        return values if len(values) > 1 else values[0]

    def shift(self, value, step):
        return lax.ppermute(value, RING, self.pairs[step])

    def partner(self, value, bit):
        return lax.ppermute(value, "tp", [(i, i ^ bit) for i in range(self.ways)])


class Task:
    def __init__(self, steps):
        self.steps, self.value = steps, None

    def step(self):
        if self.steps is not None:
            try:
                next(self.steps)
            except StopIteration as stop:
                self.value, self.steps = stop.value, None

    def result(self):
        while self.steps is not None:
            self.step()
        return self.value


def gather_ring(lanes, chunk, keep):
    count, (size, width) = lanes.count, chunk.shape
    if not ring_ok(count):
        whole = lax.all_gather(chunk, RING, axis=0) if count > 1 else chunk[None]
        return whole[:, :keep].reshape(-1, width), whole[:, keep:]
    half = split_at(size)
    chunk = lanes.pin(chunk)
    ahead = behind = chunk
    got = [(0, 0, chunk)]
    for k in range(1, count // 2):
        ahead, behind = lanes.shift(ahead, 1), lanes.shift(behind, -1)
        yield
        ahead, behind = lanes.pin(ahead, behind)
        got += [(k, 0, ahead), (count - k, 0, behind)]
    ahead, behind = lanes.shift(ahead[:half], 1), lanes.shift(behind[half:], -1)
    yield
    ahead, behind = lanes.pin(ahead, behind)
    got += [(count // 2, 0, ahead), (count // 2, half, behind)]
    return place_rows(got, count, keep, size - keep)


def place_rows(got, count, keep, extra):
    width, dtype = got[0][2].shape[1], got[0][2].dtype
    shapes = [jax.ShapeDtypeStruct((count * keep, width), dtype)]
    if extra:
        shapes.append(jax.ShapeDtypeStruct((count, extra, width), dtype))
    cuts = []
    for i, (k, first, piece) in enumerate(got):
        inside = min(piece.shape[0], keep - first)
        cuts.append((i, 0, k, first, 0, inside))
        if inside < piece.shape[0]:
            cuts.append((i, 1, k, 0, inside, piece.shape[0] - inside))

    def body(*refs):
        pieces, outs, sems = refs[: len(got)], refs[-1 - len(shapes) : -1], refs[-1]
        places = ring_places(count)
        copies = []
        for n, (i, out, k, to, start, rows) in enumerate(cuts):
            if out == 0:
                at = pl.ds(pl.multiple_of(places[k] * keep + to, math.gcd(keep, to)), rows)
                target = outs[0].at[at]
            else:
                target = outs[1].at[places[k]]
            copies.append(pltpu.make_async_copy(pieces[i].at[pl.ds(start, rows)], target, sems.at[n]))
        for copy in copies:
            copy.start()
        for copy in copies:
            copy.wait()

    outs = pl.pallas_call(
        body,
        in_specs=[pl.BlockSpec(memory_space=pl.ANY)] * len(got),
        out_specs=[pl.BlockSpec(memory_space=pltpu.VMEM)] * len(shapes),
        out_shape=shapes,
        scratch_shapes=[pltpu.SemaphoreType.DMA((len(cuts),))],
        compiler_params=pltpu.CompilerParams(vmem_limit_bytes=16 << 20),
        cost_estimate=FREE,
    )(*(piece for _, _, piece in got))
    return outs[0], outs[1] if extra else None


def scatter_ring(lanes, blocks):
    count = lanes.count
    if count == 1:
        return blocks[0]
    if not ring_ok(count):
        return lax.psum_scatter(blocks, RING, scatter_dimension=0, tiled=True)[0]
    half = split_at(blocks.shape[1])
    far = lax.dynamic_index_in_dim(blocks, ring_places(count)[count // 2], 0, keepdims=False)
    ahead, behind = lanes.pin(far[:half], far[half:])
    ahead, behind = lanes.shift(ahead, 1), lanes.shift(behind, -1)
    yield
    for j in range(count // 2 - 1, 0, -1):
        ahead, behind = lanes.pin(ahead, behind)
        ahead, behind = lanes.pin(*add_blocks(blocks, ahead, behind, j, half))
        ahead, behind = lanes.shift(ahead, 1), lanes.shift(behind, -1)
        yield
    ahead, behind = lanes.pin(ahead, behind)
    return add_blocks(blocks, ahead, behind, 0, half)


def add_blocks(blocks, ahead, behind, j, half):
    count, size, width = blocks.shape
    columns = 512 if width % 512 == 0 else 256
    whole = ahead.shape[0] == size

    def up_or_down(offset):
        return lambda c: (ring_places(count)[offset % count], 0, c)

    def body(up_ref, down_ref, ahead_ref, behind_ref, *outs):
        up, down = up_ref[0].astype(F32), down_ref[0].astype(F32)
        came, back = ahead_ref[...].astype(F32), behind_ref[...].astype(F32)
        if not whole:
            came = jnp.concatenate([came, jnp.zeros((size - half, columns), F32)], axis=0)
            back = jnp.concatenate([jnp.zeros((half, columns), F32), back], axis=0)
        if j:
            outs[0][...] = (up + came).astype(BF)
            outs[1][...] = (down + back).astype(BF)
        else:
            outs[0][...] = (up + came + back).astype(BF)

    shapes = [jax.ShapeDtypeStruct((size, width), BF)] * (2 if j else 1)
    outs = pl.pallas_call(
        body,
        grid=(width // columns,),
        in_specs=[
            pl.BlockSpec((1, size, columns), up_or_down(-j)),
            pl.BlockSpec((1, size, columns), up_or_down(j)),
            pl.BlockSpec((ahead.shape[0], columns), lambda c: (0, c)),
            pl.BlockSpec((behind.shape[0], columns), lambda c: (0, c)),
        ],
        out_specs=[pl.BlockSpec((size, columns), lambda c: (0, c))] * len(shapes),
        out_shape=shapes,
        compiler_params=pltpu.CompilerParams(vmem_limit_bytes=16 << 20),
        cost_estimate=FREE,
    )(blocks, blocks, ahead, behind)
    return outs if j else outs[0]


def block_of(index):
    return index % 2 * 2 + index // 2


def gather_tokens(lanes, value):
    for bit in (2, 1):
        value = lanes.pin(value)
        got = lanes.partner(value, bit)
        yield
        value = jnp.concatenate([value, lanes.pin(got)], axis=0)
    return value


def sum_tokens(lanes, keep, give):
    got = lanes.partner(lanes.pin(give), 1)
    yield
    low = lanes.pin(add_halves(keep, lanes.pin(got), False))
    far = lanes.partner(low, 2)
    yield
    low = lanes.pin(add_halves(low, lanes.pin(far), True))
    got = lanes.partner(low, 1)
    yield
    return low, lanes.pin(got)


def add_halves(left, right, swapped):
    half, width = left.shape[0] // 2, left.shape[1]

    def body(left_ref, right_ref, out_ref):
        out_ref[...] = (left_ref[...].astype(F32) + right_ref[...].astype(F32)).astype(BF)

    return run(
        body, (2,), [(left, (half, width), lambda i: (i, 0)),
                     (right, (half, width), (lambda i: (1 - i, 0)) if swapped else (lambda i: (i, 0)))],
        [((2 * half, width), BF, (half, width), lambda i: (i, 0))],
    )[0]


def scatter_tokens(lanes, keep, give):
    got = lanes.partner(lanes.pin(give), 1)
    yield
    low = lanes.pin(add_halves(keep, lanes.pin(got), False))
    mine = low.shape[0] // 2
    got = lanes.partner(low[mine:], 2)
    yield
    return low[:mine], lanes.pin(got)


def exchange(lanes, blocks, at_once=True):
    pieces = [blocks[0]] + [None] * 3
    for k in (2, 3, 1):
        pieces[k] = lanes.partner(lanes.pin(blocks[k]), k)
        if not at_once:
            yield
    if at_once:
        yield
    pieces[1:] = lanes.pin(*pieces[1:])
    return pieces


def by_member(pieces):
    own, chosen = lax.axis_index("tp"), []
    for a in range(4):
        piece = pieces[a]
        for mine in range(1, 4):
            piece = jnp.where(own == mine, pieces[a ^ mine], piece)
        chosen.append(piece)
    return chosen


def run(body, grid, ins, outs, scratch=(), vmem=24):
    def spec(block, index_map):
        return pl.BlockSpec(block, index_map)

    arrays, in_specs = [], []
    for item in ins:
        array, block, index_map = item if isinstance(item, tuple) else (item, item.shape, None)
        if index_map is None:
            index_map = lambda *_, n=array.ndim: (0,) * n
        arrays.append(array)
        in_specs.append(spec(block, index_map))
    out_specs = [
        spec(block or shape, index_map or (lambda *_, n=len(shape): (0,) * n)) for shape, _, block, index_map in outs
    ]
    return pl.pallas_call(
        body, grid=grid, in_specs=in_specs, out_specs=out_specs,
        out_shape=[jax.ShapeDtypeStruct(shape, dtype) for shape, dtype, _, _ in outs],
        scratch_shapes=list(scratch),
        compiler_params=pltpu.CompilerParams(
            dimension_semantics=("arbitrary",) * len(grid), vmem_limit_bytes=vmem << 20
        ),
        cost_estimate=FREE,
    )(*arrays)


def whole(shape, dtype):
    return (shape, dtype, None, None)


def pack_attn(weights, gains, width):
    depth, inner = weights[0].shape

    def body(q_ref, k_ref, v_ref, o_ref, first_ref, second_ref, out_ref):
        own = lax.axis_index("tp")
        extra = jnp.concatenate([first_ref[...], second_ref[...], jnp.zeros((EXTRA - 2, depth), F32)], axis=0)
        extra = jnp.concatenate([extra, jnp.zeros((EXTRA, 4 * width - depth), F32)], axis=1).astype(BF)
        for a in range(4):
            parts = [r[:, a * width : (a + 1) * width] for r in (q_ref, k_ref, v_ref, o_ref)]
            out_ref[a ^ own, :depth] = jnp.concatenate(parts, axis=1).astype(BF)
            out_ref[a ^ own, depth:] = extra

    (out,) = run(body, (1,), [*weights, *gains], [whole((4, depth + EXTRA, 4 * width), BF)])
    return [out[k] for k in range(4)]


def pack_mlp(weights, ff):
    depth, count = weights[0].shape

    def body(*refs):
        own, out_ref = lax.axis_index("tp"), refs[-1]
        for a in range(4):
            parts = []
            for ref in refs[:-1]:
                last = min(count, (a + 1) * ff)
                parts.append(ref[:, a * ff : last])
                if last < (a + 1) * ff:
                    parts.append(jnp.zeros((depth, (a + 1) * ff - last), F32))
            out_ref[a ^ own] = jnp.concatenate(parts, axis=1).astype(BF)

    (out,) = run(body, (1,), weights, [whole((4, depth, len(weights) * ff), BF)])
    return [out[k] for k in range(4)]


def pack_plain(weights, width, extra):
    own = lax.axis_index("tp")
    weights = [jnp.pad(w.astype(BF), ((0, 0), (0, 4 * width - w.shape[1]))) for w in weights]
    blocks = []
    for k in range(4):
        block = jnp.concatenate([lax.dynamic_slice_in_dim(w, (own ^ k) * width, width, 1) for w in weights], axis=1)
        blocks.append(block if extra is None else jnp.concatenate([block, extra], axis=0))
    return blocks


def spread_gains(rest, chunk):
    count, _, width = rest.shape

    def body(rest_ref, one_ref, two_ref):
        rows = [rest_ref[r, :, :chunk].astype(F32) for r in range(count)]
        both = jnp.concatenate(rows, axis=1)
        one_ref[...], two_ref[...] = both[0:1], both[1:2]

    return run(body, (1,), [rest], [whole((1, count * chunk), F32)] * 2)


def rsq_of(value):
    return lax.rsqrt(jnp.mean(value * value, axis=1, keepdims=True) + EPSILON)


def project(inputs, gain, weights, width):
    tokens, model = inputs.shape
    half = tokens // 2

    def body(x_ref, gain_ref, w_ref, normed_ref, rsq_ref, q_ref, k_ref, v_ref):
        x = x_ref[...].astype(F32)
        rsq = rsq_of(x)
        normed = (x * rsq * gain_ref[...]).astype(BF)
        normed_ref[...] = normed
        rsq_ref[...] = jnp.broadcast_to(rsq, rsq_ref.shape)
        three = dot(normed, w_ref[:, : 3 * width], NN).astype(BF)
        for i, ref in enumerate((q_ref, k_ref, v_ref)):
            ref[...] = three[:, i * width : (i + 1) * width]

    def rows(columns, dtype):
        return ((tokens, columns), dtype, (half, columns), lambda i: (i, 0))

    return run(
        body, (2,), [(inputs, (half, model), lambda i: (i, 0)), gain, weights],
        [rows(model, BF), rows(128, F32), rows(width, BF), rows(width, BF), rows(width, BF)],
    )


def head_scores(own, row, head, dim, rows, length, q_ref, k_ref, w_ref, qd_ref, kd_ref):
    lanes = slice(head * dim, (head + 1) * dim)
    starts = [pl.multiple_of((block_of(own ^ a) * rows + row) * length, length) for a in range(4)]
    queries = jnp.concatenate([q_ref[pl.ds(s, length), lanes] for s in starts], axis=0)
    keys = take_keys(k_ref, starts, length, lanes)
    q_len, k_len = queries.shape[0], keys.shape[0]
    scores = dot(queries, keys, NT)
    bias = jnp.broadcast_to(w_ref[pl.ds(head, 1), :], (q_len, q_len + k_len))
    bias = pltpu.roll(bias, k_len, 1, stride=1, stride_axis=0)[:, :k_len]
    same = qd_ref[0] == kd_ref[0]
    expo = jnp.where(same, jnp.exp(scores + bias), 0.0)
    return queries, keys, expo, starts, lanes


def take_keys(ref, starts, length, lanes):
    return jnp.concatenate(
        [ref[g, pl.ds(s, length), lanes] for g in range(ref.shape[0]) for s in starts], axis=0
    )


def attn_forward(q, k, v, by_distance, query_doc, key_doc, attn_w, heads, dim, rows, length):
    tokens, width = q.shape
    model = attn_w.shape[0]
    half = tokens // 2

    def body(q_ref, k_ref, v_ref, w_ref, qd_ref, kd_ref, o_ref, attn_ref, keep_ref, give_ref, part_ref):
        row, own = pl.program_id(0), lax.axis_index("tp")
        out = []
        for head in range(heads):
            _, _, expo, starts, lanes = head_scores(
                own, row, head, dim, rows, length, q_ref, k_ref, w_ref, qd_ref, kd_ref
            )
            values = take_keys(v_ref, starts, length, lanes)
            low = expo.astype(BF)
            totals = jnp.sum(low.astype(F32), axis=1, keepdims=True)
            out.append(dot(low, values, NN) / totals)
        out = jnp.concatenate(out, axis=1)
        part = dot(out.astype(BF), o_ref[:, 3 * width :], NT)
        for a, s in enumerate(starts):
            attn_ref[pl.ds(s, length), :] = out[a * length : (a + 1) * length]
            part_ref[pl.ds(s, length), :] = part[a * length : (a + 1) * length]

        @pl.when(row == rows - 1)
        def _():
            keep_ref[...] = part_ref[:half]
            give_ref[...] = part_ref[half:].astype(BF)

    by_row = lambda r: (r, 0, 0)
    return run(
        body, (rows,),
        [q, k, v, by_distance, (query_doc, (1, *query_doc.shape[1:]), by_row),
         (key_doc, (1, *key_doc.shape[1:]), by_row), attn_w],
        [whole((tokens, width), F32), whole((half, model), F32), whole((half, model), BF)],
        [pltpu.VMEM((tokens, model), F32)],
    )


def attn_backward(q, k, v, by_distance, query_doc, key_doc, attn, grad, one_hot, heads, dim, rows, length, columns):
    buckets = one_hot.shape[1]

    def body(
        q_ref, k_ref, v_ref, w_ref, qd_ref, kd_ref, attn_ref, grad_ref, hot_ref,
        gq_ref, gk_ref, gv_ref, table_ref, diag_ref,
    ):
        row, own = pl.program_id(0), lax.axis_index("tp")
        grads_q, grads_k, grads_v, diags = [], [], [], []
        for head in range(heads):
            queries, keys, expo, starts, lanes = head_scores(
                own, row, head, dim, rows, length, q_ref, k_ref, w_ref, qd_ref, kd_ref
            )
            values = take_keys(v_ref, starts, length, lanes)
            grads = jnp.concatenate([grad_ref[pl.ds(s, length), lanes] for s in starts], axis=0)
            outs = jnp.concatenate([attn_ref[pl.ds(s, length), lanes] for s in starts], axis=0)
            low = expo.astype(BF)
            totals = jnp.sum(low.astype(F32), axis=1, keepdims=True)
            grad_low = (grads / totals).astype(BF)
            grad_total = -jnp.sum(grads * outs, axis=1, keepdims=True) / totals
            grad_score = (expo * (dot(grad_low, values, NT) + grad_total)).astype(BF)
            grads_q.append(dot(grad_score, keys, NN))
            grads_k.append(dot(grad_score, queries, TN))
            grads_v.append(dot(low, grad_low, TN))
            q_len, k_len = grad_score.shape
            row_at = lax.broadcasted_iota(jnp.int32, (q_len, q_len), 0)
            column_at = lax.broadcasted_iota(jnp.int32, (q_len, q_len), 1)
            flip = jnp.where(row_at + column_at == q_len - 1, 1.0, 0.0).astype(BF)
            turned = dot(flip, grad_score, NN)
            turned = jnp.concatenate([turned, jnp.zeros((q_len, q_len), F32)], axis=1)
            turned = pltpu.roll(turned, 1, 1, stride=1, stride_axis=0)
            diags.append(jnp.sum(turned, axis=0, keepdims=True))
        joined = jnp.concatenate(grads_q, axis=1).astype(BF)
        for a, s in enumerate(starts):
            gq_ref[pl.ds(s, length), :] = joined[a * length : (a + 1) * length]
        for parts, ref in ((grads_k, gk_ref), (grads_v, gv_ref)):
            joined = jnp.concatenate(parts, axis=1).astype(BF)
            for g in range(ref.shape[0]):
                for a, s in enumerate(starts):
                    at = (g * 4 + a) * length
                    ref[g, pl.ds(s, length), :] = joined[at : at + length]
        diag = jnp.concatenate(diags, axis=0)

        @pl.when(row == 0)
        def _():
            diag_ref[...] = diag

        @pl.when(row != 0)
        def _():
            diag_ref[...] += diag

        @pl.when(row == rows - 1)
        def _():
            table = lax.dot_general(
                diag_ref[...], hot_ref[...], (NN, ((), ())), precision=HIGHEST, preferred_element_type=F32
            )
            table = [table[h : h + 1] for h in range(heads)]
            table_ref[...] = jnp.concatenate(table + [jnp.zeros((1, columns - heads * buckets), F32)], axis=1)

    by_row = lambda r: (r, 0, 0)
    return run(
        body, (rows,),
        [q, k, v, by_distance, (query_doc, (1, *query_doc.shape[1:]), by_row),
         (key_doc, (1, *key_doc.shape[1:]), by_row), attn, grad, one_hot],
        [whole(q.shape, BF), whole(k.shape, BF), whole(v.shape, BF), whole((1, columns), F32)],
        [pltpu.VMEM(by_distance.shape, F32)],
    )


def norm_again(inputs, low, other, gain):
    tokens, model = inputs.shape
    part = tokens // 4

    def body(x_ref, low_ref, other_ref, gain_ref, middle_ref, normed_ref):
        branch = jnp.where(pl.program_id(0) < 2, low_ref[...].astype(F32), other_ref[...].astype(F32))
        middle = x_ref[...].astype(F32) + branch
        middle_ref[...] = middle
        normed_ref[...] = (middle * rsq_of(middle) * gain_ref[...]).astype(BF)

    rows = lambda i: (i, 0)
    return run(
        body, (4,),
        [(inputs, (part, model), rows), (low, (part, model), lambda i: (jnp.minimum(i, 1), 0)),
         (other, (part, model), lambda i: (jnp.maximum(i - 2, 0), 0)), gain],
        [((tokens, model), F32, (part, model), rows), ((tokens, model), BF, (part, model), rows)],
    )


def norm_back(middle, cot, low, other, gain, attn_w, width):
    tokens, model = middle.shape
    part = tokens // 4

    def body(m_ref, cot_ref, low_ref, other_ref, gain_ref, w_ref, mid_ref, branch_ref, gain_out_ref, attn_ref):
        i = pl.program_id(0)
        grad = jnp.where(i < 2, low_ref[...].astype(F32), other_ref[...].astype(F32))
        middle = m_ref[...]
        rsq = rsq_of(middle)
        unit = middle * rsq
        scaled = grad * gain_ref[...]
        back = cot_ref[...].astype(F32) + rsq * (scaled - unit * jnp.mean(scaled * unit, axis=1, keepdims=True))
        mid_ref[...] = back
        branch = back.astype(BF)
        branch_ref[...] = branch
        attn_ref[...] = dot(branch, w_ref[:, 3 * width :], NN)
        partial = jnp.sum(grad * unit, axis=0, keepdims=True)

        @pl.when(i == 0)
        def _():
            gain_out_ref[...] = partial

        @pl.when(i != 0)
        def _():
            gain_out_ref[...] += partial

    rows = lambda i: (i, 0)
    return run(
        body, (4,),
        [(middle, (part, model), rows), (cot, (part, model), rows),
         (low, (part, model), lambda i: (jnp.minimum(i, 1), 0)),
         (other, (part, model), lambda i: (jnp.maximum(i - 2, 0), 0)), gain, attn_w],
        [((tokens, model), F32, (part, model), rows), ((tokens, model), BF, (part, model), rows),
         whole((1, model), F32), ((tokens, width), F32, (part, width), rows)],
    )


def gated(normed, gate_b, up_b, grad_hidden):
    tokens, model = normed.shape
    ff = gate_b.shape[1]
    tile = 256
    scale = math.sqrt(2.0 / math.pi)

    def body(x_ref, gate_ref, up_ref, grad_ref, hidden_ref, grad_gate_ref, grad_up_ref):
        x = x_ref[...]
        gate, up = dot(x, gate_ref[...], NN), dot(x, up_ref[...], NN)
        square = gate * gate
        tanh = jnp.tanh(scale * gate * (1.0 + 0.044715 * square))
        curve = 0.5 * (1.0 + tanh)
        slope = curve + 0.5 * gate * (1.0 - tanh * tanh) * (scale * (1.0 + 3 * 0.044715 * square))
        activated = gate * curve
        grad = grad_ref[...].astype(F32)
        hidden_ref[...] = (activated * up).astype(BF)
        grad_gate_ref[...] = (grad * up * slope).astype(BF)
        grad_up_ref[...] = (grad * activated).astype(BF)

    columns = lambda j: (0, j)
    return run(
        body, (ff // tile,),
        [normed, (gate_b, (model, tile), columns), (up_b, (model, tile), columns), (grad_hidden, (tokens, tile), columns)],
        [((tokens, ff), BF, (tokens, tile), columns)] * 3,
    )


def times(left, right, dtype):
    tokens, model = left.shape
    ff = right.shape[1]
    tile = 256

    def body(left_ref, right_ref, out_ref):
        out_ref[...] = dot(left_ref[...], right_ref[...], NN).astype(dtype)

    return run(
        body, (ff // tile,), [left, (right, (model, tile), lambda j: (0, j))],
        [((tokens, ff), dtype, (tokens, tile), lambda j: (0, j))],
    )[0]


def weight_grad(left, right):
    tokens, model = left.shape
    ff = right.shape[1]
    tile = 384

    def body(left_ref, right_ref, out_ref):
        out_ref[...] = dot(left_ref[...], right_ref[...], TN).astype(BF)

    return run(
        body, (model // tile,), [(left, (tokens, tile), lambda j: (0, j)), right],
        [((model, ff), BF, (tile, ff), lambda j: (j, 0))],
    )[0]


def back_through(pairs):
    tokens, ff = pairs[0][0].shape
    model = pairs[0][1].shape[0]
    half, tile = tokens // 2, 384

    def body(*refs):
        keep_ref, give_ref = refs[-2:]
        total = None
        for i in range(len(pairs)):
            term = dot(refs[2 * i][...], refs[2 * i + 1][...], NT)
            total = term if total is None else total + term
        keep_ref[...] = total[:half]
        give_ref[...] = total[half:].astype(BF)

    ins = []
    for left, right in pairs:
        ins += [left, (right, (tile, ff), lambda j: (j, 0))]
    return run(
        body, (model // tile,), ins,
        [((half, model), F32, (half, tile), lambda j: (0, j)), ((half, model), BF, (half, tile), lambda j: (0, j))],
    )


def attn_weight_grads(normed, inputs, rsq, branch, attn, grads, attn_w, second_part, table, chunk):
    tokens, model = normed.shape
    width = attn.shape[1]
    half, tile = tokens // 2, 384
    each = tile // chunk

    def body(n_ref, x_ref, rsq_ref, b_ref, attn_ref, q_ref, k_ref, v_ref, w_ref, second_ref, table_ref, out_ref, keep_ref, give_ref):
        three = jnp.concatenate([q_ref[...], k_ref[...], v_ref[...]], axis=1)
        back = dot(three, w_ref[:, : 3 * width], NT)
        keep_ref[...] = back[:half]
        give_ref[...] = back[half:].astype(BF)
        first = jnp.sum(back * x_ref[...].astype(F32) * rsq_ref[:, 0:1], axis=0, keepdims=True)
        wide = dot(n_ref[...], three, TN).astype(BF)
        last = dot(b_ref[...], attn_ref[...].astype(BF), TN).astype(BF)
        fill = jnp.zeros((1, 4 * width - chunk), F32)
        for c in range(each):
            at = slice(c * chunk, (c + 1) * chunk)
            out_ref[c, :chunk] = jnp.concatenate([wide[at], last[at]], axis=1)
            small = [jnp.concatenate([row[:, at], fill], axis=1) for row in (first, second_ref[...])]
            small += [table_ref[...], jnp.zeros((EXTRA - 3, 4 * width), F32)]
            out_ref[c, chunk:] = jnp.concatenate(small, axis=0).astype(BF)

    columns = lambda j: (0, j)
    return run(
        body, (model // tile,),
        [(normed, (tokens, tile), columns), (inputs, (tokens, tile), columns), rsq, (branch, (tokens, tile), columns),
         attn, *grads, (attn_w, (tile, attn_w.shape[1]), lambda j: (j, 0)), (second_part, (1, tile), columns), table],
        [((model // chunk, chunk + EXTRA, 4 * width), BF, (each, chunk + EXTRA, 4 * width), lambda j: (j, 0, 0)),
         ((half, model), F32, (half, tile), columns), ((half, model), BF, (half, tile), columns)],
    )


def finish_input(addends, inputs, gain, grad_middle):
    count, model = addends[0].shape

    def body(low_ref, got_ref, x_ref, gain_ref, mid_ref, out_ref):
        x = x_ref[...].astype(F32)
        rsq = rsq_of(x)
        unit = x * rsq
        scaled = (low_ref[...].astype(F32) + got_ref[...].astype(F32)) * gain_ref[...]
        out_ref[...] = mid_ref[...] + rsq * (scaled - unit * jnp.mean(scaled * unit, axis=1, keepdims=True))

    first = lambda i: (0, 0)
    return run(
        body, (1,),
        [*addends, (inputs, (count, model), first), gain, (grad_middle, (count, model), first)],
        [whole((count, model), F32)],
    )[0]


def finish_output(addends, middle):
    count, model = addends[0].shape

    def body(low_ref, got_ref, mid_ref, out_ref):
        total = mid_ref[...] + low_ref[...].astype(F32) + got_ref[...].astype(F32)
        out_ref[...] = total.astype(BF)

    return run(
        body, (1,), [*addends, (middle, (count, model), lambda i: (0, 0))], [whole((count, model), BF)]
    )[0]


def rows_of(value, depth):
    own = lax.axis_index("tp")
    return [lax.dynamic_slice_in_dim(value, (own ^ k) * depth, depth, 0) for k in range(4)]


def shards(
    block_input, cotangent, query_w, key_w, value_w, output_w, gate_w, up_w, down_w,
    first_gain, second_gain, bias_table, rel_bucket, doc_ids,
):
    rows, length, model = block_input.shape
    tokens = rows * length
    own = lax.axis_index("tp")
    parts = lax.axis_size("seq")
    count = lax.axis_size("rows") * parts
    bucket_count, head_count = bias_table.shape
    inner = query_w.shape[1]
    heads = head_count // 4
    dim = inner // head_count
    width = heads * dim
    depth = query_w.shape[0]
    chunk = 4 * depth
    hidden_count = gate_w.shape[1]
    ff = -(-hidden_count // (4 * 256)) * 256
    seq_len = doc_ids.shape[1]
    q_len = 4 * length

    lanes = Lanes(count, 4)
    attn_weights = [query_w, key_w, value_w, output_w.T]
    gains = [first_gain.reshape(1, depth), second_gain.reshape(1, depth)]
    mlp_weights = [down_w.T, gate_w, up_w]
    if depth % 16 == 0:
        four_from = pack_attn(attn_weights, gains, width)
    else:
        gains = jnp.pad(jnp.concatenate(gains, axis=0).astype(BF), ((0, EXTRA - 2), (0, 4 * width - depth)))
        four_from = pack_plain(attn_weights, width, gains)
    four_from = Task(exchange(lanes, four_from))
    four_from.step()
    mlp_from = pack_mlp(mlp_weights, ff) if depth % 16 == 0 else pack_plain(mlp_weights, ff, None)
    mlp_from = Task(exchange(lanes, mlp_from))
    mlp_from.step()
    inputs = Task(gather_tokens(lanes, block_input.reshape(tokens, model)))
    cot = Task(gather_tokens(lanes, cotangent.reshape(tokens, model)))
    pieces = by_member(four_from.result())
    gains = jnp.concatenate([p[depth : depth + 2, :depth] for p in pieces], axis=1)
    gains = jnp.pad(gains, ((0, EXTRA - 2), (0, 4 * width - chunk)))
    four = Task(gather_ring(lanes, jnp.concatenate([p[:depth] for p in pieces] + [gains], axis=0), chunk))
    four.step()
    four.step()
    pieces = jnp.concatenate(by_member(mlp_from.result()), axis=0)
    down, gate, up = (Task(gather_ring(lanes, pieces[:, i * ff : (i + 1) * ff], chunk)) for i in range(3))
    down.step()
    inputs.step()
    four.step()
    inputs.step()
    down.step()
    four.step()
    inputs = inputs.result()
    cot.step()
    down.step()
    attn_w, gains = four.result()
    gate.step()

    one_hot = (rel_bucket[:, None] == jnp.arange(bucket_count, dtype=jnp.int32)).astype(F32)
    first = lax.axis_index("seq") * q_len
    one_hot = lax.dynamic_slice_in_dim(one_hot, seq_len - first - q_len, seq_len + q_len, 0)
    own_table = lax.dynamic_slice_in_dim(bias_table, own * heads, heads, 1)
    by_distance = lax.dot_general(own_table, one_hot, (((0,), (1,)), ((), ())), precision=HIGHEST)
    query_doc = lax.dynamic_slice_in_dim(doc_ids, first, q_len, 1)[:, :, None]
    key_doc = doc_ids[:, None, :]

    gain_one, gain_two = spread_gains(gains, chunk)
    normed, rsq_one, queries, keys, values = project(inputs, gain_one, attn_w, width)
    cot.step()
    down.step()
    if parts > 1:
        keys = lax.all_gather(keys, "seq", axis=0)
        values = lax.all_gather(values, "seq", axis=0)
    else:
        keys, values = keys[None], values[None]
    shape = (heads, dim, rows, length)
    attn, keep, give = attn_forward(queries, keys, values, by_distance, query_doc, key_doc, attn_w, *shape)
    branch = Task(sum_tokens(lanes, keep, give))
    branch.step()
    cot = cot.result()
    down_b, _ = down.result()
    up.step()
    branch.step()
    gate.step()
    grad_hidden = lanes.pin(times(cot, down_b, F32))
    up.step()
    gate.step()
    branch.step()
    middle, normed_mlp = norm_again(inputs, *branch.result(), gain_two)
    normed_mlp = lanes.pin(normed_mlp)
    up.step()
    gate.step()
    up.step()
    gate_b, _ = gate.result()
    up_b, _ = up.result()

    hidden, grad_gate, grad_up = gated(normed_mlp, gate_b, up_b, grad_hidden)

    def blocks(left, right):
        return weight_grad(left, right).reshape(count, chunk, ff)

    down_grad = Task(scatter_ring(lanes, blocks(cot, hidden)))
    down_grad.step()
    branch = Task(sum_tokens(lanes, *back_through([(grad_gate, gate_b), (grad_up, up_b)])))
    branch.step()
    gate_grad = Task(scatter_ring(lanes, blocks(normed_mlp, grad_gate)))
    gate_grad.step()
    branch.step()
    down_grad.step()
    up_grad = lanes.pin(blocks(normed_mlp, grad_up))
    gate_grad.step()
    result = back_through([(hidden, down_b)])
    result = Task(scatter_tokens(lanes, result[0], lanes.pin(result[1])))
    down_grad.step()
    gate_grad.step()
    branch.step()
    down_grad.step()
    grad_middle, grad_branch, second_part, grad_attn = norm_back(
        middle, cot, *branch.result(), gain_two, attn_w, width
    )
    grad_attn = lanes.pin(grad_attn)
    gate_grad.step()
    grad_q, grad_k, grad_v, table = attn_backward(
        queries, keys, values, by_distance, query_doc, key_doc, attn, grad_attn, one_hot, *shape, 4 * width
    )
    grad_q = lanes.pin(grad_q)
    down_sum = down_grad.result()
    up_grad = Task(scatter_ring(lanes, up_grad))
    up_grad.step()
    if parts > 1:
        grad_k = lax.psum_scatter(grad_k, "seq", scatter_dimension=0, tiled=True)
        grad_v = lax.psum_scatter(grad_v, "seq", scatter_dimension=0, tiled=True)
    four_grad, keep, give = attn_weight_grads(
        normed, inputs, rsq_one, grad_branch, attn, (grad_q, grad_k[0], grad_v[0]), attn_w, second_part, table, chunk
    )
    four_grad = lanes.pin(four_grad)
    result.step()
    gate_sum = gate_grad.result()
    four_grad = Task(scatter_ring(lanes, four_grad))
    four_grad.step()
    result.step()
    up_grad.step()
    four_grad.step()
    block_output = finish_output(result.result(), middle).reshape(rows, length, model)
    grad_own = Task(scatter_tokens(lanes, keep, give))
    grad_own.step()
    up_grad.step()
    grad_own.step()
    four_grad.step()
    both = Task(exchange(lanes, rows_of(jnp.concatenate([down_sum, gate_sum], axis=1), depth), False))
    grad_own = grad_own.result()
    both.step()
    up_grad.step()
    both.step()
    four_grad.step()
    both.step()
    input_grad = finish_input(grad_own, inputs, gain_one, grad_middle).reshape(rows, length, model)
    up_own = Task(exchange(lanes, rows_of(up_grad.result(), depth)))
    up_own.step()
    four_sum = four_grad.result()

    small = rows_of(four_sum[chunk : chunk + 2, :chunk].T, depth)
    tables = jnp.pad(four_sum[chunk + 2 : chunk + 3], ((2, EXTRA - 3), (0, 0)))
    four_own = []
    for large, pair in zip(rows_of(four_sum, depth), small):
        pair = jnp.pad(pair.T, ((0, EXTRA - 2), (0, 4 * width - depth)))
        four_own.append(jnp.concatenate([large, pair + tables], axis=0))
    four_own = Task(exchange(lanes, four_own))
    four_own.step()

    def joined(pieces):
        return jnp.concatenate(pieces, axis=1).astype(F32)

    both = by_member(both.result())
    down_out = joined([p[:, :ff] for p in both])[:, :hidden_count]
    gate_out = joined([p[:, ff:] for p in both])[:, :hidden_count]
    up_out = joined(by_member(up_own.result()))[:, :hidden_count]
    pieces = by_member(four_own.result())
    grads = [joined([p[:depth, i * width : (i + 1) * width] for p in pieces]) for i in range(4)]
    first_grad = sum(p[depth, :depth].astype(F32) for p in pieces)
    second_grad = pieces[0][depth + 1, :depth].astype(F32)
    table_grad = joined([p[depth + 2 : depth + 3, : heads * bucket_count] for p in pieces])
    table_grad = table_grad.reshape(head_count, bucket_count).T
    return (
        block_output, input_grad, grads[0], grads[1], grads[2], grads[3].T,
        gate_out, up_out, down_out.T, first_grad, second_grad, table_grad,
    )


def solution(mesh):
    row_count, blk_count = mesh.shape["rows"], mesh.shape["blk"]
    fine = Mesh(mesh.devices.reshape(row_count, blk_count // 4, 4), ("rows", "seq", "tp"))
    every = ("rows", "seq", "tp")
    tokens = P("rows", ("seq", "tp"), None)
    deep, wide, flat = P(every, None), P(None, every), P(every)
    return jax.shard_map(
        shards,
        mesh=fine,
        in_specs=(tokens, tokens, deep, deep, deep, wide, deep, deep, wide, flat, flat, P(), P(), P("rows", None)),
        out_specs=(tokens, tokens, deep, deep, deep, wide, deep, deep, wide, flat, flat, P()),
        check_vma=False,
    )
```

```python
import math

import jax
import jax.numpy as jnp
from jax import lax
from jax.experimental import pallas as pl
from jax.experimental.pallas import tpu as pltpu
from jax.sharding import Mesh, PartitionSpec as P

EPSILON = 1e-06
BF = jnp.bfloat16
F32 = jnp.float32
HIGHEST = lax.Precision.HIGHEST
RING = ("rows", "seq")
MAX_RING = 8
EXTRA = 16
PADS = (8, 8, 4)
RPADS = (0, 8, 0)
CUTS = 1
FREE = pl.CostEstimate(flops=0, transcendentals=0, bytes_accessed=0)


def dot(left, right, dims, out=F32):
    return lax.dot_general(left, right, (dims, ((), ())), preferred_element_type=out)


NN = ((1,), (0,))
NT = ((1,), (1,))
TN = ((0,), (0,))


def ring_order(count):
    return list(range(0, count, 2)) + list(range(count - 1, 0, -2))


def ring_places(count):
    half = count // 2
    group = lax.axis_index(RING)
    place = jnp.where(group % 2 == 0, group // 2, count - 1 - group // 2)
    places = []
    for k in range(count):
        at = place - k
        at = jnp.where(at < 0, at + count, at)
        places.append(jnp.where(at < half, 2 * at, 2 * (count - 1 - at) + 1))
    return places


def ring_ok(count):
    return count <= MAX_RING and count % 2 == 0


class Lanes:
    def __init__(self, count, ways):
        order = ring_order(count)
        self.pairs = {
            step: [(order[i], order[(i + step) % count]) for i in range(count)] for step in (1, -1)
        }
        self.count, self.ways, self.last = count, ways, None

    def pin(self, *values):
        if self.last is not None:
            values = lax.optimization_barrier((*values, self.last))[:-1]
        self.last = values[0]
        return values if len(values) > 1 else values[0]

    def shift(self, value, step):
        return lax.ppermute(value, RING, self.pairs[step])

    def partner(self, value, bit):
        return lax.ppermute(value, "tp", [(i, i ^ bit) for i in range(self.ways)])


class Task:
    def __init__(self, steps):
        self.steps, self.value = steps, None

    def step(self):
        if self.steps is not None:
            try:
                next(self.steps)
            except StopIteration as stop:
                self.value, self.steps = stop.value, None

    def result(self):
        while self.steps is not None:
            self.step()
        return self.value


def gather_ring(lanes, chunk, keep, lead):
    count = lanes.count
    if not ring_ok(count):
        got = lax.all_gather(chunk, RING, axis=0) if count > 1 else chunk[None]
        return got[:, :keep].reshape(-1, chunk.shape[1]), [got[i] for i in range(count)]
    chunk = lanes.pin(chunk)
    moving = {lead: chunk, -lead: chunk}
    got = [chunk]
    for k in range(1, count // 2):
        moving = {step: lanes.shift(value, step) for step, value in moving.items()}
        yield
        moving = dict(zip(moving, lanes.pin(*moving.values())))
        got += [moving[1], moving[-1]]
    last = lanes.shift(moving[lead], lead)
    yield
    got.append(lanes.pin(last))
    return place_rows(got, count, keep), got


def chunk_order(count):
    order = [0]
    for k in range(1, count // 2):
        order += [k, count - k]
    return order + [count // 2]


def place_rows(got, count, keep):
    def body(*refs):
        places = ring_places(count)
        for ref, k in zip(refs, chunk_order(count)):
            refs[-1][pl.ds(pl.multiple_of(places[k] * keep, keep), keep), :] = ref[:keep]

    return near(body, got, [((count * keep, got[0].shape[1]), BF)])[0]


def scatter_ring(lanes, blocks, lead, rows):
    count, size, _ = blocks.shape
    if count == 1:
        return blocks[0]
    if not ring_ok(count):
        return lax.psum_scatter(blocks, RING, scatter_dimension=0, tiled=True)[0]
    (far,) = add_blocks(blocks, [(count // 2, None)], rows)
    moving = {lead: lanes.shift(lanes.pin(far), lead)}
    yield
    for j in range(count // 2 - 1, 0, -1):
        arrived = dict(zip(moving, lanes.pin(*moving.values()) if len(moving) > 1 else (lanes.pin(moving[lead]),)))
        sums = add_blocks(blocks, [(-j * step, arrived.get(step)) for step in (1, -1)], rows)
        moving = {step: lanes.shift(value, step) for step, value in zip((1, -1), lanes.pin(*sums))}
        yield
    came, back = lanes.pin(*moving.values())
    return add_blocks(blocks, [(0, came)], size, back)[0]


def add_blocks(blocks, terms, rows, more=None):
    count, size, width = blocks.shape
    came = [c for _, c in terms if c is not None] + ([] if more is None else [more])

    def body(blocks_ref, *refs):
        places = ring_places(count)
        given, outs = list(refs[: len(came)]), refs[len(came) :]
        for (k, c), out in zip(terms, outs):
            total = blocks_ref[places[k % count]].astype(F32)
            if c is not None:
                total = total + given.pop(0)[:size].astype(F32)
            if more is not None:
                total = total + given.pop(0)[:size].astype(F32)
            out[:size] = total.astype(BF)
            if rows > size:
                out[size:] = jnp.zeros((rows - size, width), BF)

    return near(body, [blocks, *came], [((rows, width), BF)] * len(terms))


def block_of(index):
    return index % 2 * 2 + index // 2


def gather_tokens(lanes, value):
    value = lanes.pin(value)
    got = lanes.partner(value, 2)
    yield
    value = jnp.concatenate([value, lanes.pin(got)], axis=0)
    got = yield from over_core(lanes, value, CUTS)
    return jnp.concatenate([value, *got], axis=0)


def over_core(lanes, give, cuts):
    rows, pieces, first = give.shape[0], [], 0
    for n in range(cuts):
        last = rows * (n + 1) // cuts // 16 * 16 if n + 1 < cuts else rows
        got = lanes.partner(lanes.pin(give[first:last]), 1)
        yield
        pieces.append(lanes.pin(got))
        first = last
    return pieces


def sum_tokens(lanes, keep, give):
    got = yield from over_core(lanes, give, CUTS)
    low = lanes.pin(add_halves(keep, got, False))
    got = lanes.partner(low, 2)
    yield
    low = lanes.pin(add_halves(low, [lanes.pin(got)], True))
    got = yield from over_core(lanes, low, CUTS)
    return low, got


def add_halves(left, pieces, swapped):
    rows = left.shape[0]
    half = rows // 2

    def body(left_ref, *refs):
        first = 0
        for ref in refs[:-1]:
            for at in range(0, ref.shape[0], half if swapped else ref.shape[0]):
                count = half if swapped else ref.shape[0]
                to = half - at if swapped else first + at
                total = left_ref[to : to + count].astype(F32) + ref[at : at + count].astype(F32)
                refs[-1][to : to + count] = total.astype(BF)
            first += ref.shape[0]

    return near(body, [left, *pieces], [(left.shape, BF)])[0]


def scatter_tokens(lanes, keep, give):
    got = yield from over_core(lanes, give, CUTS)
    low = lanes.pin(add_halves(keep, got, False))
    mine = low.shape[0] // 2
    got = lanes.partner(low[mine:], 2)
    yield
    return low[:mine], lanes.pin(got)


def exchange(lanes, blocks, at_once=True):
    pieces = [blocks[0]] + [None] * 3
    for k in (2, 3, 1):
        pieces[k] = lanes.partner(lanes.pin(blocks[k]), k)
        if not at_once:
            yield
    if at_once:
        yield
    pieces[1:] = lanes.pin(*pieces[1:])
    return pieces


def by_member(pieces):
    own, chosen = lax.axis_index("tp"), []
    for a in range(4):
        piece = pieces[a]
        for mine in range(1, 4):
            piece = jnp.where(own == mine, pieces[a ^ mine], piece)
        chosen.append(piece)
    return chosen


def stack_members(pieces, widths, pads):
    depth = pieces[0].shape[0]
    if depth % 16:
        pieces = jnp.concatenate(by_member(pieces), axis=0)
        starts = [sum(widths[:i]) for i in range(len(widths))]
        return [jnp.pad(pieces[:, a : a + w], ((0, p), (0, 0))) for a, w, p in zip(starts, widths, pads)]

    def body(*refs):
        own = lax.axis_index("tp")
        at = 0
        for width, pad, out in zip(widths, pads, refs[4:]):
            for k in range(4):
                out[pl.ds(pl.multiple_of((own ^ k) * depth, depth), depth), :] = refs[k][:, at : at + width]
            if pad:
                out[4 * depth :] = jnp.zeros((pad, width), BF)
            at += width

    return near(body, pieces, [((4 * depth + pad, width), BF) for width, pad in zip(widths, pads)])


def stack_attn(pieces, chunk):
    depth, width = chunk // 4, pieces[0].shape[1]
    if depth % 16:
        pieces = by_member(pieces)
        gains = jnp.concatenate([p[depth : depth + 2, :depth] for p in pieces], axis=1)
        gains = jnp.pad(gains, ((0, EXTRA - 2), (0, width - chunk)))
        return jnp.concatenate([p[:depth] for p in pieces] + [gains], axis=0)

    def body(*refs):
        own, out, gains_ref = lax.axis_index("tp"), refs[4], refs[5]
        for k in range(4):
            out[pl.ds(pl.multiple_of((own ^ k) * depth, depth), depth), :] = refs[k][:depth]
            gains_ref[own ^ k] = refs[k][depth:, :depth].astype(F32)
        gains = [gains_ref[a] for a in range(4)] + [jnp.zeros((EXTRA, width - chunk), F32)]
        out[chunk:] = jnp.concatenate(gains, axis=1).astype(BF)

    return near(body, pieces, [((chunk + EXTRA, width), BF)], [pltpu.VMEM((4, EXTRA, depth), F32)])[0]


def split_attn(total, depth, width):
    chunk = 4 * depth
    if depth % 16:
        tables = jnp.pad(total[chunk + 2 : chunk + 3], ((2, EXTRA - 3), (0, 0)))
        blocks = []
        for large, pair in zip(rows_of([total], depth), rows_of([total[chunk : chunk + 2, :chunk].T], depth)):
            pair = jnp.pad(pair.T, ((0, EXTRA - 2), (0, 4 * width - depth)))
            blocks.append(jnp.concatenate([large, pair + tables], axis=0))
        return blocks

    def body(total_ref, *refs):
        own, small_ref = lax.axis_index("tp"), refs[4]
        fill = jnp.zeros((2, 4 * width - depth), F32)
        small = total_ref[chunk : chunk + EXTRA].astype(F32)
        below = jnp.concatenate([small[2:3], jnp.zeros((EXTRA - 3, 4 * width), F32)], axis=0)
        for a in range(4):
            pair = jnp.concatenate([small[0:2, a * depth : (a + 1) * depth], fill], axis=1)
            small_ref[a] = jnp.concatenate([pair, below], axis=0)
        for k in range(4):
            refs[k][:depth] = total_ref[pl.ds(pl.multiple_of((own ^ k) * depth, depth), depth), :]
            refs[k][depth:] = small_ref[own ^ k].astype(BF)

    return near(
        body, [total], [((depth + EXTRA, 4 * width), BF)] * 4, [pltpu.VMEM((4, EXTRA, 4 * width), F32)]
    )


def run(body, grid, ins, outs, scratch=(), vmem=24):
    def spec(block, index_map):
        return pl.BlockSpec(block, index_map)

    arrays, in_specs = [], []
    for item in ins:
        array, block, index_map = item if isinstance(item, tuple) else (item, item.shape, None)
        if index_map is None:
            index_map = lambda *_, n=array.ndim: (0,) * n
        arrays.append(array)
        in_specs.append(spec(block, index_map))
    out_specs = [
        spec(block or shape, index_map or (lambda *_, n=len(shape): (0,) * n)) for shape, _, block, index_map in outs
    ]
    return pl.pallas_call(
        body, grid=grid, in_specs=in_specs, out_specs=out_specs,
        out_shape=[jax.ShapeDtypeStruct(shape, dtype) for shape, dtype, _, _ in outs],
        scratch_shapes=list(scratch),
        compiler_params=pltpu.CompilerParams(
            dimension_semantics=("arbitrary",) * len(grid), vmem_limit_bytes=vmem << 20
        ),
        cost_estimate=FREE,
    )(*arrays)


def near(body, arrays, outs, scratch=(), vmem=16):
    spec = pl.BlockSpec(memory_space=pltpu.VMEM)
    return pl.pallas_call(
        body, in_specs=[spec] * len(arrays), out_specs=[spec] * len(outs),
        out_shape=[jax.ShapeDtypeStruct(shape, dtype) for shape, dtype in outs],
        scratch_shapes=list(scratch),
        compiler_params=pltpu.CompilerParams(vmem_limit_bytes=vmem << 20),
        cost_estimate=FREE,
    )(*arrays)


def far(arrays):
    return [pltpu.with_memory_space_constraint(a, pltpu.HBM) for a in arrays]


def whole(shape, dtype):
    return (shape, dtype, None, None)


def pack_attn(weights, gains, width):
    depth, inner = weights[0].shape

    def body(q_ref, k_ref, v_ref, o_ref, first_ref, second_ref, *rest):
        outs, out_ref = rest[:4], rest[4]
        own = lax.axis_index("tp")
        extra = jnp.concatenate([first_ref[...], second_ref[...], jnp.zeros((EXTRA - 2, depth), F32)], axis=0)
        extra = jnp.concatenate([extra, jnp.zeros((EXTRA, 4 * width - depth), F32)], axis=1).astype(BF)
        for a in range(4):
            parts = [r[:, a * width : (a + 1) * width] for r in (q_ref, k_ref, v_ref, o_ref)]
            out_ref[a ^ own, :depth] = jnp.concatenate(parts, axis=1).astype(BF)
            out_ref[a ^ own, depth:] = extra
        for k in range(4):
            outs[k][...] = out_ref[k]

    shape = (depth + EXTRA, 4 * width)
    return run(body, (1,), far([*weights, *gains]), [whole(shape, BF)] * 4, [pltpu.VMEM((4, *shape), BF)])


def pack_mlp(weights, ff):
    depth, count = weights[0].shape

    def body(*refs):
        own, out_ref = lax.axis_index("tp"), refs[-1]
        for a in range(4):
            parts = []
            for ref in refs[: len(weights)]:
                last = min(count, (a + 1) * ff)
                parts.append(ref[:, a * ff : last])
                if last < (a + 1) * ff:
                    parts.append(jnp.zeros((depth, (a + 1) * ff - last), F32))
            out_ref[a ^ own] = jnp.concatenate(parts, axis=1).astype(BF)
        for k in range(4):
            refs[len(weights) + k][...] = out_ref[k]

    shape = (depth, len(weights) * ff)
    return run(body, (1,), far(weights), [whole(shape, BF)] * 4, [pltpu.VMEM((4, *shape), BF)])


def pack_plain(weights, width, extra):
    own = lax.axis_index("tp")
    weights = [jnp.pad(w.astype(BF), ((0, 0), (0, 4 * width - w.shape[1]))) for w in weights]
    blocks = []
    for k in range(4):
        block = jnp.concatenate([lax.dynamic_slice_in_dim(w, (own ^ k) * width, width, 1) for w in weights], axis=1)
        blocks.append(block if extra is None else jnp.concatenate([block, extra], axis=0))
    return blocks


def spread_gains(chunks, chunk):
    count = len(chunks)
    ring = ring_ok(count)

    def body(*refs):
        one_ref, two_ref, rows_ref = refs[-3:]
        places = ring_places(count) if ring else None
        for ref, k in zip(refs, chunk_order(count) if ring else range(count)):
            rows_ref[places[k] if ring else k] = ref[chunk : chunk + 2, :chunk].astype(F32)
        both = jnp.concatenate([rows_ref[r] for r in range(count)], axis=1)
        one_ref[...], two_ref[...] = both[0:1], both[1:2]

    return near(body, chunks, [((1, count * chunk), F32)] * 2, [pltpu.VMEM((count, 2, chunk), F32)])


def rsq_of(value):
    return lax.rsqrt(jnp.mean(value * value, axis=1, keepdims=True) + EPSILON)


def project(inputs, gain, weights, width):
    tokens, model = inputs.shape
    tile = tokens // 2

    def body(x_ref, gain_ref, w_ref, normed_ref, rsq_ref, q_ref, k_ref, v_ref):
        for at in range(0, tokens, tile):
            rows = slice(at, at + tile)
            x = x_ref[rows].astype(F32)
            rsq = rsq_of(x)
            normed = (x * rsq * gain_ref[...]).astype(BF)
            normed_ref[rows] = normed
            rsq_ref[rows] = jnp.broadcast_to(rsq, (tile, 128))
            three = dot(normed, w_ref[:, : 3 * width], NN).astype(BF)
            for i, ref in enumerate((q_ref, k_ref, v_ref)):
                ref[rows] = three[:, i * width : (i + 1) * width]

    return near(
        body, [inputs, gain, weights],
        [((tokens, model), BF), ((tokens, 128), F32)] + [((tokens, width), BF)] * 3,
    )


def head_scores(own, row, head, dim, rows, length, q_ref, k_ref, w_ref, qd_ref, kd_ref):
    lanes = slice(head * dim, (head + 1) * dim)
    starts = [pl.multiple_of((block_of(own ^ a) * rows + row) * length, length) for a in range(4)]
    queries = jnp.concatenate([q_ref[pl.ds(s, length), lanes] for s in starts], axis=0)
    keys = take_keys(k_ref, starts, length, lanes)
    q_len, k_len = queries.shape[0], keys.shape[0]
    scores = dot(queries, keys, NT)
    bias = jnp.broadcast_to(w_ref[pl.ds(head, 1), :], (q_len, q_len + k_len))
    bias = pltpu.roll(bias, k_len, 1, stride=1, stride_axis=0)[:, :k_len]
    same = qd_ref[row] == kd_ref[row]
    expo = jnp.where(same, jnp.exp(scores + bias), 0.0)
    return queries, keys, expo, starts, lanes


def take_keys(ref, starts, length, lanes):
    return jnp.concatenate(
        [ref[g, pl.ds(s, length), lanes] for g in range(ref.shape[0]) for s in starts], axis=0
    )


def attn_forward(q, k, v, by_distance, query_doc, key_doc, attn_w, heads, dim, rows, length):
    tokens, width = q.shape
    model = attn_w.shape[0]
    half = tokens // 2

    def body(q_ref, k_ref, v_ref, w_ref, qd_ref, kd_ref, o_ref, attn_ref, keep_ref, give_ref, part_ref):
        def one_row(row):
            forward_row(row, q_ref, k_ref, v_ref, w_ref, qd_ref, kd_ref, o_ref, attn_ref, part_ref)

        lax.fori_loop(0, rows, lambda row, _: one_row(row), None)
        keep_ref[...] = part_ref[:half]
        give_ref[...] = part_ref[half:].astype(BF)

    def forward_row(row, q_ref, k_ref, v_ref, w_ref, qd_ref, kd_ref, o_ref, attn_ref, part_ref):
        own, out = lax.axis_index("tp"), []
        for head in range(heads):
            _, _, expo, starts, lanes = head_scores(
                own, row, head, dim, rows, length, q_ref, k_ref, w_ref, qd_ref, kd_ref
            )
            values = take_keys(v_ref, starts, length, lanes)
            low = expo.astype(BF)
            totals = jnp.sum(low.astype(F32), axis=1, keepdims=True)
            out.append(dot(low, values, NN) / totals)
        out = jnp.concatenate(out, axis=1)
        part = dot(out.astype(BF), o_ref[:, 3 * width :], NT)
        for a, s in enumerate(starts):
            attn_ref[pl.ds(s, length), :] = out[a * length : (a + 1) * length]
            part_ref[pl.ds(s, length), :] = part[a * length : (a + 1) * length]

    return near(
        body, [q, k, v, by_distance, query_doc, key_doc, attn_w],
        [((tokens, width), F32), ((half, model), F32), ((half, model), BF)],
        [pltpu.VMEM((tokens, model), F32)],
    )


def attn_backward(q, k, v, by_distance, query_doc, key_doc, attn, grad, one_hot, heads, dim, rows, length, columns):
    buckets = one_hot.shape[1]

    def body(
        q_ref, k_ref, v_ref, w_ref, qd_ref, kd_ref, attn_ref, grad_ref, hot_ref,
        gq_ref, gk_ref, gv_ref, table_ref, diag_ref,
    ):
        diag_ref[...] = jnp.zeros(diag_ref.shape, F32)

        def one_row(row):
            backward_row(
                row, q_ref, k_ref, v_ref, w_ref, qd_ref, kd_ref, attn_ref, grad_ref, gq_ref, gk_ref, gv_ref, diag_ref
            )

        lax.fori_loop(0, rows, lambda row, _: one_row(row), None)
        table = lax.dot_general(
            diag_ref[...], hot_ref[...], (NN, ((), ())), precision=HIGHEST, preferred_element_type=F32
        )
        table = [table[h : h + 1] for h in range(heads)]
        table_ref[...] = jnp.concatenate(table + [jnp.zeros((1, columns - heads * buckets), F32)], axis=1)

    def backward_row(
        row, q_ref, k_ref, v_ref, w_ref, qd_ref, kd_ref, attn_ref, grad_ref, gq_ref, gk_ref, gv_ref, diag_ref
    ):
        own = lax.axis_index("tp")
        grads_q, grads_k, grads_v, diags = [], [], [], []
        for head in range(heads):
            queries, keys, expo, starts, lanes = head_scores(
                own, row, head, dim, rows, length, q_ref, k_ref, w_ref, qd_ref, kd_ref
            )
            values = take_keys(v_ref, starts, length, lanes)
            grads = jnp.concatenate([grad_ref[pl.ds(s, length), lanes] for s in starts], axis=0)
            outs = jnp.concatenate([attn_ref[pl.ds(s, length), lanes] for s in starts], axis=0)
            low = expo.astype(BF)
            totals = jnp.sum(low.astype(F32), axis=1, keepdims=True)
            grad_low = (grads / totals).astype(BF)
            grad_total = -jnp.sum(grads * outs, axis=1, keepdims=True) / totals
            grad_score = (expo * (dot(grad_low, values, NT) + grad_total)).astype(BF)
            grads_q.append(dot(grad_score, keys, NN))
            grads_k.append(dot(grad_score, queries, TN))
            grads_v.append(dot(low, grad_low, TN))
            q_len, k_len = grad_score.shape
            row_at = lax.broadcasted_iota(jnp.int32, (q_len, q_len), 0)
            column_at = lax.broadcasted_iota(jnp.int32, (q_len, q_len), 1)
            flip = jnp.where(row_at + column_at == q_len - 1, 1.0, 0.0).astype(BF)
            turned = dot(flip, grad_score, NN)
            turned = jnp.concatenate([turned, jnp.zeros((q_len, q_len), F32)], axis=1)
            turned = pltpu.roll(turned, 1, 1, stride=1, stride_axis=0)
            diags.append(jnp.sum(turned, axis=0, keepdims=True))
        joined = jnp.concatenate(grads_q, axis=1).astype(BF)
        for a, s in enumerate(starts):
            gq_ref[pl.ds(s, length), :] = joined[a * length : (a + 1) * length]
        for parts, ref in ((grads_k, gk_ref), (grads_v, gv_ref)):
            joined = jnp.concatenate(parts, axis=1).astype(BF)
            for g in range(ref.shape[0]):
                for a, s in enumerate(starts):
                    at = (g * 4 + a) * length
                    ref[g, pl.ds(s, length), :] = joined[at : at + length]
        diag_ref[...] += jnp.concatenate(diags, axis=0)

    return near(
        body, [q, k, v, by_distance, query_doc, key_doc, attn, grad, one_hot],
        [(q.shape, BF), (k.shape, BF), (v.shape, BF), ((1, columns), F32)],
        [pltpu.VMEM(by_distance.shape, F32)],
    )


def in_halves(low, others, tile):
    places = []
    for ref in (low, *others):
        places += [(ref, at) for at in range(0, ref.shape[0], tile)]
    return lambda i: places[i][0][places[i][1] : places[i][1] + tile].astype(F32)


def norm_again(inputs, low, others, gain):
    tokens, model = inputs.shape
    tile = tokens // 4 // max(CUTS // 2, 1)

    def body(x_ref, gain_ref, low_ref, *refs):
        middle_ref, normed_ref = refs[-2:]
        read = in_halves(low_ref, refs[:-2], tile)
        for i in range(tokens // tile):
            rows = slice(i * tile, (i + 1) * tile)
            middle = x_ref[rows].astype(F32) + read(i)
            middle_ref[rows] = middle
            normed_ref[rows] = (middle * rsq_of(middle) * gain_ref[...]).astype(BF)

    return near(body, [inputs, gain, low, *others], [((tokens, model), F32), ((tokens, model), BF)])


def norm_back(middle, cot, low, others, gain, attn_w, width):
    tokens, model = middle.shape
    tile = tokens // 4 // max(CUTS // 2, 1)

    def body(m_ref, cot_ref, gain_ref, w_ref, low_ref, *refs):
        mid_ref, branch_ref, gain_out_ref, attn_ref = refs[-4:]
        read = in_halves(low_ref, refs[:-4], tile)
        gain_sum = jnp.zeros((1, model), F32)
        for i in range(tokens // tile):
            rows = slice(i * tile, (i + 1) * tile)
            grad = read(i)
            middle = m_ref[rows]
            rsq = rsq_of(middle)
            unit = middle * rsq
            scaled = grad * gain_ref[...]
            back = cot_ref[rows].astype(F32) + rsq * (scaled - unit * jnp.mean(scaled * unit, axis=1, keepdims=True))
            mid_ref[rows] = back
            branch_ref[rows] = back.astype(BF)
            gain_sum += jnp.sum(grad * unit, axis=0, keepdims=True)
        gain_out_ref[...] = gain_sum
        attn_ref[...] = dot(branch_ref[...], w_ref[:, 3 * width :], NN)

    return near(
        body, [middle, cot, gain, attn_w, low, *others],
        [((tokens, model), F32), ((tokens, model), BF), ((1, model), F32), ((tokens, width), F32)],
    )


def gated(normed, gate_b, up_b, grad_hidden):
    tokens, model = normed.shape
    ff = grad_hidden.shape[1]
    tile = 256
    scale = math.sqrt(2.0 / math.pi)

    def body(x_ref, gate_ref, up_ref, grad_ref, hidden_ref, pair_ref):
        for at in range(0, ff, tile):
            columns, beside = slice(at, at + tile), slice(ff + at, ff + at + tile)
            gate, up = dot(x_ref[...], gate_ref[:, columns], NN), dot(x_ref[...], up_ref[:, columns], NN)
            square = gate * gate
            tanh = jnp.tanh(scale * gate * (1.0 + 0.044715 * square))
            curve = 0.5 * (1.0 + tanh)
            slope = curve + 0.5 * gate * (1.0 - tanh * tanh) * (scale * (1.0 + 3 * 0.044715 * square))
            activated = gate * curve
            grad = grad_ref[:, columns]
            hidden_ref[:, columns] = (activated * up).astype(BF)
            pair_ref[:, columns] = (grad * up * slope).astype(BF)
            pair_ref[:, beside] = (grad * activated).astype(BF)

    return near(body, [normed, gate_b, up_b, grad_hidden], [((tokens, ff), BF), ((tokens, 2 * ff), BF)])


def times(left, right):
    tokens, ff = left.shape[0], right.shape[1]

    def body(left_ref, right_ref, out_ref):
        for at in range(0, ff, 256):
            out_ref[:, at : at + 256] = dot(left_ref[...], right_ref[:, at : at + 256], NN)

    return near(body, [left, right], [((tokens, ff), F32)])[0]


def weight_grad(left, right, count, first=0, last=None):
    model = left.shape[1]
    last = last or right.shape[1]
    tile, chunk = 384, model // count

    def body(left_ref, right_ref, out_ref):
        for at in range(0, model, tile):
            part = dot(left_ref[:, at : at + tile], right_ref[:, first:last], TN).astype(BF)
            for c in range(tile // chunk):
                out_ref[at // chunk + c] = part[c * chunk : (c + 1) * chunk]

    return near(body, [left, right], [((count, chunk, last - first), BF)])[0]


def back_through(left, rights):
    tokens, model = left.shape[0], rights[0].shape[0]
    half, tile = tokens // 2, 384

    def body(left_ref, *refs):
        keep_ref, give_ref = refs[-2:]
        for at in range(0, model, tile):
            total, first = None, 0
            for ref in refs[:-2]:
                last = first + ref.shape[1]
                term = dot(left_ref[:, first:last], ref[at : at + tile], NT)
                total, first = term if total is None else total + term, last
            keep_ref[:, at : at + tile] = total[:half]
            give_ref[:, at : at + tile] = total[half:].astype(BF)

    return near(body, [left, *rights], [((half, model), F32), ((half, model), BF)])


def attn_weight_grads(normed, inputs, rsq, branch, attn, grads, attn_w, second_part, table, chunk):
    tokens, model = normed.shape
    width = attn.shape[1]
    half, tile = tokens // 2, 384
    each = tile // chunk

    def body(n_ref, x_ref, rsq_ref, b_ref, attn_ref, q_ref, k_ref, v_ref, w_ref, second_ref, table_ref, out_ref, keep_ref, give_ref):
        three = jnp.concatenate([q_ref[...], k_ref[...], v_ref[...]], axis=1)
        attended = attn_ref[...].astype(BF)
        fill = jnp.zeros((1, 4 * width - chunk), F32)
        for at in range(0, model, tile):
            columns = slice(at, at + tile)
            back = dot(three, w_ref[columns, : 3 * width], NT)
            keep_ref[:, columns] = back[:half]
            give_ref[:, columns] = back[half:].astype(BF)
            first = jnp.sum(back * x_ref[:, columns].astype(F32) * rsq_ref[:, 0:1], axis=0, keepdims=True)
            wide = dot(n_ref[:, columns], three, TN).astype(BF)
            last = dot(b_ref[:, columns], attended, TN).astype(BF)
            for c in range(each):
                rows, block = slice(c * chunk, (c + 1) * chunk), at // chunk + c
                out_ref[block, :chunk] = jnp.concatenate([wide[rows], last[rows]], axis=1)
                small = [jnp.concatenate([row[:, rows], fill], axis=1) for row in (first, second_ref[:, columns])]
                small += [table_ref[...], jnp.zeros((EXTRA - 3, 4 * width), F32)]
                out_ref[block, chunk:] = jnp.concatenate(small, axis=0).astype(BF)

    return near(
        body, [normed, inputs, rsq, branch, attn, *grads, attn_w, second_part, table],
        [((model // chunk, chunk + EXTRA, 4 * width), BF), ((half, model), F32), ((half, model), BF)],
    )


def finish_input(addends, inputs, gain, grad_middle):
    count, model = addends[0].shape

    def body(low_ref, got_ref, x_ref, gain_ref, mid_ref, out_ref):
        x = x_ref[:count].astype(F32)
        rsq = rsq_of(x)
        unit = x * rsq
        scaled = (low_ref[...].astype(F32) + got_ref[...].astype(F32)) * gain_ref[...]
        out_ref[...] = mid_ref[:count] + rsq * (scaled - unit * jnp.mean(scaled * unit, axis=1, keepdims=True))

    return near(body, [*addends, inputs, gain, grad_middle], [((count, model), F32)])[0]


def finish_output(addends, middle):
    count, model = addends[0].shape

    def body(low_ref, got_ref, mid_ref, out_ref):
        out_ref[...] = (mid_ref[:count] + low_ref[...].astype(F32) + got_ref[...].astype(F32)).astype(BF)

    return near(body, [*addends, middle], [((count, model), BF)])[0]


def rows_of(values, depth):
    if depth % 16:
        own, value = lax.axis_index("tp"), jnp.concatenate(values, axis=1)
        return [lax.dynamic_slice_in_dim(value, (own ^ k) * depth, depth, 0) for k in range(4)]

    def body(*refs):
        own = lax.axis_index("tp")
        for k in range(4):
            at = 0
            for ref in refs[: len(values)]:
                rows = ref[pl.ds(pl.multiple_of((own ^ k) * depth, depth), depth), :]
                refs[len(values) + k][:, at : at + ref.shape[1]] = rows
                at += ref.shape[1]

    return near(body, values, [((depth, sum(v.shape[1] for v in values)), BF)] * 4)


def unpack_mlp(pieces, count, ff):
    depth, width = pieces[0].shape

    def body(*refs):
        own, outs, held = lax.axis_index("tp"), refs[4:-1], refs[-1]
        for k in range(4):
            held[own ^ k] = refs[k][...]
        for i, out in enumerate(outs):
            for a in range(4):
                last = min(count, (a + 1) * ff)
                out[:, a * ff : last] = held[a, :, i * ff : i * ff + last - a * ff].astype(F32)

    return near(body, pieces, [((depth, count), F32)] * (width // ff), [pltpu.VMEM((4, depth, width), BF)])


def unpack_attn(pieces, depth, width, heads, buckets):
    rows = pieces[0].shape[0]

    def body(*refs):
        own, grads, first_ref, second_ref, table_ref, held = lax.axis_index("tp"), refs[4:8], *refs[8:]
        for k in range(4):
            held[own ^ k] = refs[k][...].astype(F32)
        for i, out in enumerate(grads):
            for a in range(4):
                out[:, a * width : (a + 1) * width] = held[a, :depth, i * width : (i + 1) * width]
        small = [held[a, depth : depth + EXTRA] for a in range(4)]
        first_ref[...] = sum(p[0:1, :depth] for p in small)
        second_ref[...] = small[0][1:2, :depth]
        for a in range(4):
            for h in range(heads):
                table_ref[a * heads + h : a * heads + h + 1] = small[a][2:3, h * buckets : (h + 1) * buckets]

    outs = [((depth, 4 * width), F32)] * 4 + [((1, depth), F32)] * 2 + [((4 * heads, buckets), F32)]
    return near(body, pieces, outs, [pltpu.VMEM((4, rows, 4 * width), F32)])


ORDER = (
    "C0", "Pa", "Pm", "a1", "a2", "I0", "M0", "g1", "a3", "g2", "a4", "I1s0", "I1e", "u1", "d1", "a5", "C1s0",
    "QK", "R0s0", "g3", "d2", "g4", "u2", "R0e", "d3", "u3", "R2s0", "d4", "u4", "d5", "C1e", "DH", "R2e", "g5",
    "u5", "ML", "rm1", "O0s0", "rd1", "B0s0", "rm2", "rd2", "B0e", "O0e", "rm3", "rd3", "B2s0", "B2e", "AB",
    "rm4", "WA", "ra1", "rd4", "ra2", "N0s0", "O2", "N0e", "rm5", "Xu0", "Xu1", "Xu2", "ra3", "Xu3", "ra4", "rd5",
    "Xd0", "Xd1", "N2", "Xd2", "ra5", "Xa0", "Xa1", "Xa2", "Xd3", "Xa3",
)


def shards(
    block_input, cotangent, query_w, key_w, value_w, output_w, gate_w, up_w, down_w,
    first_gain, second_gain, bias_table, rel_bucket, doc_ids,
):
    rows, length, model = block_input.shape
    tokens = rows * length
    own = lax.axis_index("tp")
    parts = lax.axis_size("seq")
    count = lax.axis_size("rows") * parts
    bucket_count, head_count = bias_table.shape
    inner = query_w.shape[1]
    heads = head_count // 4
    dim = inner // head_count
    width = heads * dim
    depth = query_w.shape[0]
    chunk = 4 * depth
    hidden_count = gate_w.shape[1]
    ff = -(-hidden_count // (4 * 256)) * 256
    seq_len = doc_ids.shape[1]
    q_len = 4 * length
    shape = (heads, dim, rows, length)
    lanes = Lanes(count, 4)
    steps, tasks, have = {}, {}, {}

    def do(name):
        def keep(work):
            steps[name] = work
        return keep

    def task(key, names, make):
        def start():
            tasks[key] = Task(make())
            tasks[key].step()

        def end():
            have[key] = tasks[key].result()

        steps.update({name: lambda: tasks[key].step() for name in names})
        steps[names[0]], steps[names[-1]] = start, end

    def core(name):
        return [f"{name}s{n}" for n in range(CUTS)] + [f"{name}e"]

    def attn_blocks():
        weights = [query_w, key_w, value_w, output_w.T]
        gains = [first_gain.reshape(1, depth), second_gain.reshape(1, depth)]
        if depth % 16 == 0:
            return pack_attn(weights, gains, width)
        gains = jnp.pad(jnp.concatenate(gains, axis=0).astype(BF), ((0, EXTRA - 2), (0, 4 * width - depth)))
        return pack_plain(weights, width, gains)

    def mlp_blocks():
        weights = [down_w.T, gate_w, up_w]
        return pack_mlp(weights, ff) if depth % 16 == 0 else pack_plain(weights, ff, None)

    def attn_chunk():
        return gather_ring(lanes, stack_attn(tasks["Pa"].result(), chunk), chunk, 1)

    task("Pa", ["Pa", "Pa-"], lambda: exchange(lanes, attn_blocks()))
    task("Pm", ["Pm", "M0"], lambda: exchange(lanes, mlp_blocks()))
    task("a", ["a1", "a2", "a3", "a4", "a5"], attn_chunk)

    def mlp_chunk(i):
        if "chunks" not in have:
            have["chunks"] = stack_members(have["Pm"], [ff] * 3, PADS if ring_ok(count) else (0, 0, 0))
        return have["chunks"][i]

    task("d", ["d1", "d2", "d3", "d4", "d5"], lambda: gather_ring(lanes, mlp_chunk(0), chunk, -1))
    task("g", ["g1", "g2", "g3", "g4", "g5"], lambda: gather_ring(lanes, mlp_chunk(1), chunk, 1))
    task("u", ["u1", "u2", "u3", "u4", "u5"], lambda: gather_ring(lanes, mlp_chunk(2), chunk, -1))

    task("in", ["I0", *core("I1")], lambda: gather_tokens(lanes, block_input.reshape(tokens, model)))
    task("cot", ["C0", *core("C1")], lambda: gather_tokens(lanes, cotangent.reshape(tokens, model)))

    @do("QK")
    def _():
        one_hot = (rel_bucket[:, None] == jnp.arange(bucket_count, dtype=jnp.int32)).astype(F32)
        first = lax.axis_index("seq") * q_len
        one_hot = lax.dynamic_slice_in_dim(one_hot, seq_len - first - q_len, seq_len + q_len, 0)
        own_table = lax.dynamic_slice_in_dim(bias_table, own * heads, heads, 1)
        by_distance = lax.dot_general(own_table, one_hot, (((0,), (1,)), ((), ())), precision=HIGHEST)
        query_doc = lax.dynamic_slice_in_dim(doc_ids, first, q_len, 1)[:, :, None]
        attn_w, chunks = have["a"]
        gain_one, gain_two = spread_gains(chunks, chunk)
        normed, rsq_one, queries, keys, values = project(have["in"], gain_one, attn_w, width)
        queries = lanes.pin(queries)
        if parts > 1:
            keys = lax.all_gather(keys, "seq", axis=0)
            values = lax.all_gather(values, "seq", axis=0)
        else:
            keys, values = keys[None], values[None]
        have.update(
            one_hot=one_hot, attn_w=attn_w, gain_one=gain_one, gain_two=gain_two, normed=normed, rsq_one=rsq_one,
            scores=(queries, keys, values, by_distance, query_doc, doc_ids[:, None, :]),
        )

    def attention():
        have["attn"], keep, give = attn_forward(*have["scores"], have["attn_w"], *shape)
        return sum_tokens(lanes, keep, give)

    task("branch", [*core("R0"), *core("R2")], attention)

    @do("DH")
    def _():
        have["grad_hidden"] = lanes.pin(times(have["cot"], have["d"][0]))

    @do("ML")
    def _():
        middle, normed_mlp = norm_again(have["in"], *have["branch"], have["gain_two"])
        hidden, grad_pair = gated(normed_mlp, have["g"][0], have["u"][0], have["grad_hidden"])
        have.update(middle=middle, normed_mlp=normed_mlp, hidden=lanes.pin(hidden), grad_pair=grad_pair)

    task(
        "rd", ["rd1", "rd2", "rd3", "rd4", "rd5"],
        lambda: scatter_ring(lanes, weight_grad(have["cot"], have["hidden"], count), 1, chunk + RPADS[0]),
    )
    task(
        "back", [*core("B0"), *core("B2")],
        lambda: sum_tokens(lanes, *back_through(have["grad_pair"], [have["g"][0], have["u"][0]])),
    )
    if "rm1" in ORDER:
        task(
            "rm", ["rm1", "rm2", "rm3", "rm4", "rm5"],
            lambda: scatter_ring(lanes, weight_grad(have["normed_mlp"], have["grad_pair"], count), -1, chunk + RPADS[1]),
        )
    else:
        @do("WU")
        def _():
            have["up_blocks"] = lanes.pin(weight_grad(have["normed_mlp"], have["grad_pair"], count, ff, 2 * ff))

        task(
            "rg", ["rg1", "rg2", "rg3", "rg4", "rg5"],
            lambda: scatter_ring(
                lanes, weight_grad(have["normed_mlp"], have["grad_pair"], count, 0, ff), -1, chunk + RPADS[1]
            ),
        )
        task("ru", ["ru1", "ru2", "ru3", "ru4", "ru5"], lambda: scatter_ring(lanes, have["up_blocks"], 1, chunk + RPADS[2]))
    task("out", [*core("O0"), "O2"], lambda: scatter_tokens(lanes, *back_through(have["hidden"], [have["d"][0]])))

    @do("AB")
    def _():
        grad_middle, grad_branch, second_part, grad_attn = norm_back(
            have["middle"], have["cot"], *have["back"], have["gain_two"], have["attn_w"], width
        )
        grad_q, grad_k, grad_v, table = attn_backward(
            *have["scores"], have["attn"], lanes.pin(grad_attn), have["one_hot"], *shape, 4 * width
        )
        if parts > 1:
            grad_k = lax.psum_scatter(grad_k, "seq", scatter_dimension=0, tiled=True)
            grad_v = lax.psum_scatter(grad_v, "seq", scatter_dimension=0, tiled=True)
        have.update(
            grad_middle=grad_middle, grad_branch=grad_branch, second_part=second_part, table=table,
            grads=(lanes.pin(grad_q), grad_k[0], grad_v[0]),
        )

    @do("WA")
    def _():
        four_grad, keep, give = attn_weight_grads(
            have["normed"], have["in"], have["rsq_one"], have["grad_branch"], have["attn"], have["grads"],
            have["attn_w"], have["second_part"], have["table"], chunk,
        )
        have.update(four_grad=lanes.pin(four_grad), in_parts=(keep, give))

    task("ra", ["ra1", "ra2", "ra3", "ra4", "ra5"], lambda: scatter_ring(lanes, have["four_grad"], -1, chunk + EXTRA))
    task("grad_in", [*core("N0"), "N2"], lambda: scatter_tokens(lanes, *have["in_parts"]))

    if "rm1" in ORDER:
        one, two = ["rd"], ["rm"]
    else:
        one, two = ["rd", "rg"], ["ru"]
    task("Xd", ["Xd0", "Xd1", "Xd2", "Xd3"], lambda: exchange(lanes, rows_of([have[k] for k in one], depth), False))
    task("Xu", ["Xu0", "Xu1", "Xu2", "Xu3"], lambda: exchange(lanes, rows_of([have[k] for k in two], depth), False))
    task("Xa", ["Xa0", "Xa1", "Xa2", "Xa3"], lambda: exchange(lanes, split_attn(have["ra"], depth, width), False))

    for name in ORDER:
        steps[name]()
    block_output = finish_output(have["out"], have["middle"])
    input_grad = finish_input(have["grad_in"], have["in"], have["gain_one"], have["grad_middle"])

    mlp = unpack_mlp(have["Xd"], hidden_count, ff) + unpack_mlp(have["Xu"], hidden_count, ff)
    *grads, first_grad, second_grad, table_grad = unpack_attn(have["Xa"], depth, width, heads, bucket_count)
    return (
        block_output.reshape(rows, length, model), input_grad.reshape(rows, length, model),
        grads[0], grads[1], grads[2], grads[3].T,
        mlp[1], mlp[2], mlp[0].T, first_grad.reshape(depth), second_grad.reshape(depth), table_grad.T,
    )


def solution(mesh):
    row_count, blk_count = mesh.shape["rows"], mesh.shape["blk"]
    fine = Mesh(mesh.devices.reshape(row_count, blk_count // 4, 4), ("rows", "seq", "tp"))
    every = ("rows", "seq", "tp")
    tokens = P("rows", ("seq", "tp"), None)
    deep, wide, flat = P(every, None), P(None, every), P(every)
    return jax.shard_map(
        shards,
        mesh=fine,
        in_specs=(tokens, tokens, deep, deep, deep, wide, deep, deep, wide, flat, flat, P(), P(), P("rows", None)),
        out_specs=(tokens, tokens, deep, deep, deep, wide, deep, deep, wide, flat, flat, P()),
        check_vma=False,
    )
```

```python
import math

import jax
import jax.numpy as jnp
from jax import lax
from jax.experimental import pallas as pl
from jax.experimental.pallas import tpu as pltpu
from jax.sharding import Mesh, PartitionSpec as P

EPSILON = 1e-06
BF = jnp.bfloat16
F32 = jnp.float32
HIGHEST = lax.Precision.HIGHEST
RING = ("rows", "seq")
MAX_RING = 8
EXTRA = 16
PADS = (8, 6, 4)
RPADS = (8, 4, 8)
CUTS = (2, 1)
FREE = pl.CostEstimate(flops=0, transcendentals=0, bytes_accessed=0)


def dot(left, right, dims, out=F32):
    return lax.dot_general(left, right, (dims, ((), ())), preferred_element_type=out)


NN = ((1,), (0,))
NT = ((1,), (1,))
TN = ((0,), (0,))


def ring_order(count):
    return list(range(0, count, 2)) + list(range(count - 1, 0, -2))


def ring_places(count):
    half = count // 2
    group = lax.axis_index(RING)
    place = jnp.where(group % 2 == 0, group // 2, count - 1 - group // 2)
    places = []
    for k in range(count):
        at = place - k
        at = jnp.where(at < 0, at + count, at)
        places.append(jnp.where(at < half, 2 * at, 2 * (count - 1 - at) + 1))
    return places


def ring_ok(count):
    return count <= MAX_RING and count % 2 == 0


class Lanes:
    def __init__(self, count, ways):
        order = ring_order(count)
        self.pairs = {
            step: [(order[i], order[(i + step) % count]) for i in range(count)] for step in (1, -1)
        }
        self.count, self.ways, self.last = count, ways, None

    def pin(self, *values):
        if self.last is not None:
            values = lax.optimization_barrier((*values, self.last))[:-1]
        self.last = values[0]
        return values if len(values) > 1 else values[0]

    def shift(self, value, step):
        return lax.ppermute(value, RING, self.pairs[step])

    def partner(self, value, bit):
        return lax.ppermute(value, "tp", [(i, i ^ bit) for i in range(self.ways)])


class Task:
    def __init__(self, steps):
        self.steps, self.value = steps, None

    def step(self):
        if self.steps is not None:
            try:
                next(self.steps)
            except StopIteration as stop:
                self.value, self.steps = stop.value, None

    def result(self):
        while self.steps is not None:
            self.step()
        return self.value


def gather_ring(lanes, chunk, keep, lead):
    count = lanes.count
    if not ring_ok(count):
        got = lax.all_gather(chunk, RING, axis=0) if count > 1 else chunk[None]
        return got[:, :keep].reshape(-1, chunk.shape[1]), [got[i] for i in range(count)]
    chunk = lanes.pin(chunk)
    moving = {lead: chunk, -lead: chunk}
    got = [chunk]
    for k in range(1, count // 2):
        moving = {step: lanes.shift(value, step) for step, value in moving.items()}
        yield
        moving = dict(zip(moving, lanes.pin(*moving.values())))
        got += [moving[1], moving[-1]]
    last = lanes.shift(moving[lead], lead)
    yield
    got.append(lanes.pin(last))
    return place_rows(got, count, keep), got


def chunk_order(count):
    order = [0]
    for k in range(1, count // 2):
        order += [k, count - k]
    return order + [count // 2]


def place_rows(got, count, keep):
    def body(*refs):
        places = ring_places(count)
        for ref, k in zip(refs, chunk_order(count)):
            refs[-1][pl.ds(pl.multiple_of(places[k] * keep, keep), keep), :] = ref[:keep]

    return near(body, got, [((count * keep, got[0].shape[1]), BF)])[0]


def scatter_ring(lanes, blocks, lead, rows):
    count, size, _ = blocks.shape
    if count == 1:
        return blocks[0]
    if not ring_ok(count):
        return lax.psum_scatter(blocks, RING, scatter_dimension=0, tiled=True)[0]
    (far,) = add_blocks(blocks, [(count // 2, None)], rows)
    moving = {lead: lanes.shift(lanes.pin(far), lead)}
    yield
    for j in range(count // 2 - 1, 0, -1):
        arrived = dict(zip(moving, lanes.pin(*moving.values()) if len(moving) > 1 else (lanes.pin(moving[lead]),)))
        sums = add_blocks(blocks, [(-j * step, arrived.get(step)) for step in (1, -1)], rows)
        moving = {step: lanes.shift(value, step) for step, value in zip((1, -1), lanes.pin(*sums))}
        yield
    came, back = lanes.pin(*moving.values())
    return add_blocks(blocks, [(0, came)], size, back)[0]


def add_blocks(blocks, terms, rows, more=None):
    count, size, width = blocks.shape
    came = [c for _, c in terms if c is not None] + ([] if more is None else [more])

    def body(blocks_ref, *refs):
        places = ring_places(count)
        given, outs = list(refs[: len(came)]), refs[len(came) :]
        for (k, c), out in zip(terms, outs):
            total = blocks_ref[places[k % count]].astype(F32)
            if c is not None:
                total = total + given.pop(0)[:size].astype(F32)
            if more is not None:
                total = total + given.pop(0)[:size].astype(F32)
            out[:size] = total.astype(BF)
            if rows > size:
                out[size:] = jnp.zeros((rows - size, width), BF)

    return near(body, [blocks, *came], [((rows, width), BF)] * len(terms))


def block_of(index):
    return index % 2 * 2 + index // 2


def gather_tokens(lanes, value, cuts):
    value = lanes.pin(value)
    got = lanes.partner(value, 2)
    yield
    value = jnp.concatenate([value, lanes.pin(got)], axis=0)
    got = yield from over_core(lanes, value, cuts)
    return jnp.concatenate([value, *got], axis=0)


def over_core(lanes, give, cuts):
    rows, pieces, first = give.shape[0], [], 0
    for n in range(cuts):
        last = rows * (n + 1) // cuts // 16 * 16 if n + 1 < cuts else rows
        got = lanes.partner(lanes.pin(give[first:last]), 1)
        yield
        pieces.append(lanes.pin(got))
        first = last
    return pieces


def sum_tokens(lanes, keep, give, cuts):
    got = yield from over_core(lanes, give, cuts)
    low = lanes.pin(add_halves(keep, got, False))
    got = lanes.partner(low, 2)
    yield
    low = lanes.pin(add_halves(low, [lanes.pin(got)], True))
    got = yield from over_core(lanes, low, cuts)
    return low, got


def add_halves(left, pieces, swapped):
    rows = left.shape[0]
    half = rows // 2

    def body(left_ref, *refs):
        first = 0
        for ref in refs[:-1]:
            for at in range(0, ref.shape[0], half if swapped else ref.shape[0]):
                count = half if swapped else ref.shape[0]
                to = half - at if swapped else first + at
                total = left_ref[to : to + count].astype(F32) + ref[at : at + count].astype(F32)
                refs[-1][to : to + count] = total.astype(BF)
            first += ref.shape[0]

    return near(body, [left, *pieces], [(left.shape, BF)])[0]


def scatter_tokens(lanes, keep, give, cuts):
    got = yield from over_core(lanes, give, cuts)
    low = lanes.pin(add_halves(keep, got, False))
    mine = low.shape[0] // 2
    got = lanes.partner(low[mine:], 2)
    yield
    return low[:mine], lanes.pin(got)


def exchange(lanes, blocks, at_once=True):
    pieces = [blocks[0]] + [None] * 3
    for k in (2, 3, 1):
        pieces[k] = lanes.partner(lanes.pin(blocks[k]), k)
        if not at_once:
            yield
    if at_once:
        yield
    pieces[1:] = lanes.pin(*pieces[1:])
    return pieces


def by_member(pieces):
    own, chosen = lax.axis_index("tp"), []
    for a in range(4):
        piece = pieces[a]
        for mine in range(1, 4):
            piece = jnp.where(own == mine, pieces[a ^ mine], piece)
        chosen.append(piece)
    return chosen


def stack_members(pieces, widths, pads):
    depth = pieces[0].shape[0]
    if depth % 16:
        pieces = jnp.concatenate(by_member(pieces), axis=0)
        starts = [sum(widths[:i]) for i in range(len(widths))]
        return [jnp.pad(pieces[:, a : a + w], ((0, p), (0, 0))) for a, w, p in zip(starts, widths, pads)]

    def body(*refs):
        own = lax.axis_index("tp")
        at = 0
        for width, pad, out in zip(widths, pads, refs[4:]):
            for k in range(4):
                out[pl.ds(pl.multiple_of((own ^ k) * depth, depth), depth), :] = refs[k][:, at : at + width]
            if pad:
                out[4 * depth :] = jnp.zeros((pad, width), BF)
            at += width

    return near(body, pieces, [((4 * depth + pad, width), BF) for width, pad in zip(widths, pads)])


def stack_attn(pieces, chunk):
    depth, width = chunk // 4, pieces[0].shape[1]
    if depth % 16:
        pieces = by_member(pieces)
        gains = jnp.concatenate([p[depth : depth + 2, :depth] for p in pieces], axis=1)
        gains = jnp.pad(gains, ((0, EXTRA - 2), (0, width - chunk)))
        return jnp.concatenate([p[:depth] for p in pieces] + [gains], axis=0)

    def body(*refs):
        own, out, gains_ref = lax.axis_index("tp"), refs[4], refs[5]
        for k in range(4):
            out[pl.ds(pl.multiple_of((own ^ k) * depth, depth), depth), :] = refs[k][:depth]
            gains_ref[own ^ k] = refs[k][depth:, :depth].astype(F32)
        gains = [gains_ref[a] for a in range(4)] + [jnp.zeros((EXTRA, width - chunk), F32)]
        out[chunk:] = jnp.concatenate(gains, axis=1).astype(BF)

    return near(body, pieces, [((chunk + EXTRA, width), BF)], [pltpu.VMEM((4, EXTRA, depth), F32)])[0]


def split_attn(total, depth, width):
    chunk = 4 * depth
    if depth % 16:
        tables = jnp.pad(total[chunk + 2 : chunk + 3], ((2, EXTRA - 3), (0, 0)))
        blocks = []
        for large, pair in zip(rows_of([total], depth), rows_of([total[chunk : chunk + 2, :chunk].T], depth)):
            pair = jnp.pad(pair.T, ((0, EXTRA - 2), (0, 4 * width - depth)))
            blocks.append(jnp.concatenate([large, pair + tables], axis=0))
        return blocks

    def body(total_ref, *refs):
        own, small_ref = lax.axis_index("tp"), refs[4]
        fill = jnp.zeros((2, 4 * width - depth), F32)
        small = total_ref[chunk : chunk + EXTRA].astype(F32)
        below = jnp.concatenate([small[2:3], jnp.zeros((EXTRA - 3, 4 * width), F32)], axis=0)
        for a in range(4):
            pair = jnp.concatenate([small[0:2, a * depth : (a + 1) * depth], fill], axis=1)
            small_ref[a] = jnp.concatenate([pair, below], axis=0)
        for k in range(4):
            refs[k][:depth] = total_ref[pl.ds(pl.multiple_of((own ^ k) * depth, depth), depth), :]
            refs[k][depth:] = small_ref[own ^ k].astype(BF)

    return near(
        body, [total], [((depth + EXTRA, 4 * width), BF)] * 4, [pltpu.VMEM((4, EXTRA, 4 * width), F32)]
    )


def run(body, grid, ins, outs, scratch=(), vmem=24):
    def spec(block, index_map):
        return pl.BlockSpec(block, index_map)

    arrays, in_specs = [], []
    for item in ins:
        array, block, index_map = item if isinstance(item, tuple) else (item, item.shape, None)
        if index_map is None:
            index_map = lambda *_, n=array.ndim: (0,) * n
        arrays.append(array)
        in_specs.append(spec(block, index_map))
    out_specs = [
        spec(block or shape, index_map or (lambda *_, n=len(shape): (0,) * n)) for shape, _, block, index_map in outs
    ]
    return pl.pallas_call(
        body, grid=grid, in_specs=in_specs, out_specs=out_specs,
        out_shape=[jax.ShapeDtypeStruct(shape, dtype) for shape, dtype, _, _ in outs],
        scratch_shapes=list(scratch),
        compiler_params=pltpu.CompilerParams(
            dimension_semantics=("arbitrary",) * len(grid), vmem_limit_bytes=vmem << 20
        ),
        cost_estimate=FREE,
    )(*arrays)


def near(body, arrays, outs, scratch=(), vmem=16):
    spec = pl.BlockSpec(memory_space=pltpu.VMEM)
    return pl.pallas_call(
        body, in_specs=[spec] * len(arrays), out_specs=[spec] * len(outs),
        out_shape=[jax.ShapeDtypeStruct(shape, dtype) for shape, dtype in outs],
        scratch_shapes=list(scratch),
        compiler_params=pltpu.CompilerParams(vmem_limit_bytes=vmem << 20),
        cost_estimate=FREE,
    )(*arrays)


def far(arrays):
    return [pltpu.with_memory_space_constraint(a, pltpu.HBM) for a in arrays]


def whole(shape, dtype):
    return (shape, dtype, None, None)


def pack_attn(weights, gains, width):
    depth, inner = weights[0].shape

    def body(q_ref, k_ref, v_ref, o_ref, first_ref, second_ref, *rest):
        outs, out_ref = rest[:4], rest[4]
        own = lax.axis_index("tp")
        extra = jnp.concatenate([first_ref[...], second_ref[...], jnp.zeros((EXTRA - 2, depth), F32)], axis=0)
        extra = jnp.concatenate([extra, jnp.zeros((EXTRA, 4 * width - depth), F32)], axis=1).astype(BF)
        for a in range(4):
            parts = [r[:, a * width : (a + 1) * width] for r in (q_ref, k_ref, v_ref, o_ref)]
            out_ref[a ^ own, :depth] = jnp.concatenate(parts, axis=1).astype(BF)
            out_ref[a ^ own, depth:] = extra
        for k in range(4):
            outs[k][...] = out_ref[k]

    shape = (depth + EXTRA, 4 * width)
    return run(body, (1,), far([*weights, *gains]), [whole(shape, BF)] * 4, [pltpu.VMEM((4, *shape), BF)])


def pack_mlp(weights, ff):
    depth, count = weights[0].shape

    def body(*refs):
        own, out_ref = lax.axis_index("tp"), refs[-1]
        for a in range(4):
            parts = []
            for ref in refs[: len(weights)]:
                last = min(count, (a + 1) * ff)
                parts.append(ref[:, a * ff : last])
                if last < (a + 1) * ff:
                    parts.append(jnp.zeros((depth, (a + 1) * ff - last), F32))
            out_ref[a ^ own] = jnp.concatenate(parts, axis=1).astype(BF)
        for k in range(4):
            refs[len(weights) + k][...] = out_ref[k]

    shape = (depth, len(weights) * ff)
    return run(body, (1,), far(weights), [whole(shape, BF)] * 4, [pltpu.VMEM((4, *shape), BF)])


def pack_plain(weights, width, extra):
    own = lax.axis_index("tp")
    weights = [jnp.pad(w.astype(BF), ((0, 0), (0, 4 * width - w.shape[1]))) for w in weights]
    blocks = []
    for k in range(4):
        block = jnp.concatenate([lax.dynamic_slice_in_dim(w, (own ^ k) * width, width, 1) for w in weights], axis=1)
        blocks.append(block if extra is None else jnp.concatenate([block, extra], axis=0))
    return blocks


def spread_gains(chunks, chunk):
    count = len(chunks)
    ring = ring_ok(count)

    def body(*refs):
        one_ref, two_ref, rows_ref = refs[-3:]
        places = ring_places(count) if ring else None
        for ref, k in zip(refs, chunk_order(count) if ring else range(count)):
            rows_ref[places[k] if ring else k] = ref[chunk : chunk + 2, :chunk].astype(F32)
        both = jnp.concatenate([rows_ref[r] for r in range(count)], axis=1)
        one_ref[...], two_ref[...] = both[0:1], both[1:2]

    return near(body, chunks, [((1, count * chunk), F32)] * 2, [pltpu.VMEM((count, 2, chunk), F32)])


def tiles(total, tile, work):
    lax.fori_loop(0, total // tile, lambda i, _: work(pl.multiple_of(i * tile, tile)), None)


def rsq_of(value):
    return lax.rsqrt(jnp.mean(value * value, axis=1, keepdims=True) + EPSILON)


def project(inputs, gain, weights, width):
    tokens, model = inputs.shape
    tile = tokens // 2

    def body(x_ref, gain_ref, w_ref, normed_ref, rsq_ref, q_ref, k_ref, v_ref):
        for at in range(0, tokens, tile):
            rows = slice(at, at + tile)
            x = x_ref[rows].astype(F32)
            rsq = rsq_of(x)
            normed = (x * rsq * gain_ref[...]).astype(BF)
            normed_ref[rows] = normed
            rsq_ref[rows] = jnp.broadcast_to(rsq, (tile, 128))
            three = dot(normed, w_ref[:, : 3 * width], NN).astype(BF)
            for i, ref in enumerate((q_ref, k_ref, v_ref)):
                ref[rows] = three[:, i * width : (i + 1) * width]

    return near(
        body, [inputs, gain, weights],
        [((tokens, model), BF), ((tokens, 128), F32)] + [((tokens, width), BF)] * 3,
    )


def head_scores(own, row, head, dim, rows, length, q_ref, k_ref, w_ref, qd_ref, kd_ref):
    lanes = slice(head * dim, (head + 1) * dim)
    starts = [pl.multiple_of((block_of(own ^ a) * rows + row) * length, length) for a in range(4)]
    queries = jnp.concatenate([q_ref[pl.ds(s, length), lanes] for s in starts], axis=0)
    keys = take_keys(k_ref, starts, length, lanes)
    q_len, k_len = queries.shape[0], keys.shape[0]
    scores = dot(queries, keys, NT)
    bias = jnp.broadcast_to(w_ref[pl.ds(head, 1), :], (q_len, q_len + k_len))
    bias = pltpu.roll(bias, k_len, 1, stride=1, stride_axis=0)[:, :k_len]
    same = qd_ref[row] == kd_ref[row]
    expo = jnp.where(same, jnp.exp(scores + bias), 0.0)
    return queries, keys, expo, starts, lanes


def take_keys(ref, starts, length, lanes):
    return jnp.concatenate(
        [ref[g, pl.ds(s, length), lanes] for g in range(ref.shape[0]) for s in starts], axis=0
    )


def attn_forward(q, k, v, by_distance, query_doc, key_doc, attn_w, heads, dim, rows, length):
    tokens, width = q.shape
    model = attn_w.shape[0]
    half = tokens // 2

    def body(q_ref, k_ref, v_ref, w_ref, qd_ref, kd_ref, o_ref, attn_ref, keep_ref, give_ref, part_ref):
        def one_row(row):
            forward_row(row, q_ref, k_ref, v_ref, w_ref, qd_ref, kd_ref, o_ref, attn_ref, part_ref)

        lax.fori_loop(0, rows, lambda row, _: one_row(row), None)
        keep_ref[...] = part_ref[:half]
        give_ref[...] = part_ref[half:].astype(BF)

    def forward_row(row, q_ref, k_ref, v_ref, w_ref, qd_ref, kd_ref, o_ref, attn_ref, part_ref):
        own, out = lax.axis_index("tp"), []
        for head in range(heads):
            _, _, expo, starts, lanes = head_scores(
                own, row, head, dim, rows, length, q_ref, k_ref, w_ref, qd_ref, kd_ref
            )
            values = take_keys(v_ref, starts, length, lanes)
            low = expo.astype(BF)
            totals = jnp.sum(low.astype(F32), axis=1, keepdims=True)
            out.append(dot(low, values, NN) / totals)
        out = jnp.concatenate(out, axis=1)
        part = dot(out.astype(BF), o_ref[:, 3 * width :], NT)
        for a, s in enumerate(starts):
            attn_ref[pl.ds(s, length), :] = out[a * length : (a + 1) * length]
            part_ref[pl.ds(s, length), :] = part[a * length : (a + 1) * length]

    return near(
        body, [q, k, v, by_distance, query_doc, key_doc, attn_w],
        [((tokens, width), F32), ((half, model), F32), ((half, model), BF)],
        [pltpu.VMEM((tokens, model), F32)],
    )


def attn_backward(q, k, v, by_distance, query_doc, key_doc, attn, grad, one_hot, heads, dim, rows, length, columns):
    buckets = one_hot.shape[1]

    def body(
        q_ref, k_ref, v_ref, w_ref, qd_ref, kd_ref, attn_ref, grad_ref, hot_ref,
        gq_ref, gk_ref, gv_ref, table_ref, diag_ref,
    ):
        diag_ref[...] = jnp.zeros(diag_ref.shape, F32)

        def one_row(row):
            backward_row(
                row, q_ref, k_ref, v_ref, w_ref, qd_ref, kd_ref, attn_ref, grad_ref, gq_ref, gk_ref, gv_ref, diag_ref
            )

        lax.fori_loop(0, rows, lambda row, _: one_row(row), None)
        table = lax.dot_general(
            diag_ref[...], hot_ref[...], (NN, ((), ())), precision=HIGHEST, preferred_element_type=F32
        )
        table = [table[h : h + 1] for h in range(heads)]
        table_ref[...] = jnp.concatenate(table + [jnp.zeros((1, columns - heads * buckets), F32)], axis=1)

    def backward_row(
        row, q_ref, k_ref, v_ref, w_ref, qd_ref, kd_ref, attn_ref, grad_ref, gq_ref, gk_ref, gv_ref, diag_ref
    ):
        own = lax.axis_index("tp")
        grads_q, grads_k, grads_v, diags = [], [], [], []
        for head in range(heads):
            queries, keys, expo, starts, lanes = head_scores(
                own, row, head, dim, rows, length, q_ref, k_ref, w_ref, qd_ref, kd_ref
            )
            values = take_keys(v_ref, starts, length, lanes)
            grads = jnp.concatenate([grad_ref[pl.ds(s, length), lanes] for s in starts], axis=0)
            outs = jnp.concatenate([attn_ref[pl.ds(s, length), lanes] for s in starts], axis=0)
            low = expo.astype(BF)
            totals = jnp.sum(low.astype(F32), axis=1, keepdims=True)
            grad_low = (grads / totals).astype(BF)
            grad_total = -jnp.sum(grads * outs, axis=1, keepdims=True) / totals
            grad_score = (expo * (dot(grad_low, values, NT) + grad_total)).astype(BF)
            grads_q.append(dot(grad_score, keys, NN))
            grads_k.append(dot(grad_score, queries, TN))
            grads_v.append(dot(low, grad_low, TN))
            q_len, k_len = grad_score.shape
            row_at = lax.broadcasted_iota(jnp.int32, (q_len, q_len), 0)
            column_at = lax.broadcasted_iota(jnp.int32, (q_len, q_len), 1)
            flip = jnp.where(row_at + column_at == q_len - 1, 1.0, 0.0).astype(BF)
            turned = dot(flip, grad_score, NN)
            turned = jnp.concatenate([turned, jnp.zeros((q_len, q_len), F32)], axis=1)
            turned = pltpu.roll(turned, 1, 1, stride=1, stride_axis=0)
            diags.append(jnp.sum(turned, axis=0, keepdims=True))
        joined = jnp.concatenate(grads_q, axis=1).astype(BF)
        for a, s in enumerate(starts):
            gq_ref[pl.ds(s, length), :] = joined[a * length : (a + 1) * length]
        for parts, ref in ((grads_k, gk_ref), (grads_v, gv_ref)):
            joined = jnp.concatenate(parts, axis=1).astype(BF)
            for g in range(ref.shape[0]):
                for a, s in enumerate(starts):
                    at = (g * 4 + a) * length
                    ref[g, pl.ds(s, length), :] = joined[at : at + length]
        diag_ref[...] += jnp.concatenate(diags, axis=0)

    return near(
        body, [q, k, v, by_distance, query_doc, key_doc, attn, grad, one_hot],
        [(q.shape, BF), (k.shape, BF), (v.shape, BF), ((1, columns), F32)],
        [pltpu.VMEM(by_distance.shape, F32)],
    )


def in_halves(low, others, tile):
    places = []
    for ref in (low, *others):
        places += [(ref, at) for at in range(0, ref.shape[0], tile)]
    return lambda i: places[i][0][places[i][1] : places[i][1] + tile].astype(F32)


def norm_again(inputs, low, others, gain):
    tokens, model = inputs.shape
    tile = tokens // 4

    def body(x_ref, gain_ref, low_ref, *refs):
        middle_ref, normed_ref = refs[-2:]
        read = in_halves(low_ref, refs[:-2], tile)
        for i in range(tokens // tile):
            rows = slice(i * tile, (i + 1) * tile)
            middle = x_ref[rows].astype(F32) + read(i)
            middle_ref[rows] = middle
            normed_ref[rows] = (middle * rsq_of(middle) * gain_ref[...]).astype(BF)

    return near(body, [inputs, gain, low, *others], [((tokens, model), F32), ((tokens, model), BF)])


def norm_back(middle, cot, low, others, gain, attn_w, width):
    tokens, model = middle.shape
    tile = tokens // 4

    def body(m_ref, cot_ref, gain_ref, w_ref, low_ref, *refs):
        mid_ref, branch_ref, gain_out_ref, attn_ref = refs[-4:]
        read = in_halves(low_ref, refs[:-4], tile)
        gain_sum = jnp.zeros((1, model), F32)
        for i in range(tokens // tile):
            rows = slice(i * tile, (i + 1) * tile)
            grad = read(i)
            middle = m_ref[rows]
            rsq = rsq_of(middle)
            unit = middle * rsq
            scaled = grad * gain_ref[...]
            back = cot_ref[rows].astype(F32) + rsq * (scaled - unit * jnp.mean(scaled * unit, axis=1, keepdims=True))
            mid_ref[rows] = back
            branch_ref[rows] = back.astype(BF)
            gain_sum += jnp.sum(grad * unit, axis=0, keepdims=True)
        gain_out_ref[...] = gain_sum
        attn_ref[...] = dot(branch_ref[...], w_ref[:, 3 * width :], NN)

    return near(
        body, [middle, cot, gain, attn_w, low, *others],
        [((tokens, model), F32), ((tokens, model), BF), ((1, model), F32), ((tokens, width), F32)],
    )


def gated(normed, gate_b, up_b):
    tokens, ff = normed.shape[0], gate_b.shape[1]
    tile = 256
    scale = math.sqrt(2.0 / math.pi)

    def body(x_ref, gate_ref, up_ref, hidden_ref, slopes_ref):
        def work(at):
            columns = pl.ds(at, tile)
            gate, up = dot(x_ref[...], gate_ref[:, columns], NN), dot(x_ref[...], up_ref[:, columns], NN)
            square = gate * gate
            tanh = jnp.tanh(scale * gate * (1.0 + 0.044715 * square))
            curve = 0.5 * (1.0 + tanh)
            slope = curve + 0.5 * gate * (1.0 - tanh * tanh) * (scale * (1.0 + 3 * 0.044715 * square))
            activated = gate * curve
            hidden_ref[:, columns] = (activated * up).astype(BF)
            slopes_ref[:, columns] = up * slope
            slopes_ref[:, pl.ds(pl.multiple_of(ff + at, tile), tile)] = activated

        tiles(ff, tile, work)

    return near(body, [normed, gate_b, up_b], [((tokens, ff), BF), ((tokens, 2 * ff), F32)])


def gated_back(cot, down_b, slopes):
    tokens, ff = cot.shape[0], down_b.shape[1]
    tile = 256

    def body(cot_ref, down_ref, slopes_ref, pair_ref):
        def work(at):
            grad = dot(cot_ref[...], down_ref[:, pl.ds(at, tile)], NN)
            for columns in (pl.ds(at, tile), pl.ds(pl.multiple_of(ff + at, tile), tile)):
                pair_ref[:, columns] = (grad * slopes_ref[:, columns]).astype(BF)

        tiles(ff, tile, work)

    return near(body, [cot, down_b, slopes], [((tokens, 2 * ff), BF)])[0]


def weight_grad(left, right, count, first=0, last=None):
    model = left.shape[1]
    last = last or right.shape[1]
    tile, chunk = 384, model // count

    def body(left_ref, right_ref, out_ref):
        def work(at):
            part = dot(left_ref[:, pl.ds(at, tile)], right_ref[:, first:last], TN).astype(BF)
            for c in range(tile // chunk):
                out_ref[at // chunk + c] = part[c * chunk : (c + 1) * chunk]

        tiles(model, tile, work)

    return near(body, [left, right], [((count, chunk, last - first), BF)])[0]


def back_through(left, rights):
    tokens, model = left.shape[0], rights[0].shape[0]
    half, tile = tokens // 2, 384

    def body(left_ref, *refs):
        keep_ref, give_ref = refs[-2:]

        def work(at):
            columns = pl.ds(at, tile)
            total, first = None, 0
            for ref in refs[:-2]:
                last = first + ref.shape[1]
                term = dot(left_ref[:, first:last], ref[columns, :], NT)
                total, first = term if total is None else total + term, last
            keep_ref[:, columns] = total[:half]
            give_ref[:, columns] = total[half:].astype(BF)

        tiles(model, tile, work)

    return near(body, [left, *rights], [((half, model), F32), ((half, model), BF)])


def attn_weight_grads(normed, inputs, rsq, branch, attn, grads, attn_w, second_part, table, chunk):
    tokens, model = normed.shape
    width = attn.shape[1]
    half, tile = tokens // 2, 384
    each = tile // chunk

    def body(n_ref, x_ref, rsq_ref, b_ref, attn_ref, q_ref, k_ref, v_ref, w_ref, second_ref, table_ref, out_ref, keep_ref, give_ref):
        three = jnp.concatenate([q_ref[...], k_ref[...], v_ref[...]], axis=1)
        attended = attn_ref[...].astype(BF)
        fill = jnp.zeros((1, 4 * width - chunk), F32)

        def work(at):
            columns = pl.ds(at, tile)
            back = dot(three, w_ref[columns, : 3 * width], NT)
            keep_ref[:, columns] = back[:half]
            give_ref[:, columns] = back[half:].astype(BF)
            first = jnp.sum(back * x_ref[:, columns].astype(F32) * rsq_ref[:, 0:1], axis=0, keepdims=True)
            second = second_ref[:, columns]
            wide = dot(n_ref[:, columns], three, TN).astype(BF)
            last = dot(b_ref[:, columns], attended, TN).astype(BF)
            for c in range(each):
                rows, block = slice(c * chunk, (c + 1) * chunk), at // chunk + c
                out_ref[block, :chunk] = jnp.concatenate([wide[rows], last[rows]], axis=1)
                small = [jnp.concatenate([row[:, rows], fill], axis=1) for row in (first, second)]
                small += [table_ref[...], jnp.zeros((EXTRA - 3, 4 * width), F32)]
                out_ref[block, chunk:] = jnp.concatenate(small, axis=0).astype(BF)

        tiles(model, tile, work)

    return near(
        body, [normed, inputs, rsq, branch, attn, *grads, attn_w, second_part, table],
        [((model // chunk, chunk + EXTRA, 4 * width), BF), ((half, model), F32), ((half, model), BF)],
    )


def finish_input(addends, inputs, gain, grad_middle):
    count, model = addends[0].shape

    def body(low_ref, got_ref, x_ref, gain_ref, mid_ref, out_ref):
        x = x_ref[:count].astype(F32)
        rsq = rsq_of(x)
        unit = x * rsq
        scaled = (low_ref[...].astype(F32) + got_ref[...].astype(F32)) * gain_ref[...]
        out_ref[...] = mid_ref[:count] + rsq * (scaled - unit * jnp.mean(scaled * unit, axis=1, keepdims=True))

    return near(body, [*addends, inputs, gain, grad_middle], [((count, model), F32)])[0]


def finish_output(addends, middle):
    count, model = addends[0].shape

    def body(low_ref, got_ref, mid_ref, out_ref):
        out_ref[...] = (mid_ref[:count] + low_ref[...].astype(F32) + got_ref[...].astype(F32)).astype(BF)

    return near(body, [*addends, middle], [((count, model), BF)])[0]


def rows_of(values, depth):
    if depth % 16:
        own, value = lax.axis_index("tp"), jnp.concatenate(values, axis=1)
        return [lax.dynamic_slice_in_dim(value, (own ^ k) * depth, depth, 0) for k in range(4)]

    def body(*refs):
        own = lax.axis_index("tp")
        for k in range(4):
            at = 0
            for ref in refs[: len(values)]:
                rows = ref[pl.ds(pl.multiple_of((own ^ k) * depth, depth), depth), :]
                refs[len(values) + k][:, at : at + ref.shape[1]] = rows
                at += ref.shape[1]

    return near(body, values, [((depth, sum(v.shape[1] for v in values)), BF)] * 4)


def unpack_mlp(pieces, count, ff):
    depth, width = pieces[0].shape

    def body(*refs):
        own, outs, held = lax.axis_index("tp"), refs[4:-1], refs[-1]
        for k in range(4):
            held[own ^ k] = refs[k][...]
        for i, out in enumerate(outs):
            for a in range(4):
                last = min(count, (a + 1) * ff)
                out[:, a * ff : last] = held[a, :, i * ff : i * ff + last - a * ff].astype(F32)

    return near(body, pieces, [((depth, count), F32)] * (width // ff), [pltpu.VMEM((4, depth, width), BF)])


def unpack_attn(pieces, depth, width, heads, buckets):
    rows = pieces[0].shape[0]

    def body(*refs):
        own, grads, first_ref, second_ref, table_ref, held = lax.axis_index("tp"), refs[4:8], *refs[8:]
        for k in range(4):
            held[own ^ k] = refs[k][...].astype(F32)
        for i, out in enumerate(grads):
            for a in range(4):
                out[:, a * width : (a + 1) * width] = held[a, :depth, i * width : (i + 1) * width]
        small = [held[a, depth : depth + EXTRA] for a in range(4)]
        first_ref[...] = sum(p[0:1, :depth] for p in small)
        second_ref[...] = small[0][1:2, :depth]
        for a in range(4):
            for h in range(heads):
                table_ref[a * heads + h : a * heads + h + 1] = small[a][2:3, h * buckets : (h + 1) * buckets]

    outs = [((depth, 4 * width), F32)] * 4 + [((1, depth), F32)] * 2 + [((4 * heads, buckets), F32)]
    return near(body, pieces, outs, [pltpu.VMEM((4, rows, 4 * width), F32)])


ORDER = (
    "Pa", "I0", "Pm", "a1", "a2", "C0", "M0", "g1", "a3", "u1", "g2", "I1s0", "d1", "a4", "d2", "a5", "C1s0",
    "I1s1", "I1e", "QK", "u2", "R0s0", "g3", "R0s1", "u3", "R0e", "d3", "g4", "u4", "R2s0", "d4", "R2s1", "R2e",
    "u5", "g5", "C1s1", "C1e", "d5", "ML", "rd1", "MB", "B0s0", "rd2", "O0s0", "rg1", "WU", "ru1", "B0e", "O0e",
    "rd3", "ru2", "rg2", "rd4", "B2s0", "rg3", "B2e", "AB", "ru3", "WA", "rd5", "N0s0", "ra1", "rg4", "O2", "ra2",
    "N0e", "rg5", "Xd0", "Xd1", "Xd2", "ra3", "Xd3", "ru4", "ra4", "ru5", "Xu0", "Xu1", "Xu2", "N2", "ra5", "Xa0",
    "Xa1", "Xa2", "Xu3", "Xa3",
)


def shards(
    block_input, cotangent, query_w, key_w, value_w, output_w, gate_w, up_w, down_w,
    first_gain, second_gain, bias_table, rel_bucket, doc_ids,
):
    rows, length, model = block_input.shape
    tokens = rows * length
    own = lax.axis_index("tp")
    parts = lax.axis_size("seq")
    count = lax.axis_size("rows") * parts
    bucket_count, head_count = bias_table.shape
    inner = query_w.shape[1]
    heads = head_count // 4
    dim = inner // head_count
    width = heads * dim
    depth = query_w.shape[0]
    chunk = 4 * depth
    hidden_count = gate_w.shape[1]
    ff = -(-hidden_count // (4 * 256)) * 256
    seq_len = doc_ids.shape[1]
    q_len = 4 * length
    shape = (heads, dim, rows, length)
    lanes = Lanes(count, 4)
    steps, tasks, have = {}, {}, {}

    def do(name):
        def keep(work):
            steps[name] = work
        return keep

    def task(key, names, make):
        def start():
            tasks[key] = Task(make())
            tasks[key].step()

        def end():
            have[key] = tasks[key].result()

        steps.update({name: lambda: tasks[key].step() for name in names})
        steps[names[0]], steps[names[-1]] = start, end

    def core(name, side=0):
        return [f"{name}s{n}" for n in range(CUTS[side])] + [f"{name}e"]

    def attn_blocks():
        weights = [query_w, key_w, value_w, output_w.T]
        gains = [first_gain.reshape(1, depth), second_gain.reshape(1, depth)]
        if depth % 16 == 0:
            return pack_attn(weights, gains, width)
        gains = jnp.pad(jnp.concatenate(gains, axis=0).astype(BF), ((0, EXTRA - 2), (0, 4 * width - depth)))
        return pack_plain(weights, width, gains)

    def mlp_blocks():
        weights = [down_w.T, gate_w, up_w]
        return pack_mlp(weights, ff) if depth % 16 == 0 else pack_plain(weights, ff, None)

    def attn_chunk():
        return gather_ring(lanes, stack_attn(tasks["Pa"].result(), chunk), chunk, 1)

    task("Pa", ["Pa", "Pa-"], lambda: exchange(lanes, attn_blocks()))
    task("Pm", ["Pm", "M0"], lambda: exchange(lanes, mlp_blocks()))
    task("a", ["a1", "a2", "a3", "a4", "a5"], attn_chunk)

    def mlp_chunk(i):
        if "chunks" not in have:
            have["chunks"] = stack_members(have["Pm"], [ff] * 3, PADS if ring_ok(count) else (0, 0, 0))
        return have["chunks"][i]

    task("d", ["d1", "d2", "d3", "d4", "d5"], lambda: gather_ring(lanes, mlp_chunk(0), chunk, -1))
    task("g", ["g1", "g2", "g3", "g4", "g5"], lambda: gather_ring(lanes, mlp_chunk(1), chunk, 1))
    task("u", ["u1", "u2", "u3", "u4", "u5"], lambda: gather_ring(lanes, mlp_chunk(2), chunk, -1))

    task("in", ["I0", *core("I1")], lambda: gather_tokens(lanes, block_input.reshape(tokens, model), CUTS[0]))
    task("cot", ["C0", *core("C1")], lambda: gather_tokens(lanes, cotangent.reshape(tokens, model), CUTS[0]))

    @do("QK")
    def _():
        one_hot = (rel_bucket[:, None] == jnp.arange(bucket_count, dtype=jnp.int32)).astype(F32)
        first = lax.axis_index("seq") * q_len
        one_hot = lax.dynamic_slice_in_dim(one_hot, seq_len - first - q_len, seq_len + q_len, 0)
        own_table = lax.dynamic_slice_in_dim(bias_table, own * heads, heads, 1)
        by_distance = lax.dot_general(own_table, one_hot, (((0,), (1,)), ((), ())), precision=HIGHEST)
        query_doc = lax.dynamic_slice_in_dim(doc_ids, first, q_len, 1)[:, :, None]
        attn_w, chunks = have["a"]
        gain_one, gain_two = spread_gains(chunks, chunk)
        normed, rsq_one, queries, keys, values = project(have["in"], gain_one, attn_w, width)
        queries = lanes.pin(queries)
        if parts > 1:
            keys = lax.all_gather(keys, "seq", axis=0)
            values = lax.all_gather(values, "seq", axis=0)
        else:
            keys, values = keys[None], values[None]
        have.update(
            one_hot=one_hot, attn_w=attn_w, gain_one=gain_one, gain_two=gain_two, normed=normed, rsq_one=rsq_one,
            scores=(queries, keys, values, by_distance, query_doc, doc_ids[:, None, :]),
        )

    def attention():
        have["attn"], keep, give = attn_forward(*have["scores"], have["attn_w"], *shape)
        return sum_tokens(lanes, keep, give, CUTS[0])

    task("branch", [*core("R0"), *core("R2")], attention)

    @do("ML")
    def _():
        middle, normed_mlp = norm_again(have["in"], *have["branch"], have["gain_two"])
        hidden, slopes = gated(normed_mlp, have["g"][0], have["u"][0])
        have.update(middle=middle, normed_mlp=normed_mlp, hidden=lanes.pin(hidden), slopes=slopes)

    @do("MB")
    def _():
        have["grad_pair"] = lanes.pin(gated_back(have["cot"], have["d"][0], have["slopes"]))

    task(
        "rd", ["rd1", "rd2", "rd3", "rd4", "rd5"],
        lambda: scatter_ring(lanes, weight_grad(have["cot"], have["hidden"], count), 1, chunk + RPADS[0]),
    )
    task(
        "back", [*core("B0", 1), *core("B2", 1)],
        lambda: sum_tokens(lanes, *back_through(have["grad_pair"], [have["g"][0], have["u"][0]]), CUTS[1]),
    )
    if "rm1" in ORDER:
        task(
            "rm", ["rm1", "rm2", "rm3", "rm4", "rm5"],
            lambda: scatter_ring(lanes, weight_grad(have["normed_mlp"], have["grad_pair"], count), -1, chunk + RPADS[1]),
        )
    else:
        @do("WU")
        def _():
            have["up_blocks"] = lanes.pin(weight_grad(have["normed_mlp"], have["grad_pair"], count, ff, 2 * ff))

        task(
            "rg", ["rg1", "rg2", "rg3", "rg4", "rg5"],
            lambda: scatter_ring(
                lanes, weight_grad(have["normed_mlp"], have["grad_pair"], count, 0, ff), -1, chunk + RPADS[1]
            ),
        )
        task("ru", ["ru1", "ru2", "ru3", "ru4", "ru5"], lambda: scatter_ring(lanes, have["up_blocks"], 1, chunk + RPADS[2]))
    task("out", [*core("O0", 1), "O2"], lambda: scatter_tokens(lanes, *back_through(have["hidden"], [have["d"][0]]), CUTS[1]))

    @do("AB")
    def _():
        grad_middle, grad_branch, second_part, grad_attn = norm_back(
            have["middle"], have["cot"], *have["back"], have["gain_two"], have["attn_w"], width
        )
        grad_q, grad_k, grad_v, table = attn_backward(
            *have["scores"], have["attn"], lanes.pin(grad_attn), have["one_hot"], *shape, 4 * width
        )
        if parts > 1:
            grad_k = lax.psum_scatter(grad_k, "seq", scatter_dimension=0, tiled=True)
            grad_v = lax.psum_scatter(grad_v, "seq", scatter_dimension=0, tiled=True)
        have.update(
            grad_middle=grad_middle, grad_branch=grad_branch, second_part=second_part, table=table,
            grads=(lanes.pin(grad_q), grad_k[0], grad_v[0]),
        )

    @do("WA")
    def _():
        four_grad, keep, give = attn_weight_grads(
            have["normed"], have["in"], have["rsq_one"], have["grad_branch"], have["attn"], have["grads"],
            have["attn_w"], have["second_part"], have["table"], chunk,
        )
        have.update(four_grad=lanes.pin(four_grad), in_parts=(keep, give))

    task("ra", ["ra1", "ra2", "ra3", "ra4", "ra5"], lambda: scatter_ring(lanes, have["four_grad"], 1, chunk + EXTRA))
    task("grad_in", [*core("N0", 1), "N2"], lambda: scatter_tokens(lanes, *have["in_parts"], CUTS[1]))

    if "rm1" in ORDER:
        one, two = ["rd"], ["rm"]
    else:
        one, two = ["rd", "rg"], ["ru"]
    task("Xd", ["Xd0", "Xd1", "Xd2", "Xd3"], lambda: exchange(lanes, rows_of([have[k] for k in one], depth), False))
    task("Xu", ["Xu0", "Xu1", "Xu2", "Xu3"], lambda: exchange(lanes, rows_of([have[k] for k in two], depth), False))
    task("Xa", ["Xa0", "Xa1", "Xa2", "Xa3"], lambda: exchange(lanes, split_attn(have["ra"], depth, width), False))

    for name in ORDER:
        steps[name]()
    block_output = finish_output(have["out"], have["middle"])
    input_grad = finish_input(have["grad_in"], have["in"], have["gain_one"], have["grad_middle"])

    mlp = unpack_mlp(have["Xd"], hidden_count, ff) + unpack_mlp(have["Xu"], hidden_count, ff)
    *grads, first_grad, second_grad, table_grad = unpack_attn(have["Xa"], depth, width, heads, bucket_count)
    return (
        block_output.reshape(rows, length, model), input_grad.reshape(rows, length, model),
        grads[0], grads[1], grads[2], grads[3].T,
        mlp[1], mlp[2], mlp[0].T, first_grad.reshape(depth), second_grad.reshape(depth), table_grad.T,
    )


def solution(mesh):
    row_count, blk_count = mesh.shape["rows"], mesh.shape["blk"]
    fine = Mesh(mesh.devices.reshape(row_count, blk_count // 4, 4), ("rows", "seq", "tp"))
    every = ("rows", "seq", "tp")
    tokens = P("rows", ("seq", "tp"), None)
    deep, wide, flat = P(every, None), P(None, every), P(every)
    return jax.shard_map(
        shards,
        mesh=fine,
        in_specs=(tokens, tokens, deep, deep, deep, wide, deep, deep, wide, flat, flat, P(), P(), P("rows", None)),
        out_specs=(tokens, tokens, deep, deep, deep, wide, deep, deep, wide, flat, flat, P()),
        check_vma=False,
    )
```

```python
import math

import jax
import jax.numpy as jnp
from jax import lax
from jax.experimental import pallas as pl
from jax.experimental.pallas import tpu as pltpu
from jax.sharding import Mesh, PartitionSpec as P

EPSILON = 1e-06
BF = jnp.bfloat16
F32 = jnp.float32
HIGHEST = lax.Precision.HIGHEST
RING = ("rows", "seq")
MAX_RING = 8
EXTRA = 8
PADS = (8, 6, 4)
RPADS = (8, 4, 8)
CUTS = (2, 1)
FREE = pl.CostEstimate(flops=0, transcendentals=0, bytes_accessed=0)


def dot(left, right, dims, out=F32):
    return lax.dot_general(left, right, (dims, ((), ())), preferred_element_type=out)


NN = ((1,), (0,))
NT = ((1,), (1,))
TN = ((0,), (0,))


def ring_order(count):
    return list(range(0, count, 2)) + list(range(count - 1, 0, -2))


def ring_places(count):
    half = count // 2
    group = lax.axis_index(RING)
    place = jnp.where(group % 2 == 0, group // 2, count - 1 - group // 2)
    places = []
    for k in range(count):
        at = place - k
        at = jnp.where(at < 0, at + count, at)
        places.append(jnp.where(at < half, 2 * at, 2 * (count - 1 - at) + 1))
    return places


def ring_ok(count):
    return count <= MAX_RING and count % 2 == 0


class Lanes:
    def __init__(self, count, ways):
        order = ring_order(count)
        self.pairs = {
            step: [(order[i], order[(i + step) % count]) for i in range(count)] for step in (1, -1)
        }
        self.count, self.ways, self.last = count, ways, None

    def pin(self, *values):
        if self.last is not None:
            values = lax.optimization_barrier((*values, self.last))[:-1]
        self.last = values[0]
        return values if len(values) > 1 else values[0]

    def shift(self, value, step):
        return lax.ppermute(value, RING, self.pairs[step])

    def partner(self, value, bit):
        return lax.ppermute(value, "tp", [(i, i ^ bit) for i in range(self.ways)])


class Task:
    def __init__(self, steps):
        self.steps, self.value = steps, None

    def step(self):
        if self.steps is not None:
            try:
                next(self.steps)
            except StopIteration as stop:
                self.value, self.steps = stop.value, None

    def result(self):
        while self.steps is not None:
            self.step()
        return self.value


def gather_ring(lanes, chunk, keep, lead):
    count = lanes.count
    if not ring_ok(count):
        got = lax.all_gather(chunk, RING, axis=0) if count > 1 else chunk[None]
        return got[:, :keep].reshape(-1, chunk.shape[1]), [got[i] for i in range(count)]
    chunk = lanes.pin(chunk)
    moving = {lead: chunk, -lead: chunk}
    got = [chunk]
    for k in range(1, count // 2):
        moving = {step: lanes.shift(value, step) for step, value in moving.items()}
        yield
        moving = dict(zip(moving, lanes.pin(*moving.values())))
        got += [moving[1], moving[-1]]
    last = lanes.shift(moving[lead], lead)
    yield
    got.append(lanes.pin(last))
    return place_rows(got, count, keep), got


def chunk_order(count):
    order = [0]
    for k in range(1, count // 2):
        order += [k, count - k]
    return order + [count // 2]


def place_rows(got, count, keep):
    def body(*refs):
        places = ring_places(count)
        for ref, k in zip(refs, chunk_order(count)):
            refs[-1][pl.ds(pl.multiple_of(places[k] * keep, keep), keep), :] = ref[:keep]

    return near(body, got, [((count * keep, got[0].shape[1]), BF)])[0]


def scatter_ring(lanes, blocks, lead, rows):
    count, size, _ = blocks.shape
    if count == 1:
        return blocks[0]
    if not ring_ok(count):
        return lax.psum_scatter(blocks, RING, scatter_dimension=0, tiled=True)[0]
    (far,) = add_blocks(blocks, [(count // 2, None)], rows)
    moving = {lead: lanes.shift(lanes.pin(far), lead)}
    yield
    for j in range(count // 2 - 1, 0, -1):
        arrived = dict(zip(moving, lanes.pin(*moving.values()) if len(moving) > 1 else (lanes.pin(moving[lead]),)))
        sums = add_blocks(blocks, [(-j * step, arrived.get(step)) for step in (1, -1)], rows)
        moving = {step: lanes.shift(value, step) for step, value in zip((1, -1), lanes.pin(*sums))}
        yield
    came, back = lanes.pin(*moving.values())
    return add_blocks(blocks, [(0, came)], size, back)[0]


def add_blocks(blocks, terms, rows, more=None):
    count, size, width = blocks.shape
    came = [c for _, c in terms if c is not None] + ([] if more is None else [more])

    def body(blocks_ref, *refs):
        places = ring_places(count)
        given, outs = list(refs[: len(came)]), refs[len(came) :]
        for (k, c), out in zip(terms, outs):
            total = blocks_ref[places[k % count]].astype(F32)
            if c is not None:
                total = total + given.pop(0)[:size].astype(F32)
            if more is not None:
                total = total + given.pop(0)[:size].astype(F32)
            out[:size] = total.astype(BF)
            if rows > size:
                out[size:] = jnp.zeros((rows - size, width), BF)

    return near(body, [blocks, *came], [((rows, width), BF)] * len(terms))


def block_of(index):
    return index % 2 * 2 + index // 2


def gather_tokens(lanes, value, cuts):
    value = lanes.pin(value)
    got = lanes.partner(value, 2)
    yield
    value = jnp.concatenate([value, lanes.pin(got)], axis=0)
    got = yield from over_core(lanes, value, cuts)
    return jnp.concatenate([value, *got], axis=0)


def over_core(lanes, give, cuts):
    rows, pieces, first = give.shape[0], [], 0
    for n in range(cuts):
        last = rows * (n + 1) // cuts // 16 * 16 if n + 1 < cuts else rows
        got = lanes.partner(lanes.pin(give[first:last]), 1)
        yield
        pieces.append(lanes.pin(got))
        first = last
    return pieces


def sum_tokens(lanes, keep, give, cuts):
    got = yield from over_core(lanes, give, cuts)
    low = lanes.pin(add_halves(keep, got, False))
    got = lanes.partner(low, 2)
    yield
    low = lanes.pin(add_halves(low, [lanes.pin(got)], True))
    got = yield from over_core(lanes, low, cuts)
    return low, got


def add_halves(left, pieces, swapped):
    rows = left.shape[0]
    half = rows // 2

    def body(left_ref, *refs):
        first = 0
        for ref in refs[:-1]:
            for at in range(0, ref.shape[0], half if swapped else ref.shape[0]):
                count = half if swapped else ref.shape[0]
                to = half - at if swapped else first + at
                total = left_ref[to : to + count].astype(F32) + ref[at : at + count].astype(F32)
                refs[-1][to : to + count] = total.astype(BF)
            first += ref.shape[0]

    return near(body, [left, *pieces], [(left.shape, BF)])[0]


def scatter_tokens(lanes, keep, give, cuts):
    got = yield from over_core(lanes, give, cuts)
    low = lanes.pin(add_halves(keep, got, False))
    mine = low.shape[0] // 2
    got = lanes.partner(low[mine:], 2)
    yield
    return low[:mine], lanes.pin(got)


def exchange(lanes, blocks, at_once=True):
    pieces = [blocks[0]] + [None] * 3
    for k in (2, 3, 1):
        pieces[k] = lanes.partner(lanes.pin(blocks[k]), k)
        if not at_once:
            yield
    if at_once:
        yield
    pieces[1:] = lanes.pin(*pieces[1:])
    return pieces


def by_member(pieces):
    own, chosen = lax.axis_index("tp"), []
    for a in range(4):
        piece = pieces[a]
        for mine in range(1, 4):
            piece = jnp.where(own == mine, pieces[a ^ mine], piece)
        chosen.append(piece)
    return chosen


def stack_members(pieces, widths, pads):
    depth = pieces[0].shape[0]
    if depth % 16:
        pieces = jnp.concatenate(by_member(pieces), axis=0)
        starts = [sum(widths[:i]) for i in range(len(widths))]
        return [jnp.pad(pieces[:, a : a + w], ((0, p), (0, 0))) for a, w, p in zip(starts, widths, pads)]

    def body(*refs):
        own = lax.axis_index("tp")
        at = 0
        for width, pad, out in zip(widths, pads, refs[4:]):
            for k in range(4):
                out[pl.ds(pl.multiple_of((own ^ k) * depth, depth), depth), :] = refs[k][:, at : at + width]
            if pad:
                out[4 * depth :] = jnp.zeros((pad, width), BF)
            at += width

    return near(body, pieces, [((4 * depth + pad, width), BF) for width, pad in zip(widths, pads)])


def stack_attn(pieces, chunk):
    depth, width = chunk // 4, pieces[0].shape[1]
    if depth % 16:
        pieces = by_member(pieces)
        gains = jnp.concatenate([p[depth : depth + 2, :depth] for p in pieces], axis=1)
        gains = jnp.pad(gains, ((0, EXTRA - 2), (0, width - chunk)))
        return jnp.concatenate([p[:depth] for p in pieces] + [gains], axis=0)

    def body(*refs):
        own, out, gains_ref = lax.axis_index("tp"), refs[4], refs[5]
        for k in range(4):
            out[pl.ds(pl.multiple_of((own ^ k) * depth, depth), depth), :] = refs[k][:depth]
            gains_ref[own ^ k] = refs[k][depth:, :depth].astype(F32)
        gains = [gains_ref[a] for a in range(4)] + [jnp.zeros((EXTRA, width - chunk), F32)]
        out[chunk:] = jnp.concatenate(gains, axis=1).astype(BF)

    return near(body, pieces, [((chunk + EXTRA, width), BF)], [pltpu.VMEM((4, EXTRA, depth), F32)])[0]


def split_attn(total, depth, width):
    chunk = 4 * depth
    if depth % 16:
        tables = jnp.pad(total[chunk + 2 : chunk + 3], ((2, EXTRA - 3), (0, 0)))
        blocks = []
        for large, pair in zip(rows_of([total], depth), rows_of([total[chunk : chunk + 2, :chunk].T], depth)):
            pair = jnp.pad(pair.T, ((0, EXTRA - 2), (0, 4 * width - depth)))
            blocks.append(jnp.concatenate([large, pair + tables], axis=0))
        return blocks

    def body(total_ref, *refs):
        own, small_ref = lax.axis_index("tp"), refs[4]
        fill = jnp.zeros((2, 4 * width - depth), F32)
        small = total_ref[chunk : chunk + EXTRA].astype(F32)
        below = jnp.concatenate([small[2:3], jnp.zeros((EXTRA - 3, 4 * width), F32)], axis=0)
        for a in range(4):
            pair = jnp.concatenate([small[0:2, a * depth : (a + 1) * depth], fill], axis=1)
            small_ref[a] = jnp.concatenate([pair, below], axis=0)
        for k in range(4):
            refs[k][:depth] = total_ref[pl.ds(pl.multiple_of((own ^ k) * depth, depth), depth), :]
            refs[k][depth:] = small_ref[own ^ k].astype(BF)

    return near(
        body, [total], [((depth + EXTRA, 4 * width), BF)] * 4, [pltpu.VMEM((4, EXTRA, 4 * width), F32)]
    )


def run(body, grid, ins, outs, scratch=(), vmem=24):
    def spec(block, index_map):
        return pl.BlockSpec(block, index_map)

    arrays, in_specs = [], []
    for item in ins:
        array, block, index_map = item if isinstance(item, tuple) else (item, item.shape, None)
        if index_map is None:
            index_map = lambda *_, n=array.ndim: (0,) * n
        arrays.append(array)
        in_specs.append(spec(block, index_map))
    out_specs = [
        spec(block or shape, index_map or (lambda *_, n=len(shape): (0,) * n)) for shape, _, block, index_map in outs
    ]
    return pl.pallas_call(
        body, grid=grid, in_specs=in_specs, out_specs=out_specs,
        out_shape=[jax.ShapeDtypeStruct(shape, dtype) for shape, dtype, _, _ in outs],
        scratch_shapes=list(scratch),
        compiler_params=pltpu.CompilerParams(
            dimension_semantics=("arbitrary",) * len(grid), vmem_limit_bytes=vmem << 20
        ),
        cost_estimate=FREE,
    )(*arrays)


def near(body, arrays, outs, scratch=(), vmem=16):
    spec = pl.BlockSpec(memory_space=pltpu.VMEM)
    return pl.pallas_call(
        body, in_specs=[spec] * len(arrays), out_specs=[spec] * len(outs),
        out_shape=[jax.ShapeDtypeStruct(shape, dtype) for shape, dtype in outs],
        scratch_shapes=list(scratch),
        compiler_params=pltpu.CompilerParams(vmem_limit_bytes=vmem << 20),
        cost_estimate=FREE,
    )(*arrays)


def far(arrays):
    return [pltpu.with_memory_space_constraint(a, pltpu.HBM) for a in arrays]


def whole(shape, dtype):
    return (shape, dtype, None, None)


def pack_attn(weights, gains, width):
    depth, inner = weights[0].shape

    def body(q_ref, k_ref, v_ref, o_ref, first_ref, second_ref, *rest):
        outs, out_ref = rest[:4], rest[4]
        own = lax.axis_index("tp")
        extra = jnp.concatenate([first_ref[...], second_ref[...], jnp.zeros((EXTRA - 2, depth), F32)], axis=0)
        extra = jnp.concatenate([extra, jnp.zeros((EXTRA, 4 * width - depth), F32)], axis=1).astype(BF)
        for a in range(4):
            parts = [r[:, a * width : (a + 1) * width] for r in (q_ref, k_ref, v_ref, o_ref)]
            out_ref[a ^ own, :depth] = jnp.concatenate(parts, axis=1).astype(BF)
            out_ref[a ^ own, depth:] = extra
        for k in range(4):
            outs[k][...] = out_ref[k]

    shape = (depth + EXTRA, 4 * width)
    return run(body, (1,), far([*weights, *gains]), [whole(shape, BF)] * 4, [pltpu.VMEM((4, *shape), BF)])


def pack_mlp(weights, ff):
    depth, count = weights[0].shape

    def body(*refs):
        own, out_ref = lax.axis_index("tp"), refs[-1]
        for a in range(4):
            parts = []
            for ref in refs[: len(weights)]:
                last = min(count, (a + 1) * ff)
                parts.append(ref[:, a * ff : last])
                if last < (a + 1) * ff:
                    parts.append(jnp.zeros((depth, (a + 1) * ff - last), F32))
            out_ref[a ^ own] = jnp.concatenate(parts, axis=1).astype(BF)
        for k in range(4):
            refs[len(weights) + k][...] = out_ref[k]

    shape = (depth, len(weights) * ff)
    return run(body, (1,), far(weights), [whole(shape, BF)] * 4, [pltpu.VMEM((4, *shape), BF)])


def pack_plain(weights, width, extra):
    own = lax.axis_index("tp")
    weights = [jnp.pad(w.astype(BF), ((0, 0), (0, 4 * width - w.shape[1]))) for w in weights]
    blocks = []
    for k in range(4):
        block = jnp.concatenate([lax.dynamic_slice_in_dim(w, (own ^ k) * width, width, 1) for w in weights], axis=1)
        blocks.append(block if extra is None else jnp.concatenate([block, extra], axis=0))
    return blocks


def spread_gains(chunks, chunk):
    count = len(chunks)
    ring = ring_ok(count)

    def body(*refs):
        one_ref, two_ref, rows_ref = refs[-3:]
        places = ring_places(count) if ring else None
        for ref, k in zip(refs, chunk_order(count) if ring else range(count)):
            rows_ref[places[k] if ring else k] = ref[chunk : chunk + 2, :chunk].astype(F32)
        both = jnp.concatenate([rows_ref[r] for r in range(count)], axis=1)
        one_ref[...], two_ref[...] = both[0:1], both[1:2]

    return near(body, chunks, [((1, count * chunk), F32)] * 2, [pltpu.VMEM((count, 2, chunk), F32)])


def tiles(total, tile, work):
    lax.fori_loop(0, total // tile, lambda i, _: work(pl.multiple_of(i * tile, tile)), None, unroll=2)


def rsq_of(value):
    return lax.rsqrt(jnp.mean(value * value, axis=1, keepdims=True) + EPSILON)


def project(inputs, gain, weights, width):
    tokens, model = inputs.shape
    tile = tokens // 2

    def body(x_ref, gain_ref, w_ref, normed_ref, rsq_ref, q_ref, k_ref, v_ref):
        for at in range(0, tokens, tile):
            rows = slice(at, at + tile)
            x = x_ref[rows].astype(F32)
            rsq = rsq_of(x)
            normed = (x * rsq * gain_ref[...]).astype(BF)
            normed_ref[rows] = normed
            rsq_ref[rows] = jnp.broadcast_to(rsq, (tile, 128))
            three = dot(normed, w_ref[:, : 3 * width], NN).astype(BF)
            for i, ref in enumerate((q_ref, k_ref, v_ref)):
                ref[rows] = three[:, i * width : (i + 1) * width]

    return near(
        body, [inputs, gain, weights],
        [((tokens, model), BF), ((tokens, 128), F32)] + [((tokens, width), BF)] * 3,
    )


def head_scores(own, row, head, dim, rows, length, q_ref, k_ref, w_ref, qd_ref, kd_ref):
    lanes = slice(head * dim, (head + 1) * dim)
    starts = [pl.multiple_of((block_of(own ^ a) * rows + row) * length, length) for a in range(4)]
    queries = jnp.concatenate([q_ref[pl.ds(s, length), lanes] for s in starts], axis=0)
    keys = take_keys(k_ref, starts, length, lanes)
    q_len, k_len = queries.shape[0], keys.shape[0]
    scores = dot(queries, keys, NT)
    bias = jnp.broadcast_to(w_ref[pl.ds(head, 1), :], (q_len, q_len + k_len))
    bias = pltpu.roll(bias, k_len, 1, stride=1, stride_axis=0)[:, :k_len]
    same = qd_ref[row] == kd_ref[row]
    expo = jnp.where(same, jnp.exp(scores + bias), 0.0)
    return queries, keys, expo, starts, lanes


def take_keys(ref, starts, length, lanes):
    return jnp.concatenate(
        [ref[g, pl.ds(s, length), lanes] for g in range(ref.shape[0]) for s in starts], axis=0
    )


def attn_forward(q, k, v, by_distance, query_doc, key_doc, attn_w, heads, dim, rows, length):
    tokens, width = q.shape
    model = attn_w.shape[0]
    half = tokens // 2

    def body(q_ref, k_ref, v_ref, w_ref, qd_ref, kd_ref, o_ref, attn_ref, keep_ref, give_ref, part_ref):
        def one_row(row):
            forward_row(row, q_ref, k_ref, v_ref, w_ref, qd_ref, kd_ref, o_ref, attn_ref, part_ref)

        lax.fori_loop(0, rows, lambda row, _: one_row(row), None)
        keep_ref[...] = part_ref[:half]
        give_ref[...] = part_ref[half:].astype(BF)

    def forward_row(row, q_ref, k_ref, v_ref, w_ref, qd_ref, kd_ref, o_ref, attn_ref, part_ref):
        own, out = lax.axis_index("tp"), []
        for head in range(heads):
            _, _, expo, starts, lanes = head_scores(
                own, row, head, dim, rows, length, q_ref, k_ref, w_ref, qd_ref, kd_ref
            )
            values = take_keys(v_ref, starts, length, lanes)
            low = expo.astype(BF)
            totals = jnp.sum(low.astype(F32), axis=1, keepdims=True)
            out.append(dot(low, values, NN) / totals)
        out = jnp.concatenate(out, axis=1)
        part = dot(out.astype(BF), o_ref[:, 3 * width :], NT)
        for a, s in enumerate(starts):
            attn_ref[pl.ds(s, length), :] = out[a * length : (a + 1) * length]
            part_ref[pl.ds(s, length), :] = part[a * length : (a + 1) * length]

    return near(
        body, [q, k, v, by_distance, query_doc, key_doc, attn_w],
        [((tokens, width), F32), ((half, model), F32), ((half, model), BF)],
        [pltpu.VMEM((tokens, model), F32)],
    )


def attn_backward(q, k, v, by_distance, query_doc, key_doc, attn, grad, one_hot, heads, dim, rows, length, columns):
    buckets = one_hot.shape[1]

    def body(
        q_ref, k_ref, v_ref, w_ref, qd_ref, kd_ref, attn_ref, grad_ref, hot_ref,
        gq_ref, gk_ref, gv_ref, table_ref, diag_ref,
    ):
        diag_ref[...] = jnp.zeros(diag_ref.shape, F32)

        def one_row(row):
            backward_row(
                row, q_ref, k_ref, v_ref, w_ref, qd_ref, kd_ref, attn_ref, grad_ref, gq_ref, gk_ref, gv_ref, diag_ref
            )

        lax.fori_loop(0, rows, lambda row, _: one_row(row), None)
        table = lax.dot_general(
            diag_ref[...], hot_ref[...], (NN, ((), ())), precision=HIGHEST, preferred_element_type=F32
        )
        table = [table[h : h + 1] for h in range(heads)]
        table_ref[...] = jnp.concatenate(table + [jnp.zeros((1, columns - heads * buckets), F32)], axis=1)

    def backward_row(
        row, q_ref, k_ref, v_ref, w_ref, qd_ref, kd_ref, attn_ref, grad_ref, gq_ref, gk_ref, gv_ref, diag_ref
    ):
        own = lax.axis_index("tp")
        grads_q, grads_k, grads_v, diags = [], [], [], []
        for head in range(heads):
            queries, keys, expo, starts, lanes = head_scores(
                own, row, head, dim, rows, length, q_ref, k_ref, w_ref, qd_ref, kd_ref
            )
            values = take_keys(v_ref, starts, length, lanes)
            grads = jnp.concatenate([grad_ref[pl.ds(s, length), lanes] for s in starts], axis=0)
            outs = jnp.concatenate([attn_ref[pl.ds(s, length), lanes] for s in starts], axis=0)
            low = expo.astype(BF)
            totals = jnp.sum(low.astype(F32), axis=1, keepdims=True)
            grad_low = (grads / totals).astype(BF)
            grad_total = -jnp.sum(grads * outs, axis=1, keepdims=True) / totals
            grad_score = (expo * (dot(grad_low, values, NT) + grad_total)).astype(BF)
            grads_q.append(dot(grad_score, keys, NN))
            grads_k.append(dot(grad_score, queries, TN))
            grads_v.append(dot(low, grad_low, TN))
            q_len, k_len = grad_score.shape
            row_at = lax.broadcasted_iota(jnp.int32, (q_len, q_len), 0)
            column_at = lax.broadcasted_iota(jnp.int32, (q_len, q_len), 1)
            flip = jnp.where(row_at + column_at == q_len - 1, 1.0, 0.0).astype(BF)
            turned = dot(flip, grad_score, NN)
            turned = jnp.concatenate([turned, jnp.zeros((q_len, q_len), F32)], axis=1)
            turned = pltpu.roll(turned, 1, 1, stride=1, stride_axis=0)
            diags.append(jnp.sum(turned, axis=0, keepdims=True))
        joined = jnp.concatenate(grads_q, axis=1).astype(BF)
        for a, s in enumerate(starts):
            gq_ref[pl.ds(s, length), :] = joined[a * length : (a + 1) * length]
        for parts, ref in ((grads_k, gk_ref), (grads_v, gv_ref)):
            joined = jnp.concatenate(parts, axis=1).astype(BF)
            for g in range(ref.shape[0]):
                for a, s in enumerate(starts):
                    at = (g * 4 + a) * length
                    ref[g, pl.ds(s, length), :] = joined[at : at + length]
        diag_ref[...] += jnp.concatenate(diags, axis=0)

    return near(
        body, [q, k, v, by_distance, query_doc, key_doc, attn, grad, one_hot],
        [(q.shape, BF), (k.shape, BF), (v.shape, BF), ((1, columns), F32)],
        [pltpu.VMEM(by_distance.shape, F32)],
    )


def in_halves(low, others, tile):
    places = []
    for ref in (low, *others):
        places += [(ref, at) for at in range(0, ref.shape[0], tile)]
    return lambda i: places[i][0][places[i][1] : places[i][1] + tile].astype(F32)


def norm_again(inputs, low, others, gain):
    tokens, model = inputs.shape
    tile = tokens // 4

    def body(x_ref, gain_ref, low_ref, *refs):
        middle_ref, normed_ref = refs[-2:]
        read = in_halves(low_ref, refs[:-2], tile)
        for i in range(tokens // tile):
            rows = slice(i * tile, (i + 1) * tile)
            middle = x_ref[rows].astype(F32) + read(i)
            middle_ref[rows] = middle
            normed_ref[rows] = (middle * rsq_of(middle) * gain_ref[...]).astype(BF)

    return near(body, [inputs, gain, low, *others], [((tokens, model), F32), ((tokens, model), BF)])


def norm_back(middle, cot, low, others, gain, attn_w, width):
    tokens, model = middle.shape
    tile = tokens // 4

    def body(m_ref, cot_ref, gain_ref, w_ref, low_ref, *refs):
        mid_ref, branch_ref, gain_out_ref, attn_ref = refs[-4:]
        read = in_halves(low_ref, refs[:-4], tile)
        gain_sum = jnp.zeros((1, model), F32)
        for i in range(tokens // tile):
            rows = slice(i * tile, (i + 1) * tile)
            grad = read(i)
            middle = m_ref[rows]
            rsq = rsq_of(middle)
            unit = middle * rsq
            scaled = grad * gain_ref[...]
            back = cot_ref[rows].astype(F32) + rsq * (scaled - unit * jnp.mean(scaled * unit, axis=1, keepdims=True))
            mid_ref[rows] = back
            branch_ref[rows] = back.astype(BF)
            gain_sum += jnp.sum(grad * unit, axis=0, keepdims=True)
        gain_out_ref[...] = gain_sum
        attn_ref[...] = dot(branch_ref[...], w_ref[:, 3 * width :], NN)

    return near(
        body, [middle, cot, gain, attn_w, low, *others],
        [((tokens, model), F32), ((tokens, model), BF), ((1, model), F32), ((tokens, width), F32)],
    )


def gated(normed, gate_b, up_b):
    tokens, ff = normed.shape[0], gate_b.shape[1]
    tile = 256
    scale = math.sqrt(2.0 / math.pi)

    def body(x_ref, gate_ref, up_ref, hidden_ref, slopes_ref):
        def work(at):
            columns = pl.ds(at, tile)
            gate, up = dot(x_ref[...], gate_ref[:, columns], NN), dot(x_ref[...], up_ref[:, columns], NN)
            square = gate * gate
            tanh = jnp.tanh(scale * gate * (1.0 + 0.044715 * square))
            curve = 0.5 * (1.0 + tanh)
            slope = curve + 0.5 * gate * (1.0 - tanh * tanh) * (scale * (1.0 + 3 * 0.044715 * square))
            activated = gate * curve
            hidden_ref[:, columns] = (activated * up).astype(BF)
            slopes_ref[:, columns] = up * slope
            slopes_ref[:, pl.ds(pl.multiple_of(ff + at, tile), tile)] = activated

        tiles(ff, tile, work)

    return near(body, [normed, gate_b, up_b], [((tokens, ff), BF), ((tokens, 2 * ff), F32)])


def gated_back(cot, down_b, slopes):
    tokens, ff = cot.shape[0], down_b.shape[1]
    tile = 256

    def body(cot_ref, down_ref, slopes_ref, pair_ref):
        def work(at):
            grad = dot(cot_ref[...], down_ref[:, pl.ds(at, tile)], NN)
            for columns in (pl.ds(at, tile), pl.ds(pl.multiple_of(ff + at, tile), tile)):
                pair_ref[:, columns] = (grad * slopes_ref[:, columns]).astype(BF)

        tiles(ff, tile, work)

    return near(body, [cot, down_b, slopes], [((tokens, 2 * ff), BF)])[0]


def weight_grad(left, right, count, first=0, last=None):
    model = left.shape[1]
    last = last or right.shape[1]
    tile, chunk = 384, model // count

    def body(left_ref, right_ref, out_ref):
        def work(at):
            part = dot(left_ref[:, pl.ds(at, tile)], right_ref[:, first:last], TN).astype(BF)
            for c in range(tile // chunk):
                out_ref[at // chunk + c] = part[c * chunk : (c + 1) * chunk]

        tiles(model, tile, work)

    return near(body, [left, right], [((count, chunk, last - first), BF)])[0]


def back_through(left, rights):
    tokens, model = left.shape[0], rights[0].shape[0]
    half, tile = tokens // 2, 384

    def body(left_ref, *refs):
        keep_ref, give_ref = refs[-2:]

        def work(at):
            columns = pl.ds(at, tile)
            total, first = None, 0
            for ref in refs[:-2]:
                last = first + ref.shape[1]
                term = dot(left_ref[:, first:last], ref[columns, :], NT)
                total, first = term if total is None else total + term, last
            keep_ref[:, columns] = total[:half]
            give_ref[:, columns] = total[half:].astype(BF)

        tiles(model, tile, work)

    return near(body, [left, *rights], [((half, model), F32), ((half, model), BF)])


def attn_weight_grads(normed, inputs, rsq, branch, attn, grads, attn_w, second_part, table, chunk):
    tokens, model = normed.shape
    width = attn.shape[1]
    half, tile = tokens // 2, 384
    each = tile // chunk

    def body(n_ref, x_ref, rsq_ref, b_ref, attn_ref, q_ref, k_ref, v_ref, w_ref, second_ref, table_ref, out_ref, keep_ref, give_ref):
        three = jnp.concatenate([q_ref[...], k_ref[...], v_ref[...]], axis=1)
        attended = attn_ref[...].astype(BF)
        fill = jnp.zeros((1, 4 * width - chunk), F32)

        def work(at):
            columns = pl.ds(at, tile)
            back = dot(three, w_ref[columns, : 3 * width], NT)
            keep_ref[:, columns] = back[:half]
            give_ref[:, columns] = back[half:].astype(BF)
            first = jnp.sum(back * x_ref[:, columns].astype(F32) * rsq_ref[:, 0:1], axis=0, keepdims=True)
            second = second_ref[:, columns]
            wide = dot(n_ref[:, columns], three, TN).astype(BF)
            last = dot(b_ref[:, columns], attended, TN).astype(BF)
            for c in range(each):
                rows, block = slice(c * chunk, (c + 1) * chunk), at // chunk + c
                out_ref[block, :chunk] = jnp.concatenate([wide[rows], last[rows]], axis=1)
                small = [jnp.concatenate([row[:, rows], fill], axis=1) for row in (first, second)]
                small += [table_ref[...], jnp.zeros((EXTRA - 3, 4 * width), F32)]
                out_ref[block, chunk:] = jnp.concatenate(small, axis=0).astype(BF)

        tiles(model, tile, work)

    return near(
        body, [normed, inputs, rsq, branch, attn, *grads, attn_w, second_part, table],
        [((model // chunk, chunk + EXTRA, 4 * width), BF), ((half, model), F32), ((half, model), BF)],
    )


def finish_input(addends, inputs, gain, grad_middle):
    count, model = addends[0].shape

    def body(low_ref, got_ref, x_ref, gain_ref, mid_ref, out_ref):
        x = x_ref[:count].astype(F32)
        rsq = rsq_of(x)
        unit = x * rsq
        scaled = (low_ref[...].astype(F32) + got_ref[...].astype(F32)) * gain_ref[...]
        out_ref[...] = mid_ref[:count] + rsq * (scaled - unit * jnp.mean(scaled * unit, axis=1, keepdims=True))

    return near(body, [*addends, inputs, gain, grad_middle], [((count, model), F32)])[0]


def finish_output(addends, middle):
    count, model = addends[0].shape

    def body(low_ref, got_ref, mid_ref, out_ref):
        out_ref[...] = (mid_ref[:count] + low_ref[...].astype(F32) + got_ref[...].astype(F32)).astype(BF)

    return near(body, [*addends, middle], [((count, model), BF)])[0]


def rows_of(values, depth):
    if depth % 16:
        own, value = lax.axis_index("tp"), jnp.concatenate(values, axis=1)
        return [lax.dynamic_slice_in_dim(value, (own ^ k) * depth, depth, 0) for k in range(4)]

    def body(*refs):
        own = lax.axis_index("tp")
        for k in range(4):
            at = 0
            for ref in refs[: len(values)]:
                rows = ref[pl.ds(pl.multiple_of((own ^ k) * depth, depth), depth), :]
                refs[len(values) + k][:, at : at + ref.shape[1]] = rows
                at += ref.shape[1]

    return near(body, values, [((depth, sum(v.shape[1] for v in values)), BF)] * 4)


def unpack_mlp(pieces, count, ff):
    depth, width = pieces[0].shape

    def body(*refs):
        own, outs, held = lax.axis_index("tp"), refs[4:-1], refs[-1]
        for k in range(4):
            held[own ^ k] = refs[k][...]
        for i, out in enumerate(outs):
            for a in range(4):
                last = min(count, (a + 1) * ff)
                out[:, a * ff : last] = held[a, :, i * ff : i * ff + last - a * ff].astype(F32)

    return near(body, pieces, [((depth, count), F32)] * (width // ff), [pltpu.VMEM((4, depth, width), BF)])


def unpack_attn(pieces, depth, width, heads, buckets):
    rows = pieces[0].shape[0]

    def body(*refs):
        own, grads, first_ref, second_ref, table_ref, held = lax.axis_index("tp"), refs[4:8], *refs[8:]
        for k in range(4):
            held[own ^ k] = refs[k][...].astype(F32)
        for i, out in enumerate(grads):
            for a in range(4):
                out[:, a * width : (a + 1) * width] = held[a, :depth, i * width : (i + 1) * width]
        small = [held[a, depth : depth + EXTRA] for a in range(4)]
        first_ref[...] = sum(p[0:1, :depth] for p in small)
        second_ref[...] = small[0][1:2, :depth]
        for a in range(4):
            for h in range(heads):
                table_ref[a * heads + h : a * heads + h + 1] = small[a][2:3, h * buckets : (h + 1) * buckets]

    outs = [((depth, 4 * width), F32)] * 4 + [((1, depth), F32)] * 2 + [((4 * heads, buckets), F32)]
    return near(body, pieces, outs, [pltpu.VMEM((4, rows, 4 * width), F32)])


ORDER = (
    "Pa", "I0", "Pm", "a1", "a2", "C0", "M0", "g1", "a3", "u1", "g2", "I1s0", "d1", "a4", "d2", "a5", "C1s0",
    "I1s1", "I1e", "QK", "u2", "R0s0", "g3", "R0s1", "u3", "R0e", "d3", "g4", "u4", "R2s0", "d4", "R2s1", "R2e",
    "u5", "g5", "C1s1", "C1e", "d5", "ML", "rd1", "MB", "B0s0", "rd2", "O0s0", "rg1", "WU", "ru1", "B0e", "O0e",
    "rd3", "ru2", "rg2", "rd4", "B2s0", "rg3", "B2e", "AB", "ru3", "WA", "rd5", "N0s0", "ra1", "rg4", "O2", "ra2",
    "N0e", "rg5", "Xd0", "Xd1", "Xd2", "ra3", "Xd3", "ru4", "ra4", "ru5", "Xu0", "Xu1", "Xu2", "N2", "ra5", "Xa0",
    "Xa1", "Xa2", "Xu3", "Xa3",
)


def shards(
    block_input, cotangent, query_w, key_w, value_w, output_w, gate_w, up_w, down_w,
    first_gain, second_gain, bias_table, rel_bucket, doc_ids,
):
    rows, length, model = block_input.shape
    tokens = rows * length
    own = lax.axis_index("tp")
    parts = lax.axis_size("seq")
    count = lax.axis_size("rows") * parts
    bucket_count, head_count = bias_table.shape
    inner = query_w.shape[1]
    heads = head_count // 4
    dim = inner // head_count
    width = heads * dim
    depth = query_w.shape[0]
    chunk = 4 * depth
    hidden_count = gate_w.shape[1]
    ff = -(-hidden_count // (4 * 256)) * 256
    seq_len = doc_ids.shape[1]
    q_len = 4 * length
    shape = (heads, dim, rows, length)
    lanes = Lanes(count, 4)
    steps, tasks, have = {}, {}, {}

    def do(name):
        def keep(work):
            steps[name] = work
        return keep

    def task(key, names, make):
        def start():
            tasks[key] = Task(make())
            tasks[key].step()

        def end():
            have[key] = tasks[key].result()

        steps.update({name: lambda: tasks[key].step() for name in names})
        steps[names[0]], steps[names[-1]] = start, end

    def core(name, side=0):
        return [f"{name}s{n}" for n in range(CUTS[side])] + [f"{name}e"]

    def attn_blocks():
        weights = [query_w, key_w, value_w, output_w.T]
        gains = [first_gain.reshape(1, depth), second_gain.reshape(1, depth)]
        if depth % 16 == 0:
            return pack_attn(weights, gains, width)
        gains = jnp.pad(jnp.concatenate(gains, axis=0).astype(BF), ((0, EXTRA - 2), (0, 4 * width - depth)))
        return pack_plain(weights, width, gains)

    def mlp_blocks():
        weights = [down_w.T, gate_w, up_w]
        return pack_mlp(weights, ff) if depth % 16 == 0 else pack_plain(weights, ff, None)

    def attn_chunk():
        return gather_ring(lanes, stack_attn(tasks["Pa"].result(), chunk), chunk, 1)

    task("Pa", ["Pa", "Pa-"], lambda: exchange(lanes, attn_blocks()))
    task("Pm", ["Pm", "M0"], lambda: exchange(lanes, mlp_blocks()))
    task("a", ["a1", "a2", "a3", "a4", "a5"], attn_chunk)

    def mlp_chunk(i):
        if "chunks" not in have:
            have["chunks"] = stack_members(have["Pm"], [ff] * 3, PADS if ring_ok(count) else (0, 0, 0))
        return have["chunks"][i]

    task("d", ["d1", "d2", "d3", "d4", "d5"], lambda: gather_ring(lanes, mlp_chunk(0), chunk, -1))
    task("g", ["g1", "g2", "g3", "g4", "g5"], lambda: gather_ring(lanes, mlp_chunk(1), chunk, 1))
    task("u", ["u1", "u2", "u3", "u4", "u5"], lambda: gather_ring(lanes, mlp_chunk(2), chunk, -1))

    task("in", ["I0", *core("I1")], lambda: gather_tokens(lanes, block_input.reshape(tokens, model), CUTS[0]))
    task("cot", ["C0", *core("C1")], lambda: gather_tokens(lanes, cotangent.reshape(tokens, model), CUTS[0]))

    @do("QK")
    def _():
        one_hot = (rel_bucket[:, None] == jnp.arange(bucket_count, dtype=jnp.int32)).astype(F32)
        first = lax.axis_index("seq") * q_len
        one_hot = lax.dynamic_slice_in_dim(one_hot, seq_len - first - q_len, seq_len + q_len, 0)
        own_table = lax.dynamic_slice_in_dim(bias_table, own * heads, heads, 1)
        by_distance = lax.dot_general(own_table, one_hot, (((0,), (1,)), ((), ())), precision=HIGHEST)
        query_doc = lax.dynamic_slice_in_dim(doc_ids, first, q_len, 1)[:, :, None]
        attn_w, chunks = have["a"]
        gain_one, gain_two = spread_gains(chunks, chunk)
        normed, rsq_one, queries, keys, values = project(have["in"], gain_one, attn_w, width)
        queries = lanes.pin(queries)
        if parts > 1:
            keys = lax.all_gather(keys, "seq", axis=0)
            values = lax.all_gather(values, "seq", axis=0)
        else:
            keys, values = keys[None], values[None]
        have.update(
            one_hot=one_hot, attn_w=attn_w, gain_one=gain_one, gain_two=gain_two, normed=normed, rsq_one=rsq_one,
            scores=(queries, keys, values, by_distance, query_doc, doc_ids[:, None, :]),
        )

    def attention():
        have["attn"], keep, give = attn_forward(*have["scores"], have["attn_w"], *shape)
        return sum_tokens(lanes, keep, give, CUTS[0])

    task("branch", [*core("R0"), *core("R2")], attention)

    branch_end, cot_end = steps[core("R2")[-1]], steps[core("C1")[-1]]

    @do(core("R2")[-1])
    def _():
        branch_end()
        middle, normed_mlp = norm_again(have["in"], *have["branch"], have["gain_two"])
        have.update(middle=middle, normed_mlp=lanes.pin(normed_mlp))

    @do(core("C1")[-1])
    def _():
        cot_end()
        have["cot"] = lanes.pin(have["cot"])

    @do("ML")
    def _():
        hidden, slopes = gated(have["normed_mlp"], have["g"][0], have["u"][0])
        have.update(hidden=lanes.pin(hidden), slopes=slopes)

    @do("MB")
    def _():
        have["grad_pair"] = lanes.pin(gated_back(have["cot"], have["d"][0], have["slopes"]))

    task(
        "rd", ["rd1", "rd2", "rd3", "rd4", "rd5"],
        lambda: scatter_ring(lanes, weight_grad(have["cot"], have["hidden"], count), 1, chunk + RPADS[0]),
    )
    task(
        "back", [*core("B0", 1), *core("B2", 1)],
        lambda: sum_tokens(lanes, *back_through(have["grad_pair"], [have["g"][0], have["u"][0]]), CUTS[1]),
    )
    if "rm1" in ORDER:
        task(
            "rm", ["rm1", "rm2", "rm3", "rm4", "rm5"],
            lambda: scatter_ring(lanes, weight_grad(have["normed_mlp"], have["grad_pair"], count), -1, chunk + RPADS[1]),
        )
    else:
        @do("WU")
        def _():
            have["up_blocks"] = lanes.pin(weight_grad(have["normed_mlp"], have["grad_pair"], count, ff, 2 * ff))

        task(
            "rg", ["rg1", "rg2", "rg3", "rg4", "rg5"],
            lambda: scatter_ring(
                lanes, weight_grad(have["normed_mlp"], have["grad_pair"], count, 0, ff), -1, chunk + RPADS[1]
            ),
        )
        task("ru", ["ru1", "ru2", "ru3", "ru4", "ru5"], lambda: scatter_ring(lanes, have["up_blocks"], 1, chunk + RPADS[2]))
    task("out", [*core("O0", 1), "O2"], lambda: scatter_tokens(lanes, *back_through(have["hidden"], [have["d"][0]]), CUTS[1]))

    @do("AB")
    def _():
        grad_middle, grad_branch, second_part, grad_attn = norm_back(
            have["middle"], have["cot"], *have["back"], have["gain_two"], have["attn_w"], width
        )
        grad_q, grad_k, grad_v, table = attn_backward(
            *have["scores"], have["attn"], lanes.pin(grad_attn), have["one_hot"], *shape, 4 * width
        )
        if parts > 1:
            grad_k = lax.psum_scatter(grad_k, "seq", scatter_dimension=0, tiled=True)
            grad_v = lax.psum_scatter(grad_v, "seq", scatter_dimension=0, tiled=True)
        have.update(
            grad_middle=grad_middle, grad_branch=grad_branch, second_part=second_part, table=table,
            grads=(lanes.pin(grad_q), grad_k[0], grad_v[0]),
        )

    @do("WA")
    def _():
        four_grad, keep, give = attn_weight_grads(
            have["normed"], have["in"], have["rsq_one"], have["grad_branch"], have["attn"], have["grads"],
            have["attn_w"], have["second_part"], have["table"], chunk,
        )
        have.update(four_grad=lanes.pin(four_grad), in_parts=(keep, give))

    task("ra", ["ra1", "ra2", "ra3", "ra4", "ra5"], lambda: scatter_ring(lanes, have["four_grad"], -1, chunk + EXTRA))
    task("grad_in", [*core("N0", 1), "N2"], lambda: scatter_tokens(lanes, *have["in_parts"], CUTS[1]))

    if "rm1" in ORDER:
        one, two = ["rd"], ["rm"]
    else:
        one, two = ["rd", "rg"], ["ru"]
    task("Xd", ["Xd0", "Xd1", "Xd2", "Xd3"], lambda: exchange(lanes, rows_of([have[k] for k in one], depth), False))
    task("Xu", ["Xu0", "Xu1", "Xu2", "Xu3"], lambda: exchange(lanes, rows_of([have[k] for k in two], depth), False))
    task("Xa", ["Xa0", "Xa1", "Xa2", "Xa3"], lambda: exchange(lanes, split_attn(have["ra"], depth, width), False))

    for name in ORDER:
        steps[name]()
    block_output = finish_output(have["out"], have["middle"])
    input_grad = finish_input(have["grad_in"], have["in"], have["gain_one"], have["grad_middle"])

    mlp = unpack_mlp(have["Xd"], hidden_count, ff) + unpack_mlp(have["Xu"], hidden_count, ff)
    *grads, first_grad, second_grad, table_grad = unpack_attn(have["Xa"], depth, width, heads, bucket_count)
    return (
        block_output.reshape(rows, length, model), input_grad.reshape(rows, length, model),
        grads[0], grads[1], grads[2], grads[3].T,
        mlp[1], mlp[2], mlp[0].T, first_grad.reshape(depth), second_grad.reshape(depth), table_grad.T,
    )


def solution(mesh):
    row_count, blk_count = mesh.shape["rows"], mesh.shape["blk"]
    fine = Mesh(mesh.devices.reshape(row_count, blk_count // 4, 4), ("rows", "seq", "tp"))
    every = ("rows", "seq", "tp")
    tokens = P("rows", ("seq", "tp"), None)
    deep, wide, flat = P(every, None), P(None, every), P(every)
    return jax.shard_map(
        shards,
        mesh=fine,
        in_specs=(tokens, tokens, deep, deep, deep, wide, deep, deep, wide, flat, flat, P(), P(), P("rows", None)),
        out_specs=(tokens, tokens, deep, deep, deep, wide, deep, deep, wide, flat, flat, P()),
        check_vma=False,
    )
```

```python
import math

import jax
import jax.numpy as jnp
from jax import lax
from jax.experimental import pallas as pl
from jax.experimental.pallas import tpu as pltpu
from jax.sharding import Mesh, PartitionSpec as P

EPSILON = 1e-06
BF = jnp.bfloat16
F32 = jnp.float32
HIGHEST = lax.Precision.HIGHEST
RING = ("rows", "seq")
MAX_RING = 8
EXTRA = 8
PADS = (8, 6, 4)
RPADS = (6, 4, 6)
CUTS = (2, 1)
FREE = pl.CostEstimate(flops=0, transcendentals=0, bytes_accessed=0)


def dot(left, right, dims, out=F32):
    return lax.dot_general(left, right, (dims, ((), ())), preferred_element_type=out)


NN = ((1,), (0,))
NT = ((1,), (1,))
TN = ((0,), (0,))


def ring_order(count):
    return list(range(0, count, 2)) + list(range(count - 1, 0, -2))


def ring_places(count):
    half = count // 2
    group = lax.axis_index(RING)
    place = jnp.where(group % 2 == 0, group // 2, count - 1 - group // 2)
    places = []
    for k in range(count):
        at = place - k
        at = jnp.where(at < 0, at + count, at)
        places.append(jnp.where(at < half, 2 * at, 2 * (count - 1 - at) + 1))
    return places


def ring_ok(count):
    return count <= MAX_RING and count % 2 == 0


class Lanes:
    def __init__(self, count, ways):
        order = ring_order(count)
        self.pairs = {
            step: [(order[i], order[(i + step) % count]) for i in range(count)] for step in (1, -1)
        }
        self.count, self.ways, self.last = count, ways, None

    def pin(self, *values):
        if self.last is not None:
            values = lax.optimization_barrier((*values, self.last))[:-1]
        self.last = values[0]
        return values if len(values) > 1 else values[0]

    def shift(self, value, step):
        return lax.ppermute(value, RING, self.pairs[step])

    def partner(self, value, bit):
        return lax.ppermute(value, "tp", [(i, i ^ bit) for i in range(self.ways)])


class Task:
    def __init__(self, steps):
        self.steps, self.value = steps, None

    def step(self):
        if self.steps is not None:
            try:
                next(self.steps)
            except StopIteration as stop:
                self.value, self.steps = stop.value, None

    def result(self):
        while self.steps is not None:
            self.step()
        return self.value


def gather_ring(lanes, chunk, keep, lead):
    count = lanes.count
    if not ring_ok(count):
        got = lax.all_gather(chunk, RING, axis=0) if count > 1 else chunk[None]
        return got[:, :keep].reshape(-1, chunk.shape[1]), [got[i] for i in range(count)]
    chunk = lanes.pin(chunk)
    moving = {lead: chunk, -lead: chunk}
    got = [chunk]
    for k in range(1, count // 2):
        moving = {step: lanes.shift(value, step) for step, value in moving.items()}
        yield
        moving = dict(zip(moving, lanes.pin(*moving.values())))
        got += [moving[1], moving[-1]]
    last = lanes.shift(moving[lead], lead)
    yield
    got.append(lanes.pin(last))
    return place_rows(got, count, keep), got


def chunk_order(count):
    order = [0]
    for k in range(1, count // 2):
        order += [k, count - k]
    return order + [count // 2]


def place_rows(got, count, keep):
    def body(*refs):
        places = ring_places(count)
        for ref, k in zip(refs, chunk_order(count)):
            refs[-1][pl.ds(pl.multiple_of(places[k] * keep, keep), keep), :] = ref[:keep]

    return near(body, got, [((count * keep, got[0].shape[1]), BF)])[0]


def scatter_ring(lanes, blocks, lead, rows):
    count, size, _ = blocks.shape
    if count == 1:
        return blocks[0]
    if not ring_ok(count):
        return lax.psum_scatter(blocks, RING, scatter_dimension=0, tiled=True)[0]
    (far,) = add_blocks(blocks, [(count // 2, None)], rows)
    moving = {lead: lanes.shift(lanes.pin(far), lead)}
    yield
    for j in range(count // 2 - 1, 0, -1):
        arrived = dict(zip(moving, lanes.pin(*moving.values()) if len(moving) > 1 else (lanes.pin(moving[lead]),)))
        sums = add_blocks(blocks, [(-j * step, arrived.get(step)) for step in (1, -1)], rows)
        moving = {step: lanes.shift(value, step) for step, value in zip((1, -1), lanes.pin(*sums))}
        yield
    came, back = lanes.pin(*moving.values())
    return add_blocks(blocks, [(0, came)], size, back)[0]


def add_blocks(blocks, terms, rows, more=None):
    count, size, width = blocks.shape
    came = [c for _, c in terms if c is not None] + ([] if more is None else [more])

    def body(blocks_ref, *refs):
        places = ring_places(count)
        given, outs = list(refs[: len(came)]), refs[len(came) :]
        for (k, c), out in zip(terms, outs):
            total = blocks_ref[places[k % count]].astype(F32)
            if c is not None:
                total = total + given.pop(0)[:size].astype(F32)
            if more is not None:
                total = total + given.pop(0)[:size].astype(F32)
            out[:size] = total.astype(BF)
            if rows > size:
                out[size:] = jnp.zeros((rows - size, width), BF)

    return near(body, [blocks, *came], [((rows, width), BF)] * len(terms))


def block_of(index):
    return index % 2 * 2 + index // 2


def gather_tokens(lanes, value, cuts):
    value = lanes.pin(value)
    got = lanes.partner(value, 2)
    yield
    value = jnp.concatenate([value, lanes.pin(got)], axis=0)
    got = yield from over_core(lanes, value, cuts)
    return jnp.concatenate([value, *got], axis=0)


def over_core(lanes, give, cuts):
    rows, pieces, first = give.shape[0], [], 0
    for n in range(cuts):
        last = rows * (n + 1) // cuts // 16 * 16 if n + 1 < cuts else rows
        got = lanes.partner(lanes.pin(give[first:last]), 1)
        yield
        pieces.append(lanes.pin(got))
        first = last
    return pieces


def sum_tokens(lanes, keep, give, cuts):
    got = yield from over_core(lanes, give, cuts)
    low = lanes.pin(add_halves(keep, got, False))
    got = lanes.partner(low, 2)
    yield
    low = lanes.pin(add_halves(low, [lanes.pin(got)], True))
    got = yield from over_core(lanes, low, cuts)
    return low, got


def add_halves(left, pieces, swapped):
    rows = left.shape[0]
    half = rows // 2

    def body(left_ref, *refs):
        first = 0
        for ref in refs[:-1]:
            for at in range(0, ref.shape[0], half if swapped else ref.shape[0]):
                count = half if swapped else ref.shape[0]
                to = half - at if swapped else first + at
                total = left_ref[to : to + count].astype(F32) + ref[at : at + count].astype(F32)
                refs[-1][to : to + count] = total.astype(BF)
            first += ref.shape[0]

    return near(body, [left, *pieces], [(left.shape, BF)])[0]


def scatter_tokens(lanes, keep, give, cuts):
    got = yield from over_core(lanes, give, cuts)
    low = lanes.pin(add_halves(keep, got, False))
    mine = low.shape[0] // 2
    got = lanes.partner(low[mine:], 2)
    yield
    return low[:mine], lanes.pin(got)


def exchange(lanes, blocks, at_once=True):
    pieces = [blocks[0]] + [None] * 3
    for k in (2, 3, 1):
        pieces[k] = lanes.partner(lanes.pin(blocks[k]), k)
        if not at_once:
            yield
    if at_once:
        yield
    pieces[1:] = lanes.pin(*pieces[1:])
    return pieces


def by_member(pieces):
    own, chosen = lax.axis_index("tp"), []
    for a in range(4):
        piece = pieces[a]
        for mine in range(1, 4):
            piece = jnp.where(own == mine, pieces[a ^ mine], piece)
        chosen.append(piece)
    return chosen


def stack_members(pieces, widths, pads):
    depth = pieces[0].shape[0]
    if depth % 16:
        pieces = jnp.concatenate(by_member(pieces), axis=0)
        starts = [sum(widths[:i]) for i in range(len(widths))]
        return [jnp.pad(pieces[:, a : a + w], ((0, p), (0, 0))) for a, w, p in zip(starts, widths, pads)]

    def body(*refs):
        own = lax.axis_index("tp")
        at = 0
        for width, pad, out in zip(widths, pads, refs[4:]):
            for k in range(4):
                out[pl.ds(pl.multiple_of((own ^ k) * depth, depth), depth), :] = refs[k][:, at : at + width]
            if pad:
                out[4 * depth :] = jnp.zeros((pad, width), BF)
            at += width

    return near(body, pieces, [((4 * depth + pad, width), BF) for width, pad in zip(widths, pads)])


def stack_attn(pieces, chunk):
    depth, width = chunk // 4, pieces[0].shape[1]
    if depth % 16:
        pieces = by_member(pieces)
        gains = jnp.concatenate([p[depth : depth + 2, :depth] for p in pieces], axis=1)
        gains = jnp.pad(gains, ((0, EXTRA - 2), (0, width - chunk)))
        return jnp.concatenate([p[:depth] for p in pieces] + [gains], axis=0)

    def body(*refs):
        own, out, gains_ref = lax.axis_index("tp"), refs[4], refs[5]
        for k in range(4):
            out[pl.ds(pl.multiple_of((own ^ k) * depth, depth), depth), :] = refs[k][:depth]
            gains_ref[own ^ k] = refs[k][depth:, :depth].astype(F32)
        gains = [gains_ref[a] for a in range(4)] + [jnp.zeros((EXTRA, width - chunk), F32)]
        out[chunk:] = jnp.concatenate(gains, axis=1).astype(BF)

    return near(body, pieces, [((chunk + EXTRA, width), BF)], [pltpu.VMEM((4, EXTRA, depth), F32)])[0]


def split_attn(total, depth, width):
    chunk = 4 * depth
    if depth % 16:
        tables = jnp.pad(total[chunk + 2 : chunk + 3], ((2, EXTRA - 3), (0, 0)))
        blocks = []
        for large, pair in zip(rows_of([total], depth), rows_of([total[chunk : chunk + 2, :chunk].T], depth)):
            pair = jnp.pad(pair.T, ((0, EXTRA - 2), (0, 4 * width - depth)))
            blocks.append(jnp.concatenate([large, pair + tables], axis=0))
        return blocks

    def body(total_ref, *refs):
        own, small_ref = lax.axis_index("tp"), refs[4]
        fill = jnp.zeros((2, 4 * width - depth), F32)
        small = total_ref[chunk : chunk + EXTRA].astype(F32)
        below = jnp.concatenate([small[2:3], jnp.zeros((EXTRA - 3, 4 * width), F32)], axis=0)
        for a in range(4):
            pair = jnp.concatenate([small[0:2, a * depth : (a + 1) * depth], fill], axis=1)
            small_ref[a] = jnp.concatenate([pair, below], axis=0)
        for k in range(4):
            refs[k][:depth] = total_ref[pl.ds(pl.multiple_of((own ^ k) * depth, depth), depth), :]
            refs[k][depth:] = small_ref[own ^ k].astype(BF)

    return near(
        body, [total], [((depth + EXTRA, 4 * width), BF)] * 4, [pltpu.VMEM((4, EXTRA, 4 * width), F32)]
    )


def run(body, grid, ins, outs, scratch=(), vmem=24):
    def spec(block, index_map):
        return pl.BlockSpec(block, index_map)

    arrays, in_specs = [], []
    for item in ins:
        array, block, index_map = item if isinstance(item, tuple) else (item, item.shape, None)
        if index_map is None:
            index_map = lambda *_, n=array.ndim: (0,) * n
        arrays.append(array)
        in_specs.append(spec(block, index_map))
    out_specs = [
        spec(block or shape, index_map or (lambda *_, n=len(shape): (0,) * n)) for shape, _, block, index_map in outs
    ]
    return pl.pallas_call(
        body, grid=grid, in_specs=in_specs, out_specs=out_specs,
        out_shape=[jax.ShapeDtypeStruct(shape, dtype) for shape, dtype, _, _ in outs],
        scratch_shapes=list(scratch),
        compiler_params=pltpu.CompilerParams(
            dimension_semantics=("arbitrary",) * len(grid), vmem_limit_bytes=vmem << 20
        ),
        cost_estimate=FREE,
    )(*arrays)


def near(body, arrays, outs, scratch=(), vmem=16):
    spec = pl.BlockSpec(memory_space=pltpu.VMEM)
    return pl.pallas_call(
        body, in_specs=[spec] * len(arrays), out_specs=[spec] * len(outs),
        out_shape=[jax.ShapeDtypeStruct(shape, dtype) for shape, dtype in outs],
        scratch_shapes=list(scratch),
        compiler_params=pltpu.CompilerParams(vmem_limit_bytes=vmem << 20),
        cost_estimate=FREE,
    )(*arrays)


def far(arrays):
    return [pltpu.with_memory_space_constraint(a, pltpu.HBM) for a in arrays]


def whole(shape, dtype):
    return (shape, dtype, None, None)


def pack_attn(weights, gains, width):
    depth, inner = weights[0].shape

    def body(q_ref, k_ref, v_ref, o_ref, first_ref, second_ref, *rest):
        outs, out_ref = rest[:4], rest[4]
        own = lax.axis_index("tp")
        extra = jnp.concatenate([first_ref[...], second_ref[...], jnp.zeros((EXTRA - 2, depth), F32)], axis=0)
        extra = jnp.concatenate([extra, jnp.zeros((EXTRA, 4 * width - depth), F32)], axis=1).astype(BF)
        for a in range(4):
            parts = [r[:, a * width : (a + 1) * width] for r in (q_ref, k_ref, v_ref, o_ref)]
            out_ref[a ^ own, :depth] = jnp.concatenate(parts, axis=1).astype(BF)
            out_ref[a ^ own, depth:] = extra
        for k in range(4):
            outs[k][...] = out_ref[k]

    shape = (depth + EXTRA, 4 * width)
    return run(body, (1,), far([*weights, *gains]), [whole(shape, BF)] * 4, [pltpu.VMEM((4, *shape), BF)])


def pack_mlp(weights, ff):
    depth, count = weights[0].shape

    def body(*refs):
        own, out_ref = lax.axis_index("tp"), refs[-1]
        for a in range(4):
            parts = []
            for ref in refs[: len(weights)]:
                last = min(count, (a + 1) * ff)
                parts.append(ref[:, a * ff : last])
                if last < (a + 1) * ff:
                    parts.append(jnp.zeros((depth, (a + 1) * ff - last), F32))
            out_ref[a ^ own] = jnp.concatenate(parts, axis=1).astype(BF)
        for k in range(4):
            refs[len(weights) + k][...] = out_ref[k]

    shape = (depth, len(weights) * ff)
    return run(body, (1,), far(weights), [whole(shape, BF)] * 4, [pltpu.VMEM((4, *shape), BF)])


def pack_plain(weights, width, extra):
    own = lax.axis_index("tp")
    weights = [jnp.pad(w.astype(BF), ((0, 0), (0, 4 * width - w.shape[1]))) for w in weights]
    blocks = []
    for k in range(4):
        block = jnp.concatenate([lax.dynamic_slice_in_dim(w, (own ^ k) * width, width, 1) for w in weights], axis=1)
        blocks.append(block if extra is None else jnp.concatenate([block, extra], axis=0))
    return blocks


def spread_gains(chunks, chunk):
    count = len(chunks)
    ring = ring_ok(count)

    def body(*refs):
        one_ref, two_ref, rows_ref = refs[-3:]
        places = ring_places(count) if ring else None
        for ref, k in zip(refs, chunk_order(count) if ring else range(count)):
            rows_ref[places[k] if ring else k] = ref[chunk : chunk + 2, :chunk].astype(F32)
        both = jnp.concatenate([rows_ref[r] for r in range(count)], axis=1)
        one_ref[...], two_ref[...] = both[0:1], both[1:2]

    return near(body, chunks, [((1, count * chunk), F32)] * 2, [pltpu.VMEM((count, 2, chunk), F32)])


def tiles(total, tile, work):
    lax.fori_loop(0, total // tile, lambda i, _: work(pl.multiple_of(i * tile, tile)), None, unroll=2)


def rsq_of(value):
    return lax.rsqrt(jnp.mean(value * value, axis=1, keepdims=True) + EPSILON)


def project(inputs, gain, weights, width):
    tokens, model = inputs.shape
    tile = tokens // 2

    def body(x_ref, gain_ref, w_ref, normed_ref, rsq_ref, q_ref, k_ref, v_ref):
        for at in range(0, tokens, tile):
            rows = slice(at, at + tile)
            x = x_ref[rows].astype(F32)
            rsq = rsq_of(x)
            normed = (x * rsq * gain_ref[...]).astype(BF)
            normed_ref[rows] = normed
            rsq_ref[rows] = jnp.broadcast_to(rsq, (tile, 128))
            three = dot(normed, w_ref[:, : 3 * width], NN).astype(BF)
            for i, ref in enumerate((q_ref, k_ref, v_ref)):
                ref[rows] = three[:, i * width : (i + 1) * width]

    return near(
        body, [inputs, gain, weights],
        [((tokens, model), BF), ((tokens, 128), F32)] + [((tokens, width), BF)] * 3,
    )


def head_scores(own, row, head, dim, rows, length, q_ref, k_ref, w_ref, qd_ref, kd_ref):
    lanes = slice(head * dim, (head + 1) * dim)
    starts = [pl.multiple_of((block_of(own ^ a) * rows + row) * length, length) for a in range(4)]
    queries = jnp.concatenate([q_ref[pl.ds(s, length), lanes] for s in starts], axis=0)
    keys = take_keys(k_ref, starts, length, lanes)
    q_len, k_len = queries.shape[0], keys.shape[0]
    scores = dot(queries, keys, NT)
    bias = jnp.broadcast_to(w_ref[pl.ds(head, 1), :], (q_len, q_len + k_len))
    bias = pltpu.roll(bias, k_len, 1, stride=1, stride_axis=0)[:, :k_len]
    same = qd_ref[row] == kd_ref[row]
    expo = jnp.where(same, jnp.exp(scores + bias), 0.0)
    return queries, keys, expo, starts, lanes


def take_keys(ref, starts, length, lanes):
    return jnp.concatenate(
        [ref[g, pl.ds(s, length), lanes] for g in range(ref.shape[0]) for s in starts], axis=0
    )


def attn_forward(q, k, v, by_distance, query_doc, key_doc, attn_w, heads, dim, rows, length):
    tokens, width = q.shape
    model = attn_w.shape[0]
    half = tokens // 2

    def body(q_ref, k_ref, v_ref, w_ref, qd_ref, kd_ref, o_ref, attn_ref, keep_ref, give_ref, part_ref):
        def one_row(row):
            forward_row(row, q_ref, k_ref, v_ref, w_ref, qd_ref, kd_ref, o_ref, attn_ref, part_ref)

        lax.fori_loop(0, rows, lambda row, _: one_row(row), None)
        keep_ref[...] = part_ref[:half]
        give_ref[...] = part_ref[half:].astype(BF)

    def forward_row(row, q_ref, k_ref, v_ref, w_ref, qd_ref, kd_ref, o_ref, attn_ref, part_ref):
        own, out = lax.axis_index("tp"), []
        for head in range(heads):
            _, _, expo, starts, lanes = head_scores(
                own, row, head, dim, rows, length, q_ref, k_ref, w_ref, qd_ref, kd_ref
            )
            values = take_keys(v_ref, starts, length, lanes)
            low = expo.astype(BF)
            totals = jnp.sum(low.astype(F32), axis=1, keepdims=True)
            out.append(dot(low, values, NN) / totals)
        out = jnp.concatenate(out, axis=1)
        part = dot(out.astype(BF), o_ref[:, 3 * width :], NT)
        for a, s in enumerate(starts):
            attn_ref[pl.ds(s, length), :] = out[a * length : (a + 1) * length]
            part_ref[pl.ds(s, length), :] = part[a * length : (a + 1) * length]

    return near(
        body, [q, k, v, by_distance, query_doc, key_doc, attn_w],
        [((tokens, width), F32), ((half, model), F32), ((half, model), BF)],
        [pltpu.VMEM((tokens, model), F32)],
    )


def attn_backward(q, k, v, by_distance, query_doc, key_doc, attn, grad, one_hot, heads, dim, rows, length, columns):
    buckets = one_hot.shape[1]

    def body(
        q_ref, k_ref, v_ref, w_ref, qd_ref, kd_ref, attn_ref, grad_ref, hot_ref,
        gq_ref, gk_ref, gv_ref, table_ref, diag_ref,
    ):
        diag_ref[...] = jnp.zeros(diag_ref.shape, F32)

        def one_row(row):
            backward_row(
                row, q_ref, k_ref, v_ref, w_ref, qd_ref, kd_ref, attn_ref, grad_ref, gq_ref, gk_ref, gv_ref, diag_ref
            )

        lax.fori_loop(0, rows, lambda row, _: one_row(row), None)
        table = lax.dot_general(
            diag_ref[...], hot_ref[...], (NN, ((), ())), precision=HIGHEST, preferred_element_type=F32
        )
        table = [table[h : h + 1] for h in range(heads)]
        table_ref[...] = jnp.concatenate(table + [jnp.zeros((1, columns - heads * buckets), F32)], axis=1)

    def backward_row(
        row, q_ref, k_ref, v_ref, w_ref, qd_ref, kd_ref, attn_ref, grad_ref, gq_ref, gk_ref, gv_ref, diag_ref
    ):
        own = lax.axis_index("tp")
        grads_q, grads_k, grads_v, diags = [], [], [], []
        for head in range(heads):
            queries, keys, expo, starts, lanes = head_scores(
                own, row, head, dim, rows, length, q_ref, k_ref, w_ref, qd_ref, kd_ref
            )
            values = take_keys(v_ref, starts, length, lanes)
            grads = jnp.concatenate([grad_ref[pl.ds(s, length), lanes] for s in starts], axis=0)
            outs = jnp.concatenate([attn_ref[pl.ds(s, length), lanes] for s in starts], axis=0)
            low = expo.astype(BF)
            totals = jnp.sum(low.astype(F32), axis=1, keepdims=True)
            grad_low = (grads / totals).astype(BF)
            grad_total = -jnp.sum(grads * outs, axis=1, keepdims=True) / totals
            grad_score = (expo * (dot(grad_low, values, NT) + grad_total)).astype(BF)
            grads_q.append(dot(grad_score, keys, NN))
            grads_k.append(dot(grad_score, queries, TN))
            grads_v.append(dot(low, grad_low, TN))
            q_len, k_len = grad_score.shape
            row_at = lax.broadcasted_iota(jnp.int32, (q_len, q_len), 0)
            column_at = lax.broadcasted_iota(jnp.int32, (q_len, q_len), 1)
            flip = jnp.where(row_at + column_at == q_len - 1, 1.0, 0.0).astype(BF)
            turned = dot(flip, grad_score, NN)
            turned = jnp.concatenate([turned, jnp.zeros((q_len, q_len), F32)], axis=1)
            turned = pltpu.roll(turned, 1, 1, stride=1, stride_axis=0)
            diags.append(jnp.sum(turned, axis=0, keepdims=True))
        joined = jnp.concatenate(grads_q, axis=1).astype(BF)
        for a, s in enumerate(starts):
            gq_ref[pl.ds(s, length), :] = joined[a * length : (a + 1) * length]
        for parts, ref in ((grads_k, gk_ref), (grads_v, gv_ref)):
            joined = jnp.concatenate(parts, axis=1).astype(BF)
            for g in range(ref.shape[0]):
                for a, s in enumerate(starts):
                    at = (g * 4 + a) * length
                    ref[g, pl.ds(s, length), :] = joined[at : at + length]
        diag_ref[...] += jnp.concatenate(diags, axis=0)

    return near(
        body, [q, k, v, by_distance, query_doc, key_doc, attn, grad, one_hot],
        [(q.shape, BF), (k.shape, BF), (v.shape, BF), ((1, columns), F32)],
        [pltpu.VMEM(by_distance.shape, F32)],
    )


def in_halves(low, others, tile):
    places = []
    for ref in (low, *others):
        places += [(ref, at) for at in range(0, ref.shape[0], tile)]
    return lambda i: places[i][0][places[i][1] : places[i][1] + tile].astype(F32)


def norm_again(inputs, low, others, gain):
    tokens, model = inputs.shape
    tile = tokens // 4

    def body(x_ref, gain_ref, low_ref, *refs):
        middle_ref, normed_ref = refs[-2:]
        read = in_halves(low_ref, refs[:-2], tile)
        for i in range(tokens // tile):
            rows = slice(i * tile, (i + 1) * tile)
            middle = x_ref[rows].astype(F32) + read(i)
            middle_ref[rows] = middle
            normed_ref[rows] = (middle * rsq_of(middle) * gain_ref[...]).astype(BF)

    return near(body, [inputs, gain, low, *others], [((tokens, model), F32), ((tokens, model), BF)])


def norm_back(middle, cot, low, others, gain, attn_w, width):
    tokens, model = middle.shape
    tile = tokens // 4

    def body(m_ref, cot_ref, gain_ref, w_ref, low_ref, *refs):
        mid_ref, branch_ref, gain_out_ref, attn_ref = refs[-4:]
        read = in_halves(low_ref, refs[:-4], tile)
        gain_sum = jnp.zeros((1, model), F32)
        for i in range(tokens // tile):
            rows = slice(i * tile, (i + 1) * tile)
            grad = read(i)
            middle = m_ref[rows]
            rsq = rsq_of(middle)
            unit = middle * rsq
            scaled = grad * gain_ref[...]
            back = cot_ref[rows].astype(F32) + rsq * (scaled - unit * jnp.mean(scaled * unit, axis=1, keepdims=True))
            mid_ref[rows] = back
            branch_ref[rows] = back.astype(BF)
            gain_sum += jnp.sum(grad * unit, axis=0, keepdims=True)
        gain_out_ref[...] = gain_sum
        attn_ref[...] = dot(branch_ref[...], w_ref[:, 3 * width :], NN)

    return near(
        body, [middle, cot, gain, attn_w, low, *others],
        [((tokens, model), F32), ((tokens, model), BF), ((1, model), F32), ((tokens, width), F32)],
    )


def gated(normed, gate_b, up_b):
    tokens, ff = normed.shape[0], gate_b.shape[1]
    tile = 256
    scale = math.sqrt(2.0 / math.pi)

    def body(x_ref, gate_ref, up_ref, hidden_ref, slopes_ref):
        def work(at):
            columns = pl.ds(at, tile)
            gate, up = dot(x_ref[...], gate_ref[:, columns], NN), dot(x_ref[...], up_ref[:, columns], NN)
            square = gate * gate
            tanh = jnp.tanh(scale * gate * (1.0 + 0.044715 * square))
            curve = 0.5 * (1.0 + tanh)
            slope = curve + 0.5 * gate * (1.0 - tanh * tanh) * (scale * (1.0 + 3 * 0.044715 * square))
            activated = gate * curve
            hidden_ref[:, columns] = (activated * up).astype(BF)
            slopes_ref[:, columns] = up * slope
            slopes_ref[:, pl.ds(pl.multiple_of(ff + at, tile), tile)] = activated

        tiles(ff, tile, work)

    return near(body, [normed, gate_b, up_b], [((tokens, ff), BF), ((tokens, 2 * ff), F32)])


def gated_back(cot, down_b, slopes):
    tokens, ff = cot.shape[0], down_b.shape[1]
    tile = 256

    def body(cot_ref, down_ref, slopes_ref, pair_ref):
        def work(at):
            grad = dot(cot_ref[...], down_ref[:, pl.ds(at, tile)], NN)
            for columns in (pl.ds(at, tile), pl.ds(pl.multiple_of(ff + at, tile), tile)):
                pair_ref[:, columns] = (grad * slopes_ref[:, columns]).astype(BF)

        tiles(ff, tile, work)

    return near(body, [cot, down_b, slopes], [((tokens, 2 * ff), BF)])[0]


def weight_grad(left, right, count, first=0, last=None):
    model = left.shape[1]
    last = last or right.shape[1]
    tile, chunk = 384, model // count

    def body(left_ref, right_ref, out_ref):
        def work(at):
            part = dot(left_ref[:, pl.ds(at, tile)], right_ref[:, first:last], TN).astype(BF)
            for c in range(tile // chunk):
                out_ref[at // chunk + c] = part[c * chunk : (c + 1) * chunk]

        tiles(model, tile, work)

    return near(body, [left, right], [((count, chunk, last - first), BF)])[0]


def back_through(left, rights):
    tokens, model = left.shape[0], rights[0].shape[0]
    half, tile = tokens // 2, 384

    def body(left_ref, *refs):
        keep_ref, give_ref = refs[-2:]

        def work(at):
            columns = pl.ds(at, tile)
            total, first = None, 0
            for ref in refs[:-2]:
                last = first + ref.shape[1]
                term = dot(left_ref[:, first:last], ref[columns, :], NT)
                total, first = term if total is None else total + term, last
            keep_ref[:, columns] = total[:half]
            give_ref[:, columns] = total[half:].astype(BF)

        tiles(model, tile, work)

    return near(body, [left, *rights], [((half, model), F32), ((half, model), BF)])


def attn_weight_grads(normed, inputs, rsq, branch, attn, grads, attn_w, second_part, table, chunk):
    tokens, model = normed.shape
    width = attn.shape[1]
    half, tile = tokens // 2, 384
    each = tile // chunk

    def body(n_ref, x_ref, rsq_ref, b_ref, attn_ref, q_ref, k_ref, v_ref, w_ref, second_ref, table_ref, out_ref, keep_ref, give_ref):
        three = jnp.concatenate([q_ref[...], k_ref[...], v_ref[...]], axis=1)
        attended = attn_ref[...].astype(BF)
        fill = jnp.zeros((1, 4 * width - chunk), F32)

        def work(at):
            columns = pl.ds(at, tile)
            back = dot(three, w_ref[columns, : 3 * width], NT)
            keep_ref[:, columns] = back[:half]
            give_ref[:, columns] = back[half:].astype(BF)
            first = jnp.sum(back * x_ref[:, columns].astype(F32) * rsq_ref[:, 0:1], axis=0, keepdims=True)
            second = second_ref[:, columns]
            wide = dot(n_ref[:, columns], three, TN).astype(BF)
            last = dot(b_ref[:, columns], attended, TN).astype(BF)
            for c in range(each):
                rows, block = slice(c * chunk, (c + 1) * chunk), at // chunk + c
                out_ref[block, :chunk] = jnp.concatenate([wide[rows], last[rows]], axis=1)
                small = [jnp.concatenate([row[:, rows], fill], axis=1) for row in (first, second)]
                small += [table_ref[...], jnp.zeros((EXTRA - 3, 4 * width), F32)]
                out_ref[block, chunk:] = jnp.concatenate(small, axis=0).astype(BF)

        tiles(model, tile, work)

    return near(
        body, [normed, inputs, rsq, branch, attn, *grads, attn_w, second_part, table],
        [((model // chunk, chunk + EXTRA, 4 * width), BF), ((half, model), F32), ((half, model), BF)],
    )


def finish_input(addends, inputs, gain, grad_middle):
    count, model = addends[0].shape

    def body(low_ref, got_ref, x_ref, gain_ref, mid_ref, out_ref):
        x = x_ref[:count].astype(F32)
        rsq = rsq_of(x)
        unit = x * rsq
        scaled = (low_ref[...].astype(F32) + got_ref[...].astype(F32)) * gain_ref[...]
        out_ref[...] = mid_ref[:count] + rsq * (scaled - unit * jnp.mean(scaled * unit, axis=1, keepdims=True))

    return near(body, [*addends, inputs, gain, grad_middle], [((count, model), F32)])[0]


def finish_output(addends, middle):
    count, model = addends[0].shape

    def body(low_ref, got_ref, mid_ref, out_ref):
        out_ref[...] = (mid_ref[:count] + low_ref[...].astype(F32) + got_ref[...].astype(F32)).astype(BF)

    return near(body, [*addends, middle], [((count, model), BF)])[0]


def rows_of(values, depth):
    if depth % 16:
        own, value = lax.axis_index("tp"), jnp.concatenate(values, axis=1)
        return [lax.dynamic_slice_in_dim(value, (own ^ k) * depth, depth, 0) for k in range(4)]

    def body(*refs):
        own = lax.axis_index("tp")
        for k in range(4):
            at = 0
            for ref in refs[: len(values)]:
                rows = ref[pl.ds(pl.multiple_of((own ^ k) * depth, depth), depth), :]
                refs[len(values) + k][:, at : at + ref.shape[1]] = rows
                at += ref.shape[1]

    return near(body, values, [((depth, sum(v.shape[1] for v in values)), BF)] * 4)


def unpack_mlp(pieces, count, ff):
    depth, width = pieces[0].shape

    def body(*refs):
        own, outs, held = lax.axis_index("tp"), refs[4:-1], refs[-1]
        for k in range(4):
            held[own ^ k] = refs[k][...]
        for i, out in enumerate(outs):
            for a in range(4):
                last = min(count, (a + 1) * ff)
                out[:, a * ff : last] = held[a, :, i * ff : i * ff + last - a * ff].astype(F32)

    return near(body, pieces, [((depth, count), F32)] * (width // ff), [pltpu.VMEM((4, depth, width), BF)])


def unpack_attn(pieces, depth, width, heads, buckets):
    rows = pieces[0].shape[0]

    def body(*refs):
        own, grads, first_ref, second_ref, table_ref, held = lax.axis_index("tp"), refs[4:8], *refs[8:]
        for k in range(4):
            held[own ^ k] = refs[k][...].astype(F32)
        for i, out in enumerate(grads):
            for a in range(4):
                out[:, a * width : (a + 1) * width] = held[a, :depth, i * width : (i + 1) * width]
        small = [held[a, depth : depth + EXTRA] for a in range(4)]
        first_ref[...] = sum(p[0:1, :depth] for p in small)
        second_ref[...] = small[0][1:2, :depth]
        for a in range(4):
            for h in range(heads):
                table_ref[a * heads + h : a * heads + h + 1] = small[a][2:3, h * buckets : (h + 1) * buckets]

    outs = [((depth, 4 * width), F32)] * 4 + [((1, depth), F32)] * 2 + [((4 * heads, buckets), F32)]
    return near(body, pieces, outs, [pltpu.VMEM((4, rows, 4 * width), F32)])


ORDER = (
    "Pa", "I0", "Pm", "a1", "a2", "C0", "M0", "g1", "a3", "u1", "g2", "I1s0", "d1", "a4", "d2", "a5", "C1s0",
    "I1s1", "I1e", "QK", "u2", "R0s0", "g3", "R0s1", "u3", "R0e", "d3", "g4", "u4", "R2s0", "d4", "R2s1", "R2e",
    "u5", "g5", "C1s1", "C1e", "ML", "rd1", "d5", "MB", "B0s0", "rd2", "O0s0", "rg1", "WU", "O0e", "ru1", "B0e",
    "rd3", "ru2", "rg2", "rd4", "B2s0", "rg3", "B2e", "AB", "WA", "ru3", "rd5", "N0s0", "ra1", "rg4", "O2", "ra2",
    "N0e", "rg5", "Xd0", "Xd1", "Xd2", "ra3", "Xd3", "ru4", "ra4", "ru5", "Xu0", "Xu1", "N2", "ra5", "Xa0", "Xu2",
    "Xa1", "Xu3", "Xa2", "Xa3",
)


def shards(
    block_input, cotangent, query_w, key_w, value_w, output_w, gate_w, up_w, down_w,
    first_gain, second_gain, bias_table, rel_bucket, doc_ids,
):
    rows, length, model = block_input.shape
    tokens = rows * length
    own = lax.axis_index("tp")
    parts = lax.axis_size("seq")
    count = lax.axis_size("rows") * parts
    bucket_count, head_count = bias_table.shape
    inner = query_w.shape[1]
    heads = head_count // 4
    dim = inner // head_count
    width = heads * dim
    depth = query_w.shape[0]
    chunk = 4 * depth
    hidden_count = gate_w.shape[1]
    ff = -(-hidden_count // (4 * 256)) * 256
    seq_len = doc_ids.shape[1]
    q_len = 4 * length
    shape = (heads, dim, rows, length)
    lanes = Lanes(count, 4)
    steps, tasks, have = {}, {}, {}

    def do(name):
        def keep(work):
            steps[name] = work
        return keep

    def task(key, names, make):
        def start():
            tasks[key] = Task(make())
            tasks[key].step()

        def end():
            have[key] = tasks[key].result()

        steps.update({name: lambda: tasks[key].step() for name in names})
        steps[names[0]], steps[names[-1]] = start, end

    def core(name, side=0):
        return [f"{name}s{n}" for n in range(CUTS[side])] + [f"{name}e"]

    def attn_blocks():
        weights = [query_w, key_w, value_w, output_w.T]
        gains = [first_gain.reshape(1, depth), second_gain.reshape(1, depth)]
        if depth % 16 == 0:
            return pack_attn(weights, gains, width)
        gains = jnp.pad(jnp.concatenate(gains, axis=0).astype(BF), ((0, EXTRA - 2), (0, 4 * width - depth)))
        return pack_plain(weights, width, gains)

    def mlp_blocks():
        weights = [down_w.T, gate_w, up_w]
        return pack_mlp(weights, ff) if depth % 16 == 0 else pack_plain(weights, ff, None)

    def attn_chunk():
        return gather_ring(lanes, stack_attn(tasks["Pa"].result(), chunk), chunk, 1)

    task("Pa", ["Pa", "Pa-"], lambda: exchange(lanes, attn_blocks()))
    task("Pm", ["Pm", "M0"], lambda: exchange(lanes, mlp_blocks()))
    task("a", ["a1", "a2", "a3", "a4", "a5"], attn_chunk)

    def mlp_chunk(i):
        if "chunks" not in have:
            have["chunks"] = stack_members(have["Pm"], [ff] * 3, PADS if ring_ok(count) else (0, 0, 0))
        return have["chunks"][i]

    task("d", ["d1", "d2", "d3", "d4", "d5"], lambda: gather_ring(lanes, mlp_chunk(0), chunk, -1))
    task("g", ["g1", "g2", "g3", "g4", "g5"], lambda: gather_ring(lanes, mlp_chunk(1), chunk, 1))
    task("u", ["u1", "u2", "u3", "u4", "u5"], lambda: gather_ring(lanes, mlp_chunk(2), chunk, -1))

    task("in", ["I0", *core("I1")], lambda: gather_tokens(lanes, block_input.reshape(tokens, model), CUTS[0]))
    task("cot", ["C0", *core("C1")], lambda: gather_tokens(lanes, cotangent.reshape(tokens, model), CUTS[0]))

    @do("QK")
    def _():
        one_hot = (rel_bucket[:, None] == jnp.arange(bucket_count, dtype=jnp.int32)).astype(F32)
        first = lax.axis_index("seq") * q_len
        one_hot = lax.dynamic_slice_in_dim(one_hot, seq_len - first - q_len, seq_len + q_len, 0)
        own_table = lax.dynamic_slice_in_dim(bias_table, own * heads, heads, 1)
        by_distance = lax.dot_general(own_table, one_hot, (((0,), (1,)), ((), ())), precision=HIGHEST)
        query_doc = lax.dynamic_slice_in_dim(doc_ids, first, q_len, 1)[:, :, None]
        attn_w, chunks = have["a"]
        gain_one, gain_two = spread_gains(chunks, chunk)
        normed, rsq_one, queries, keys, values = project(have["in"], gain_one, attn_w, width)
        queries = lanes.pin(queries)
        if parts > 1:
            keys = lax.all_gather(keys, "seq", axis=0)
            values = lax.all_gather(values, "seq", axis=0)
        else:
            keys, values = keys[None], values[None]
        have.update(
            one_hot=one_hot, attn_w=attn_w, gain_one=gain_one, gain_two=gain_two, normed=normed, rsq_one=rsq_one,
            scores=(queries, keys, values, by_distance, query_doc, doc_ids[:, None, :]),
        )

    def attention():
        have["attn"], keep, give = attn_forward(*have["scores"], have["attn_w"], *shape)
        return sum_tokens(lanes, keep, give, CUTS[0])

    task("branch", [*core("R0"), *core("R2")], attention)

    branch_end, cot_end = steps[core("R2")[-1]], steps[core("C1")[-1]]

    @do(core("R2")[-1])
    def _():
        branch_end()
        middle, normed_mlp = norm_again(have["in"], *have["branch"], have["gain_two"])
        have.update(middle=middle, normed_mlp=lanes.pin(normed_mlp))

    @do(core("C1")[-1])
    def _():
        cot_end()
        have["cot"] = lanes.pin(have["cot"])

    @do("ML")
    def _():
        hidden, slopes = gated(have["normed_mlp"], have["g"][0], have["u"][0])
        have.update(hidden=lanes.pin(hidden), slopes=slopes)

    @do("MB")
    def _():
        have["grad_pair"] = lanes.pin(gated_back(have["cot"], have["d"][0], have["slopes"]))

    task(
        "rd", ["rd1", "rd2", "rd3", "rd4", "rd5"],
        lambda: scatter_ring(lanes, weight_grad(have["cot"], have["hidden"], count), 1, chunk + RPADS[0]),
    )
    task(
        "back", [*core("B0", 1), *core("B2", 1)],
        lambda: sum_tokens(lanes, *back_through(have["grad_pair"], [have["g"][0], have["u"][0]]), CUTS[1]),
    )
    if "rm1" in ORDER:
        task(
            "rm", ["rm1", "rm2", "rm3", "rm4", "rm5"],
            lambda: scatter_ring(lanes, weight_grad(have["normed_mlp"], have["grad_pair"], count), -1, chunk + RPADS[1]),
        )
    else:
        @do("WU")
        def _():
            have["up_blocks"] = lanes.pin(weight_grad(have["normed_mlp"], lanes.pin(have["grad_pair"]), count, ff, 2 * ff))

        task(
            "rg", ["rg1", "rg2", "rg3", "rg4", "rg5"],
            lambda: scatter_ring(
                lanes, weight_grad(have["normed_mlp"], lanes.pin(have["grad_pair"]), count, 0, ff), -1, chunk + RPADS[1]
            ),
        )
        task("ru", ["ru1", "ru2", "ru3", "ru4", "ru5"], lambda: scatter_ring(lanes, have["up_blocks"], 1, chunk + RPADS[2]))
    task("out", [*core("O0", 1), "O2"], lambda: scatter_tokens(lanes, *back_through(lanes.pin(have["hidden"]), [have["d"][0]]), CUTS[1]))

    @do("AB")
    def _():
        grad_middle, grad_branch, second_part, grad_attn = norm_back(
            have["middle"], have["cot"], *have["back"], have["gain_two"], have["attn_w"], width
        )
        grad_q, grad_k, grad_v, table = attn_backward(
            *have["scores"], have["attn"], lanes.pin(grad_attn), have["one_hot"], *shape, 4 * width
        )
        if parts > 1:
            grad_k = lax.psum_scatter(grad_k, "seq", scatter_dimension=0, tiled=True)
            grad_v = lax.psum_scatter(grad_v, "seq", scatter_dimension=0, tiled=True)
        have.update(
            grad_middle=grad_middle, grad_branch=grad_branch, second_part=second_part, table=table,
            grads=(lanes.pin(grad_q), grad_k[0], grad_v[0]),
        )

    @do("WA")
    def _():
        four_grad, keep, give = attn_weight_grads(
            have["normed"], have["in"], have["rsq_one"], have["grad_branch"], have["attn"], have["grads"],
            have["attn_w"], have["second_part"], have["table"], chunk,
        )
        have.update(four_grad=lanes.pin(four_grad), in_parts=(keep, give))

    task("ra", ["ra1", "ra2", "ra3", "ra4", "ra5"], lambda: scatter_ring(lanes, have["four_grad"], -1, chunk + EXTRA))
    task("grad_in", [*core("N0", 1), "N2"], lambda: scatter_tokens(lanes, *have["in_parts"], CUTS[1]))

    if "rm1" in ORDER:
        one, two = ["rd"], ["rm"]
    else:
        one, two = ["rd", "rg"], ["ru"]
    task("Xd", ["Xd0", "Xd1", "Xd2", "Xd3"], lambda: exchange(lanes, rows_of([have[k] for k in one], depth), False))
    task("Xu", ["Xu0", "Xu1", "Xu2", "Xu3"], lambda: exchange(lanes, rows_of([have[k] for k in two], depth), False))
    task("Xa", ["Xa0", "Xa1", "Xa2", "Xa3"], lambda: exchange(lanes, split_attn(have["ra"], depth, width), False))

    for name in ORDER:
        steps[name]()
    block_output = finish_output(have["out"], have["middle"])
    input_grad = finish_input(have["grad_in"], have["in"], have["gain_one"], have["grad_middle"])

    mlp = unpack_mlp(have["Xd"], hidden_count, ff) + unpack_mlp(have["Xu"], hidden_count, ff)
    *grads, first_grad, second_grad, table_grad = unpack_attn(have["Xa"], depth, width, heads, bucket_count)
    return (
        block_output.reshape(rows, length, model), input_grad.reshape(rows, length, model),
        grads[0], grads[1], grads[2], grads[3].T,
        mlp[1], mlp[2], mlp[0].T, first_grad.reshape(depth), second_grad.reshape(depth), table_grad.T,
    )


def solution(mesh):
    row_count, blk_count = mesh.shape["rows"], mesh.shape["blk"]
    fine = Mesh(mesh.devices.reshape(row_count, blk_count // 4, 4), ("rows", "seq", "tp"))
    every = ("rows", "seq", "tp")
    tokens = P("rows", ("seq", "tp"), None)
    deep, wide, flat = P(every, None), P(None, every), P(every)
    return jax.shard_map(
        shards,
        mesh=fine,
        in_specs=(tokens, tokens, deep, deep, deep, wide, deep, deep, wide, flat, flat, P(), P(), P("rows", None)),
        out_specs=(tokens, tokens, deep, deep, deep, wide, deep, deep, wide, flat, flat, P()),
        check_vma=False,
    )
```

```python
import math

import jax
import jax.numpy as jnp
from jax import lax
from jax.experimental import pallas as pl
from jax.experimental.pallas import tpu as pltpu
from jax.sharding import Mesh, PartitionSpec as P

EPSILON = 1e-06
BF = jnp.bfloat16
F32 = jnp.float32
HIGHEST = lax.Precision.HIGHEST
RING = ("rows", "seq")
MAX_RING = 8
EXTRA = 8
PADS = (8, 7, 5)
RPADS = (6, 4, 6)
CUTS = (2, 1)
FREE = pl.CostEstimate(flops=0, transcendentals=0, bytes_accessed=0)


def dot(left, right, dims, out=F32):
    return lax.dot_general(left, right, (dims, ((), ())), preferred_element_type=out)


NN = ((1,), (0,))
NT = ((1,), (1,))
TN = ((0,), (0,))


def ring_order(count):
    return list(range(0, count, 2)) + list(range(count - 1, 0, -2))


def ring_places(count):
    half = count // 2
    group = lax.axis_index(RING)
    place = jnp.where(group % 2 == 0, group // 2, count - 1 - group // 2)
    places = []
    for k in range(count):
        at = place - k
        at = jnp.where(at < 0, at + count, at)
        places.append(jnp.where(at < half, 2 * at, 2 * (count - 1 - at) + 1))
    return places


def ring_ok(count):
    return count <= MAX_RING and count % 2 == 0


class Lanes:
    def __init__(self, count, ways):
        order = ring_order(count)
        self.pairs = {
            step: [(order[i], order[(i + step) % count]) for i in range(count)] for step in (1, -1)
        }
        self.count, self.ways, self.last = count, ways, None

    def pin(self, *values):
        if self.last is not None:
            values = lax.optimization_barrier((*values, self.last))[:-1]
        self.last = values[0]
        return values if len(values) > 1 else values[0]

    def shift(self, value, step):
        return lax.ppermute(value, RING, self.pairs[step])

    def partner(self, value, bit):
        return lax.ppermute(value, "tp", [(i, i ^ bit) for i in range(self.ways)])


class Task:
    def __init__(self, steps):
        self.steps, self.value = steps, None

    def step(self):
        if self.steps is not None:
            try:
                next(self.steps)
            except StopIteration as stop:
                self.value, self.steps = stop.value, None

    def result(self):
        while self.steps is not None:
            self.step()
        return self.value


def gather_ring(lanes, chunk, keep, lead):
    count = lanes.count
    if not ring_ok(count):
        got = lax.all_gather(chunk, RING, axis=0) if count > 1 else chunk[None]
        return got[:, :keep].reshape(-1, chunk.shape[1]), [got[i] for i in range(count)]
    chunk = lanes.pin(chunk)
    moving = {lead: chunk, -lead: chunk}
    got = [chunk]
    for k in range(1, count // 2):
        moving = {step: lanes.shift(value, step) for step, value in moving.items()}
        yield
        moving = dict(zip(moving, lanes.pin(*moving.values())))
        got += [moving[1], moving[-1]]
    last = lanes.shift(moving[lead], lead)
    yield
    got.append(lanes.pin(last))
    return place_rows(got, count, keep), got


def chunk_order(count):
    order = [0]
    for k in range(1, count // 2):
        order += [k, count - k]
    return order + [count // 2]


def place_rows(got, count, keep):
    def body(*refs):
        places = ring_places(count)
        for ref, k in zip(refs, chunk_order(count)):
            refs[-1][pl.ds(pl.multiple_of(places[k] * keep, keep), keep), :] = ref[:keep]

    return near(body, got, [((count * keep, got[0].shape[1]), BF)])[0]


def scatter_ring(lanes, blocks, lead, rows):
    count, size, _ = blocks.shape
    if count == 1:
        return blocks[0]
    if not ring_ok(count):
        return lax.psum_scatter(blocks, RING, scatter_dimension=0, tiled=True)[0]
    (far,) = add_blocks(blocks, [(count // 2, None)], rows)
    moving = {lead: lanes.shift(lanes.pin(far), lead)}
    yield
    for j in range(count // 2 - 1, 0, -1):
        arrived = dict(zip(moving, lanes.pin(*moving.values()) if len(moving) > 1 else (lanes.pin(moving[lead]),)))
        sums = add_blocks(blocks, [(-j * step, arrived.get(step)) for step in (1, -1)], rows)
        moving = {step: lanes.shift(value, step) for step, value in zip((1, -1), lanes.pin(*sums))}
        yield
    came, back = lanes.pin(*moving.values())
    return add_blocks(blocks, [(0, came)], size, back)[0]


def add_blocks(blocks, terms, rows, more=None):
    count, size, width = blocks.shape
    came = [c for _, c in terms if c is not None] + ([] if more is None else [more])

    def body(blocks_ref, *refs):
        places = ring_places(count)
        given, outs = list(refs[: len(came)]), refs[len(came) :]
        for (k, c), out in zip(terms, outs):
            total = blocks_ref[places[k % count]].astype(F32)
            if c is not None:
                total = total + given.pop(0)[:size].astype(F32)
            if more is not None:
                total = total + given.pop(0)[:size].astype(F32)
            out[:size] = total.astype(BF)
            if rows > size:
                out[size:] = jnp.zeros((rows - size, width), BF)

    return near(body, [blocks, *came], [((rows, width), BF)] * len(terms))


def block_of(index):
    return index % 2 * 2 + index // 2


def gather_tokens(lanes, value, cuts):
    value = lanes.pin(value)
    got = lanes.partner(value, 2)
    yield
    value = jnp.concatenate([value, lanes.pin(got)], axis=0)
    got = yield from over_core(lanes, value, cuts)
    return jnp.concatenate([value, *got], axis=0)


def over_core(lanes, give, cuts):
    rows, pieces, first = give.shape[0], [], 0
    for n in range(cuts):
        last = rows * (n + 1) // cuts // 16 * 16 if n + 1 < cuts else rows
        got = lanes.partner(lanes.pin(give[first:last]), 1)
        yield
        pieces.append(lanes.pin(got))
        first = last
    return pieces


def sum_tokens(lanes, keep, give, cuts):
    got = yield from over_core(lanes, give, cuts)
    low = lanes.pin(add_halves(keep, got, False))
    got = lanes.partner(low, 2)
    yield
    low = lanes.pin(add_halves(low, [lanes.pin(got)], True))
    got = yield from over_core(lanes, low, cuts)
    return low, got


def add_halves(left, pieces, swapped):
    rows = left.shape[0]
    half = rows // 2

    def body(left_ref, *refs):
        first = 0
        for ref in refs[:-1]:
            for at in range(0, ref.shape[0], half if swapped else ref.shape[0]):
                count = half if swapped else ref.shape[0]
                to = half - at if swapped else first + at
                total = left_ref[to : to + count].astype(F32) + ref[at : at + count].astype(F32)
                refs[-1][to : to + count] = total.astype(BF)
            first += ref.shape[0]

    return near(body, [left, *pieces], [(left.shape, BF)])[0]


def scatter_tokens(lanes, keep, give, cuts):
    got = yield from over_core(lanes, give, cuts)
    low = lanes.pin(add_halves(keep, got, False))
    mine = low.shape[0] // 2
    got = lanes.partner(low[mine:], 2)
    yield
    return low[:mine], lanes.pin(got)


def exchange(lanes, blocks, at_once=True):
    pieces = [blocks[0]] + [None] * 3
    for k in (2, 3, 1):
        pieces[k] = lanes.partner(lanes.pin(blocks[k]), k)
        if not at_once:
            yield
    if at_once:
        yield
    pieces[1:] = lanes.pin(*pieces[1:])
    return pieces


def by_member(pieces):
    own, chosen = lax.axis_index("tp"), []
    for a in range(4):
        piece = pieces[a]
        for mine in range(1, 4):
            piece = jnp.where(own == mine, pieces[a ^ mine], piece)
        chosen.append(piece)
    return chosen


def stack_members(pieces, widths, pads):
    depth = pieces[0].shape[0]
    if depth % 16:
        pieces = jnp.concatenate(by_member(pieces), axis=0)
        starts = [sum(widths[:i]) for i in range(len(widths))]
        return [jnp.pad(pieces[:, a : a + w], ((0, p), (0, 0))) for a, w, p in zip(starts, widths, pads)]

    def body(*refs):
        own = lax.axis_index("tp")
        at = 0
        for width, pad, out in zip(widths, pads, refs[4:]):
            for k in range(4):
                out[pl.ds(pl.multiple_of((own ^ k) * depth, depth), depth), :] = refs[k][:, at : at + width]
            if pad:
                out[4 * depth :] = jnp.zeros((pad, width), BF)
            at += width

    return near(body, pieces, [((4 * depth + pad, width), BF) for width, pad in zip(widths, pads)])


def stack_attn(pieces, chunk):
    depth, width = chunk // 4, pieces[0].shape[1]
    if depth % 16:
        pieces = by_member(pieces)
        gains = jnp.concatenate([p[depth : depth + 2, :depth] for p in pieces], axis=1)
        gains = jnp.pad(gains, ((0, EXTRA - 2), (0, width - chunk)))
        return jnp.concatenate([p[:depth] for p in pieces] + [gains], axis=0)

    def body(*refs):
        own, out, gains_ref = lax.axis_index("tp"), refs[4], refs[5]
        for k in range(4):
            out[pl.ds(pl.multiple_of((own ^ k) * depth, depth), depth), :] = refs[k][:depth]
            gains_ref[own ^ k] = refs[k][depth:, :depth].astype(F32)
        gains = [gains_ref[a] for a in range(4)] + [jnp.zeros((EXTRA, width - chunk), F32)]
        out[chunk:] = jnp.concatenate(gains, axis=1).astype(BF)

    return near(body, pieces, [((chunk + EXTRA, width), BF)], [pltpu.VMEM((4, EXTRA, depth), F32)])[0]


def split_attn(total, depth, width):
    chunk = 4 * depth
    if depth % 16:
        tables = jnp.pad(total[chunk + 2 : chunk + 3], ((2, EXTRA - 3), (0, 0)))
        blocks = []
        for large, pair in zip(rows_of([total], depth), rows_of([total[chunk : chunk + 2, :chunk].T], depth)):
            pair = jnp.pad(pair.T, ((0, EXTRA - 2), (0, 4 * width - depth)))
            blocks.append(jnp.concatenate([large, pair + tables], axis=0))
        return blocks

    def body(total_ref, *refs):
        own, small_ref = lax.axis_index("tp"), refs[4]
        fill = jnp.zeros((2, 4 * width - depth), F32)
        small = total_ref[chunk : chunk + EXTRA].astype(F32)
        below = jnp.concatenate([small[2:3], jnp.zeros((EXTRA - 3, 4 * width), F32)], axis=0)
        for a in range(4):
            pair = jnp.concatenate([small[0:2, a * depth : (a + 1) * depth], fill], axis=1)
            small_ref[a] = jnp.concatenate([pair, below], axis=0)
        for k in range(4):
            refs[k][:depth] = total_ref[pl.ds(pl.multiple_of((own ^ k) * depth, depth), depth), :]
            refs[k][depth:] = small_ref[own ^ k].astype(BF)

    return near(
        body, [total], [((depth + EXTRA, 4 * width), BF)] * 4, [pltpu.VMEM((4, EXTRA, 4 * width), F32)]
    )


def run(body, grid, ins, outs, scratch=(), vmem=24):
    def spec(block, index_map):
        return pl.BlockSpec(block, index_map)

    arrays, in_specs = [], []
    for item in ins:
        array, block, index_map = item if isinstance(item, tuple) else (item, item.shape, None)
        if index_map is None:
            index_map = lambda *_, n=array.ndim: (0,) * n
        arrays.append(array)
        in_specs.append(spec(block, index_map))
    out_specs = [
        spec(block or shape, index_map or (lambda *_, n=len(shape): (0,) * n)) for shape, _, block, index_map in outs
    ]
    return pl.pallas_call(
        body, grid=grid, in_specs=in_specs, out_specs=out_specs,
        out_shape=[jax.ShapeDtypeStruct(shape, dtype) for shape, dtype, _, _ in outs],
        scratch_shapes=list(scratch),
        compiler_params=pltpu.CompilerParams(
            dimension_semantics=("arbitrary",) * len(grid), vmem_limit_bytes=vmem << 20
        ),
        cost_estimate=FREE,
    )(*arrays)


def near(body, arrays, outs, scratch=(), vmem=16):
    spec = pl.BlockSpec(memory_space=pltpu.VMEM)
    return pl.pallas_call(
        body, in_specs=[spec] * len(arrays), out_specs=[spec] * len(outs),
        out_shape=[jax.ShapeDtypeStruct(shape, dtype) for shape, dtype in outs],
        scratch_shapes=list(scratch),
        compiler_params=pltpu.CompilerParams(vmem_limit_bytes=vmem << 20),
        cost_estimate=FREE,
    )(*arrays)


def far(arrays):
    return [pltpu.with_memory_space_constraint(a, pltpu.HBM) for a in arrays]


def whole(shape, dtype):
    return (shape, dtype, None, None)


def pack_attn(weights, gains, width):
    depth, inner = weights[0].shape

    def body(q_ref, k_ref, v_ref, o_ref, first_ref, second_ref, *rest):
        outs, out_ref = rest[:4], rest[4]
        own = lax.axis_index("tp")
        extra = jnp.concatenate([first_ref[...], second_ref[...], jnp.zeros((EXTRA - 2, depth), F32)], axis=0)
        extra = jnp.concatenate([extra, jnp.zeros((EXTRA, 4 * width - depth), F32)], axis=1).astype(BF)
        for a in range(4):
            parts = [r[:, a * width : (a + 1) * width] for r in (q_ref, k_ref, v_ref, o_ref)]
            out_ref[a ^ own, :depth] = jnp.concatenate(parts, axis=1).astype(BF)
            out_ref[a ^ own, depth:] = extra
        for k in range(4):
            outs[k][...] = out_ref[k]

    shape = (depth + EXTRA, 4 * width)
    return run(body, (1,), far([*weights, *gains]), [whole(shape, BF)] * 4, [pltpu.VMEM((4, *shape), BF)])


def pack_mlp(weights, ff):
    depth, count = weights[0].shape

    def body(*refs):
        own, out_ref = lax.axis_index("tp"), refs[-1]
        for a in range(4):
            parts = []
            for ref in refs[: len(weights)]:
                last = min(count, (a + 1) * ff)
                parts.append(ref[:, a * ff : last])
                if last < (a + 1) * ff:
                    parts.append(jnp.zeros((depth, (a + 1) * ff - last), F32))
            out_ref[a ^ own] = jnp.concatenate(parts, axis=1).astype(BF)
        for k in range(4):
            refs[len(weights) + k][...] = out_ref[k]

    shape = (depth, len(weights) * ff)
    return run(body, (1,), far(weights), [whole(shape, BF)] * 4, [pltpu.VMEM((4, *shape), BF)])


def pack_plain(weights, width, extra):
    own = lax.axis_index("tp")
    weights = [jnp.pad(w.astype(BF), ((0, 0), (0, 4 * width - w.shape[1]))) for w in weights]
    blocks = []
    for k in range(4):
        block = jnp.concatenate([lax.dynamic_slice_in_dim(w, (own ^ k) * width, width, 1) for w in weights], axis=1)
        blocks.append(block if extra is None else jnp.concatenate([block, extra], axis=0))
    return blocks


def spread_gains(chunks, chunk):
    count = len(chunks)
    ring = ring_ok(count)

    def body(*refs):
        one_ref, two_ref, rows_ref = refs[-3:]
        places = ring_places(count) if ring else None
        for ref, k in zip(refs, chunk_order(count) if ring else range(count)):
            rows_ref[places[k] if ring else k] = ref[chunk : chunk + 2, :chunk].astype(F32)
        both = jnp.concatenate([rows_ref[r] for r in range(count)], axis=1)
        one_ref[...], two_ref[...] = both[0:1], both[1:2]

    return near(body, chunks, [((1, count * chunk), F32)] * 2, [pltpu.VMEM((count, 2, chunk), F32)])


def tiles(total, tile, work):
    lax.fori_loop(0, total // tile, lambda i, _: work(pl.multiple_of(i * tile, tile)), None, unroll=2)


def rsq_of(value):
    return lax.rsqrt(jnp.mean(value * value, axis=1, keepdims=True) + EPSILON)


def project(inputs, gain, weights, width):
    tokens, model = inputs.shape
    tile = tokens // 2

    def body(x_ref, gain_ref, w_ref, normed_ref, rsq_ref, q_ref, k_ref, v_ref):
        for at in range(0, tokens, tile):
            rows = slice(at, at + tile)
            x = x_ref[rows].astype(F32)
            rsq = rsq_of(x)
            normed = (x * rsq * gain_ref[...]).astype(BF)
            normed_ref[rows] = normed
            rsq_ref[rows] = jnp.broadcast_to(rsq, (tile, 128))
            three = dot(normed, w_ref[:, : 3 * width], NN).astype(BF)
            for i, ref in enumerate((q_ref, k_ref, v_ref)):
                ref[rows] = three[:, i * width : (i + 1) * width]

    return near(
        body, [inputs, gain, weights],
        [((tokens, model), BF), ((tokens, 128), F32)] + [((tokens, width), BF)] * 3,
    )


def head_scores(own, row, head, dim, rows, length, q_ref, k_ref, w_ref, qd_ref, kd_ref):
    lanes = slice(head * dim, (head + 1) * dim)
    starts = [pl.multiple_of((block_of(own ^ a) * rows + row) * length, length) for a in range(4)]
    queries = jnp.concatenate([q_ref[pl.ds(s, length), lanes] for s in starts], axis=0)
    keys = take_keys(k_ref, starts, length, lanes)
    q_len, k_len = queries.shape[0], keys.shape[0]
    scores = dot(queries, keys, NT)
    bias = jnp.broadcast_to(w_ref[pl.ds(head, 1), :], (q_len, q_len + k_len))
    bias = pltpu.roll(bias, k_len, 1, stride=1, stride_axis=0)[:, :k_len]
    same = qd_ref[row] == kd_ref[row]
    expo = jnp.where(same, jnp.exp(scores + bias), 0.0)
    return queries, keys, expo, starts, lanes


def take_keys(ref, starts, length, lanes):
    return jnp.concatenate(
        [ref[g, pl.ds(s, length), lanes] for g in range(ref.shape[0]) for s in starts], axis=0
    )


def attn_forward(q, k, v, by_distance, query_doc, key_doc, attn_w, heads, dim, rows, length):
    tokens, width = q.shape
    model = attn_w.shape[0]
    half = tokens // 2

    def body(q_ref, k_ref, v_ref, w_ref, qd_ref, kd_ref, o_ref, attn_ref, keep_ref, give_ref, part_ref):
        def one_row(row):
            forward_row(row, q_ref, k_ref, v_ref, w_ref, qd_ref, kd_ref, o_ref, attn_ref, part_ref)

        lax.fori_loop(0, rows, lambda row, _: one_row(row), None)
        keep_ref[...] = part_ref[:half]
        give_ref[...] = part_ref[half:].astype(BF)

    def forward_row(row, q_ref, k_ref, v_ref, w_ref, qd_ref, kd_ref, o_ref, attn_ref, part_ref):
        own, out = lax.axis_index("tp"), []
        for head in range(heads):
            _, _, expo, starts, lanes = head_scores(
                own, row, head, dim, rows, length, q_ref, k_ref, w_ref, qd_ref, kd_ref
            )
            values = take_keys(v_ref, starts, length, lanes)
            low = expo.astype(BF)
            totals = jnp.sum(low.astype(F32), axis=1, keepdims=True)
            out.append(dot(low, values, NN) / totals)
        out = jnp.concatenate(out, axis=1)
        part = dot(out.astype(BF), o_ref[:, 3 * width :], NT)
        for a, s in enumerate(starts):
            attn_ref[pl.ds(s, length), :] = out[a * length : (a + 1) * length]
            part_ref[pl.ds(s, length), :] = part[a * length : (a + 1) * length]

    return near(
        body, [q, k, v, by_distance, query_doc, key_doc, attn_w],
        [((tokens, width), F32), ((half, model), F32), ((half, model), BF)],
        [pltpu.VMEM((tokens, model), F32)],
    )


def attn_backward(q, k, v, by_distance, query_doc, key_doc, attn, grad, one_hot, heads, dim, rows, length, columns):
    buckets = one_hot.shape[1]

    def body(
        q_ref, k_ref, v_ref, w_ref, qd_ref, kd_ref, attn_ref, grad_ref, hot_ref,
        gq_ref, gk_ref, gv_ref, table_ref, diag_ref,
    ):
        diag_ref[...] = jnp.zeros(diag_ref.shape, F32)

        def one_row(row):
            backward_row(
                row, q_ref, k_ref, v_ref, w_ref, qd_ref, kd_ref, attn_ref, grad_ref, gq_ref, gk_ref, gv_ref, diag_ref
            )

        lax.fori_loop(0, rows, lambda row, _: one_row(row), None)
        table = lax.dot_general(
            diag_ref[...], hot_ref[...], (NN, ((), ())), precision=HIGHEST, preferred_element_type=F32
        )
        table = [table[h : h + 1] for h in range(heads)]
        table_ref[...] = jnp.concatenate(table + [jnp.zeros((1, columns - heads * buckets), F32)], axis=1)

    def backward_row(
        row, q_ref, k_ref, v_ref, w_ref, qd_ref, kd_ref, attn_ref, grad_ref, gq_ref, gk_ref, gv_ref, diag_ref
    ):
        own = lax.axis_index("tp")
        grads_q, grads_k, grads_v, diags = [], [], [], []
        for head in range(heads):
            queries, keys, expo, starts, lanes = head_scores(
                own, row, head, dim, rows, length, q_ref, k_ref, w_ref, qd_ref, kd_ref
            )
            values = take_keys(v_ref, starts, length, lanes)
            grads = jnp.concatenate([grad_ref[pl.ds(s, length), lanes] for s in starts], axis=0)
            outs = jnp.concatenate([attn_ref[pl.ds(s, length), lanes] for s in starts], axis=0)
            low = expo.astype(BF)
            totals = jnp.sum(low.astype(F32), axis=1, keepdims=True)
            grad_low = (grads / totals).astype(BF)
            grad_total = -jnp.sum(grads * outs, axis=1, keepdims=True) / totals
            grad_score = (expo * (dot(grad_low, values, NT) + grad_total)).astype(BF)
            grads_q.append(dot(grad_score, keys, NN))
            grads_k.append(dot(grad_score, queries, TN))
            grads_v.append(dot(low, grad_low, TN))
            q_len, k_len = grad_score.shape
            row_at = lax.broadcasted_iota(jnp.int32, (q_len, q_len), 0)
            column_at = lax.broadcasted_iota(jnp.int32, (q_len, q_len), 1)
            flip = jnp.where(row_at + column_at == q_len - 1, 1.0, 0.0).astype(BF)
            turned = dot(flip, grad_score, NN)
            turned = jnp.concatenate([turned, jnp.zeros((q_len, q_len), F32)], axis=1)
            turned = pltpu.roll(turned, 1, 1, stride=1, stride_axis=0)
            diags.append(jnp.sum(turned, axis=0, keepdims=True))
        joined = jnp.concatenate(grads_q, axis=1).astype(BF)
        for a, s in enumerate(starts):
            gq_ref[pl.ds(s, length), :] = joined[a * length : (a + 1) * length]
        for parts, ref in ((grads_k, gk_ref), (grads_v, gv_ref)):
            joined = jnp.concatenate(parts, axis=1).astype(BF)
            for g in range(ref.shape[0]):
                for a, s in enumerate(starts):
                    at = (g * 4 + a) * length
                    ref[g, pl.ds(s, length), :] = joined[at : at + length]
        diag_ref[...] += jnp.concatenate(diags, axis=0)

    return near(
        body, [q, k, v, by_distance, query_doc, key_doc, attn, grad, one_hot],
        [(q.shape, BF), (k.shape, BF), (v.shape, BF), ((1, columns), F32)],
        [pltpu.VMEM(by_distance.shape, F32)],
    )


def in_halves(low, others, tile):
    places = []
    for ref in (low, *others):
        places += [(ref, at) for at in range(0, ref.shape[0], tile)]
    return lambda i: places[i][0][places[i][1] : places[i][1] + tile].astype(F32)


def norm_again(inputs, low, others, gain):
    tokens, model = inputs.shape
    tile = tokens // 4

    def body(x_ref, gain_ref, low_ref, *refs):
        middle_ref, normed_ref = refs[-2:]
        read = in_halves(low_ref, refs[:-2], tile)
        for i in range(tokens // tile):
            rows = slice(i * tile, (i + 1) * tile)
            middle = x_ref[rows].astype(F32) + read(i)
            middle_ref[rows] = middle
            normed_ref[rows] = (middle * rsq_of(middle) * gain_ref[...]).astype(BF)

    return near(body, [inputs, gain, low, *others], [((tokens, model), F32), ((tokens, model), BF)])


def norm_back(middle, cot, low, others, gain, attn_w, width):
    tokens, model = middle.shape
    tile = tokens // 4

    def body(m_ref, cot_ref, gain_ref, w_ref, low_ref, *refs):
        mid_ref, branch_ref, gain_out_ref, attn_ref = refs[-4:]
        read = in_halves(low_ref, refs[:-4], tile)
        gain_sum = jnp.zeros((1, model), F32)
        for i in range(tokens // tile):
            rows = slice(i * tile, (i + 1) * tile)
            grad = read(i)
            middle = m_ref[rows]
            rsq = rsq_of(middle)
            unit = middle * rsq
            scaled = grad * gain_ref[...]
            back = cot_ref[rows].astype(F32) + rsq * (scaled - unit * jnp.mean(scaled * unit, axis=1, keepdims=True))
            mid_ref[rows] = back
            branch_ref[rows] = back.astype(BF)
            gain_sum += jnp.sum(grad * unit, axis=0, keepdims=True)
        gain_out_ref[...] = gain_sum
        attn_ref[...] = dot(branch_ref[...], w_ref[:, 3 * width :], NN)

    return near(
        body, [middle, cot, gain, attn_w, low, *others],
        [((tokens, model), F32), ((tokens, model), BF), ((1, model), F32), ((tokens, width), F32)],
    )


def gated(normed, gate_b, up_b):
    tokens, ff = normed.shape[0], gate_b.shape[1]
    tile = 256
    scale = math.sqrt(2.0 / math.pi)

    def body(x_ref, gate_ref, up_ref, hidden_ref, slopes_ref):
        def work(at):
            columns = pl.ds(at, tile)
            gate, up = dot(x_ref[...], gate_ref[:, columns], NN), dot(x_ref[...], up_ref[:, columns], NN)
            square = gate * gate
            tanh = jnp.tanh(scale * gate * (1.0 + 0.044715 * square))
            curve = 0.5 * (1.0 + tanh)
            slope = curve + 0.5 * gate * (1.0 - tanh * tanh) * (scale * (1.0 + 3 * 0.044715 * square))
            activated = gate * curve
            hidden_ref[:, columns] = (activated * up).astype(BF)
            slopes_ref[:, columns] = up * slope
            slopes_ref[:, pl.ds(pl.multiple_of(ff + at, tile), tile)] = activated

        tiles(ff, tile, work)

    return near(body, [normed, gate_b, up_b], [((tokens, ff), BF), ((tokens, 2 * ff), F32)])


def gated_back(cot, down_b, slopes):
    tokens, ff = cot.shape[0], down_b.shape[1]
    tile = 256

    def body(cot_ref, down_ref, slopes_ref, pair_ref):
        def work(at):
            grad = dot(cot_ref[...], down_ref[:, pl.ds(at, tile)], NN)
            for columns in (pl.ds(at, tile), pl.ds(pl.multiple_of(ff + at, tile), tile)):
                pair_ref[:, columns] = (grad * slopes_ref[:, columns]).astype(BF)

        tiles(ff, tile, work)

    return near(body, [cot, down_b, slopes], [((tokens, 2 * ff), BF)])[0]


def weight_grad(left, right, count, first=0, last=None):
    model = left.shape[1]
    last = last or right.shape[1]
    tile, chunk = 384, model // count

    def body(left_ref, right_ref, out_ref):
        def work(at):
            part = dot(left_ref[:, pl.ds(at, tile)], right_ref[:, first:last], TN).astype(BF)
            for c in range(tile // chunk):
                out_ref[at // chunk + c] = part[c * chunk : (c + 1) * chunk]

        tiles(model, tile, work)

    return near(body, [left, right], [((count, chunk, last - first), BF)])[0]


def back_through(left, rights):
    tokens, model = left.shape[0], rights[0].shape[0]
    half, tile = tokens // 2, 384

    def body(left_ref, *refs):
        keep_ref, give_ref = refs[-2:]

        def work(at):
            columns = pl.ds(at, tile)
            total, first = None, 0
            for ref in refs[:-2]:
                last = first + ref.shape[1]
                term = dot(left_ref[:, first:last], ref[columns, :], NT)
                total, first = term if total is None else total + term, last
            keep_ref[:, columns] = total[:half]
            give_ref[:, columns] = total[half:].astype(BF)

        tiles(model, tile, work)

    return near(body, [left, *rights], [((half, model), F32), ((half, model), BF)])


def attn_weight_grads(normed, inputs, rsq, branch, attn, grads, attn_w, second_part, table, chunk):
    tokens, model = normed.shape
    width = attn.shape[1]
    half, tile = tokens // 2, 384
    each = tile // chunk

    def body(n_ref, x_ref, rsq_ref, b_ref, attn_ref, q_ref, k_ref, v_ref, w_ref, second_ref, table_ref, out_ref, keep_ref, give_ref):
        three = jnp.concatenate([q_ref[...], k_ref[...], v_ref[...]], axis=1)
        attended = attn_ref[...].astype(BF)
        fill = jnp.zeros((1, 4 * width - chunk), F32)

        def work(at):
            columns = pl.ds(at, tile)
            back = dot(three, w_ref[columns, : 3 * width], NT)
            keep_ref[:, columns] = back[:half]
            give_ref[:, columns] = back[half:].astype(BF)
            first = jnp.sum(back * x_ref[:, columns].astype(F32) * rsq_ref[:, 0:1], axis=0, keepdims=True)
            second = second_ref[:, columns]
            wide = dot(n_ref[:, columns], three, TN).astype(BF)
            last = dot(b_ref[:, columns], attended, TN).astype(BF)
            for c in range(each):
                rows, block = slice(c * chunk, (c + 1) * chunk), at // chunk + c
                out_ref[block, :chunk] = jnp.concatenate([wide[rows], last[rows]], axis=1)
                small = [jnp.concatenate([row[:, rows], fill], axis=1) for row in (first, second)]
                small += [table_ref[...], jnp.zeros((EXTRA - 3, 4 * width), F32)]
                out_ref[block, chunk:] = jnp.concatenate(small, axis=0).astype(BF)

        tiles(model, tile, work)

    return near(
        body, [normed, inputs, rsq, branch, attn, *grads, attn_w, second_part, table],
        [((model // chunk, chunk + EXTRA, 4 * width), BF), ((half, model), F32), ((half, model), BF)],
    )


def finish_input(addends, inputs, gain, grad_middle):
    count, model = addends[0].shape

    def body(low_ref, got_ref, x_ref, gain_ref, mid_ref, out_ref):
        x = x_ref[:count].astype(F32)
        rsq = rsq_of(x)
        unit = x * rsq
        scaled = (low_ref[...].astype(F32) + got_ref[...].astype(F32)) * gain_ref[...]
        out_ref[...] = mid_ref[:count] + rsq * (scaled - unit * jnp.mean(scaled * unit, axis=1, keepdims=True))

    return near(body, [*addends, inputs, gain, grad_middle], [((count, model), F32)])[0]


def finish_output(addends, middle):
    count, model = addends[0].shape

    def body(low_ref, got_ref, mid_ref, out_ref):
        out_ref[...] = (mid_ref[:count] + low_ref[...].astype(F32) + got_ref[...].astype(F32)).astype(BF)

    return near(body, [*addends, middle], [((count, model), BF)])[0]


def rows_of(values, depth):
    if depth % 16:
        own, value = lax.axis_index("tp"), jnp.concatenate(values, axis=1)
        return [lax.dynamic_slice_in_dim(value, (own ^ k) * depth, depth, 0) for k in range(4)]

    def body(*refs):
        own = lax.axis_index("tp")
        for k in range(4):
            at = 0
            for ref in refs[: len(values)]:
                rows = ref[pl.ds(pl.multiple_of((own ^ k) * depth, depth), depth), :]
                refs[len(values) + k][:, at : at + ref.shape[1]] = rows
                at += ref.shape[1]

    return near(body, values, [((depth, sum(v.shape[1] for v in values)), BF)] * 4)


def unpack_mlp(pieces, count, ff):
    depth, width = pieces[0].shape

    def body(*refs):
        own, outs, held = lax.axis_index("tp"), refs[4:-1], refs[-1]
        for k in range(4):
            held[own ^ k] = refs[k][...]
        for i, out in enumerate(outs):
            for a in range(4):
                last = min(count, (a + 1) * ff)
                out[:, a * ff : last] = held[a, :, i * ff : i * ff + last - a * ff].astype(F32)

    return near(body, pieces, [((depth, count), F32)] * (width // ff), [pltpu.VMEM((4, depth, width), BF)])


def unpack_attn(pieces, depth, width, heads, buckets):
    rows = pieces[0].shape[0]

    def body(*refs):
        own, grads, first_ref, second_ref, table_ref, held = lax.axis_index("tp"), refs[4:8], *refs[8:]
        for k in range(4):
            held[own ^ k] = refs[k][...].astype(F32)
        for i, out in enumerate(grads):
            for a in range(4):
                out[:, a * width : (a + 1) * width] = held[a, :depth, i * width : (i + 1) * width]
        small = [held[a, depth : depth + EXTRA] for a in range(4)]
        first_ref[...] = sum(p[0:1, :depth] for p in small)
        second_ref[...] = small[0][1:2, :depth]
        for a in range(4):
            for h in range(heads):
                table_ref[a * heads + h : a * heads + h + 1] = small[a][2:3, h * buckets : (h + 1) * buckets]

    outs = [((depth, 4 * width), F32)] * 4 + [((1, depth), F32)] * 2 + [((4 * heads, buckets), F32)]
    return near(body, pieces, outs, [pltpu.VMEM((4, rows, 4 * width), F32)])


ORDER = (
    "Pa", "I0", "Pm", "a1", "a2", "C0", "M0", "g1", "a3", "u1", "g2", "I1s0", "d1", "a4", "d2", "a5", "C1s0",
    "I1s1", "I1e", "QK", "u2", "R0s0", "g3", "R0s1", "u3", "R0e", "d3", "g4", "u4", "R2s0", "d4", "R2s1", "R2e",
    "u5", "g5", "C1s1", "C1e", "ML", "rd1", "d5", "MB", "B0s0", "rd2", "O0s0", "rg1", "WU", "O0e", "ru1", "B0e",
    "rd3", "ru2", "rg2", "rd4", "B2s0", "rg3", "B2e", "AB", "WA", "ru3", "rd5", "N0s0", "ra1", "rg4", "O2", "ra2",
    "N0e", "rg5", "Xd0", "Xd1", "Xd2", "ra3", "Xd3", "ru4", "ra4", "ru5", "Xu0", "Xu1", "N2", "ra5", "Xa0", "Xu2",
    "Xa1", "Xu3", "Xa2", "Xa3",
)


def shards(
    block_input, cotangent, query_w, key_w, value_w, output_w, gate_w, up_w, down_w,
    first_gain, second_gain, bias_table, rel_bucket, doc_ids,
):
    rows, length, model = block_input.shape
    tokens = rows * length
    own = lax.axis_index("tp")
    parts = lax.axis_size("seq")
    count = lax.axis_size("rows") * parts
    bucket_count, head_count = bias_table.shape
    inner = query_w.shape[1]
    heads = head_count // 4
    dim = inner // head_count
    width = heads * dim
    depth = query_w.shape[0]
    chunk = 4 * depth
    hidden_count = gate_w.shape[1]
    ff = -(-hidden_count // (4 * 256)) * 256
    seq_len = doc_ids.shape[1]
    q_len = 4 * length
    shape = (heads, dim, rows, length)
    lanes = Lanes(count, 4)
    steps, tasks, have = {}, {}, {}

    def do(name):
        def keep(work):
            steps[name] = work
        return keep

    def task(key, names, make):
        def start():
            tasks[key] = Task(make())
            tasks[key].step()

        def end():
            have[key] = tasks[key].result()

        steps.update({name: lambda: tasks[key].step() for name in names})
        steps[names[0]], steps[names[-1]] = start, end

    def core(name, side=0):
        return [f"{name}s{n}" for n in range(CUTS[side])] + [f"{name}e"]

    def attn_blocks():
        weights = [query_w, key_w, value_w, output_w.T]
        gains = [first_gain.reshape(1, depth), second_gain.reshape(1, depth)]
        if depth % 16 == 0:
            return pack_attn(weights, gains, width)
        gains = jnp.pad(jnp.concatenate(gains, axis=0).astype(BF), ((0, EXTRA - 2), (0, 4 * width - depth)))
        return pack_plain(weights, width, gains)

    def mlp_blocks():
        weights = [down_w.T, gate_w, up_w]
        return pack_mlp(weights, ff) if depth % 16 == 0 else pack_plain(weights, ff, None)

    def attn_chunk():
        return gather_ring(lanes, stack_attn(tasks["Pa"].result(), chunk), chunk, 1)

    task("Pa", ["Pa", "Pa-"], lambda: exchange(lanes, attn_blocks()))
    task("Pm", ["Pm", "M0"], lambda: exchange(lanes, mlp_blocks()))
    task("a", ["a1", "a2", "a3", "a4", "a5"], attn_chunk)

    def mlp_chunk(i):
        if "chunks" not in have:
            have["chunks"] = stack_members(have["Pm"], [ff] * 3, PADS if ring_ok(count) else (0, 0, 0))
        return have["chunks"][i]

    task("d", ["d1", "d2", "d3", "d4", "d5"], lambda: gather_ring(lanes, mlp_chunk(0), chunk, -1))
    task("g", ["g1", "g2", "g3", "g4", "g5"], lambda: gather_ring(lanes, mlp_chunk(1), chunk, 1))
    task("u", ["u1", "u2", "u3", "u4", "u5"], lambda: gather_ring(lanes, mlp_chunk(2), chunk, -1))

    task("in", ["I0", *core("I1")], lambda: gather_tokens(lanes, block_input.reshape(tokens, model), CUTS[0]))
    task("cot", ["C0", *core("C1")], lambda: gather_tokens(lanes, cotangent.reshape(tokens, model), CUTS[0]))

    @do("QK")
    def _():
        one_hot = (rel_bucket[:, None] == jnp.arange(bucket_count, dtype=jnp.int32)).astype(F32)
        first = lax.axis_index("seq") * q_len
        one_hot = lax.dynamic_slice_in_dim(one_hot, seq_len - first - q_len, seq_len + q_len, 0)
        own_table = lax.dynamic_slice_in_dim(bias_table, own * heads, heads, 1)
        by_distance = lax.dot_general(own_table, one_hot, (((0,), (1,)), ((), ())), precision=HIGHEST)
        query_doc = lax.dynamic_slice_in_dim(doc_ids, first, q_len, 1)[:, :, None]
        attn_w, chunks = have["a"]
        gain_one, gain_two = spread_gains(chunks, chunk)
        normed, rsq_one, queries, keys, values = project(have["in"], gain_one, attn_w, width)
        queries = lanes.pin(queries)
        if parts > 1:
            keys = lax.all_gather(keys, "seq", axis=0)
            values = lax.all_gather(values, "seq", axis=0)
        else:
            keys, values = keys[None], values[None]
        have.update(
            one_hot=one_hot, attn_w=attn_w, gain_one=gain_one, gain_two=gain_two, normed=normed, rsq_one=rsq_one,
            scores=(queries, keys, values, by_distance, query_doc, doc_ids[:, None, :]),
        )

    def attention():
        have["attn"], keep, give = attn_forward(*have["scores"], have["attn_w"], *shape)
        return sum_tokens(lanes, keep, give, CUTS[0])

    task("branch", [*core("R0"), *core("R2")], attention)

    branch_end, cot_end = steps[core("R2")[-1]], steps[core("C1")[-1]]

    @do(core("R2")[-1])
    def _():
        branch_end()
        middle, normed_mlp = norm_again(have["in"], *have["branch"], have["gain_two"])
        have.update(middle=middle, normed_mlp=lanes.pin(normed_mlp))

    @do(core("C1")[-1])
    def _():
        cot_end()
        have["cot"] = lanes.pin(have["cot"])

    @do("ML")
    def _():
        hidden, slopes = gated(have["normed_mlp"], have["g"][0], have["u"][0])
        have.update(hidden=lanes.pin(hidden), slopes=slopes)

    @do("MB")
    def _():
        have["grad_pair"] = lanes.pin(gated_back(have["cot"], have["d"][0], have["slopes"]))

    task(
        "rd", ["rd1", "rd2", "rd3", "rd4", "rd5"],
        lambda: scatter_ring(lanes, weight_grad(have["cot"], have["hidden"], count), 1, chunk + RPADS[0]),
    )
    task(
        "back", [*core("B0", 1), *core("B2", 1)],
        lambda: sum_tokens(lanes, *back_through(have["grad_pair"], [have["g"][0], have["u"][0]]), CUTS[1]),
    )
    if "rm1" in ORDER:
        task(
            "rm", ["rm1", "rm2", "rm3", "rm4", "rm5"],
            lambda: scatter_ring(lanes, weight_grad(have["normed_mlp"], have["grad_pair"], count), -1, chunk + RPADS[1]),
        )
    else:
        @do("WU")
        def _():
            have["up_blocks"] = lanes.pin(weight_grad(have["normed_mlp"], lanes.pin(have["grad_pair"]), count, ff, 2 * ff))

        task(
            "rg", ["rg1", "rg2", "rg3", "rg4", "rg5"],
            lambda: scatter_ring(
                lanes, weight_grad(have["normed_mlp"], lanes.pin(have["grad_pair"]), count, 0, ff), -1, chunk + RPADS[1]
            ),
        )
        task("ru", ["ru1", "ru2", "ru3", "ru4", "ru5"], lambda: scatter_ring(lanes, have["up_blocks"], 1, chunk + RPADS[2]))
    task("out", [*core("O0", 1), "O2"], lambda: scatter_tokens(lanes, *back_through(lanes.pin(have["hidden"]), [have["d"][0]]), CUTS[1]))

    @do("AB")
    def _():
        grad_middle, grad_branch, second_part, grad_attn = norm_back(
            have["middle"], have["cot"], *have["back"], have["gain_two"], have["attn_w"], width
        )
        grad_q, grad_k, grad_v, table = attn_backward(
            *have["scores"], have["attn"], lanes.pin(grad_attn), have["one_hot"], *shape, 4 * width
        )
        if parts > 1:
            grad_k = lax.psum_scatter(grad_k, "seq", scatter_dimension=0, tiled=True)
            grad_v = lax.psum_scatter(grad_v, "seq", scatter_dimension=0, tiled=True)
        have.update(
            grad_middle=grad_middle, grad_branch=grad_branch, second_part=second_part, table=table,
            grads=(lanes.pin(grad_q), grad_k[0], grad_v[0]),
        )

    @do("WA")
    def _():
        four_grad, keep, give = attn_weight_grads(
            have["normed"], have["in"], have["rsq_one"], have["grad_branch"], have["attn"], have["grads"],
            have["attn_w"], have["second_part"], have["table"], chunk,
        )
        have.update(four_grad=lanes.pin(four_grad), in_parts=(keep, give))

    task("ra", ["ra1", "ra2", "ra3", "ra4", "ra5"], lambda: scatter_ring(lanes, have["four_grad"], -1, chunk + EXTRA))
    task("grad_in", [*core("N0", 1), "N2"], lambda: scatter_tokens(lanes, *have["in_parts"], CUTS[1]))

    if "rm1" in ORDER:
        one, two = ["rd"], ["rm"]
    else:
        one, two = ["rd", "rg"], ["ru"]
    task("Xd", ["Xd0", "Xd1", "Xd2", "Xd3"], lambda: exchange(lanes, rows_of([have[k] for k in one], depth), False))
    task("Xu", ["Xu0", "Xu1", "Xu2", "Xu3"], lambda: exchange(lanes, rows_of([have[k] for k in two], depth), False))
    task("Xa", ["Xa0", "Xa1", "Xa2", "Xa3"], lambda: exchange(lanes, split_attn(have["ra"], depth, width), False))

    for name in ORDER:
        steps[name]()
    block_output = finish_output(have["out"], have["middle"])
    input_grad = finish_input(have["grad_in"], have["in"], have["gain_one"], have["grad_middle"])

    mlp = unpack_mlp(have["Xd"], hidden_count, ff) + unpack_mlp(have["Xu"], hidden_count, ff)
    *grads, first_grad, second_grad, table_grad = unpack_attn(have["Xa"], depth, width, heads, bucket_count)
    return (
        block_output.reshape(rows, length, model), input_grad.reshape(rows, length, model),
        grads[0], grads[1], grads[2], grads[3].T,
        mlp[1], mlp[2], mlp[0].T, first_grad.reshape(depth), second_grad.reshape(depth), table_grad.T,
    )


def solution(mesh):
    row_count, blk_count = mesh.shape["rows"], mesh.shape["blk"]
    fine = Mesh(mesh.devices.reshape(row_count, blk_count // 4, 4), ("rows", "seq", "tp"))
    every = ("rows", "seq", "tp")
    tokens = P("rows", ("seq", "tp"), None)
    deep, wide, flat = P(every, None), P(None, every), P(every)
    return jax.shard_map(
        shards,
        mesh=fine,
        in_specs=(tokens, tokens, deep, deep, deep, wide, deep, deep, wide, flat, flat, P(), P(), P("rows", None)),
        out_specs=(tokens, tokens, deep, deep, deep, wide, deep, deep, wide, flat, flat, P()),
        check_vma=False,
    )
```
